256 devices in a mesh: tile: 64 (over x, z, core), section: 4 (over y).
Axes of the slice: x: 4, y: 4, z: 8, core: 2. Of those that a mesh axis runs over, the one named last changes fastest.
Arguments:
- block_inputs: bfloat16 [4, 4, 4, 2048, 1024], P('section', None, None, 'tile'), may hold values from -16 to 16
- out_grad: bfloat16 [4, 4, 2048, 1024], P(None, None, 'tile'), may hold values from -4 to 4
- tissue: int32 [4, 256], P(None, 'tile'), may hold values 0 or 1
- w_reduce: bfloat16 [4, 1024, 256], P('section'), may hold values from -0.1875 to 0.1875
- w_conv: bfloat16 [4, 3, 3, 256, 256], P('section'), may hold values from -0.125 to 0.125
- w_expand: bfloat16 [4, 256, 1024], P('section'), may hold values from -0.375 to 0.375
- inner_affine: float32 [4, 4, 256], P('section'), may hold values from -0.5 to 1
- outer_affine: float32 [4, 2, 1024], P('section'), may hold values from -0.5 to 1
Outputs:
- grad_inputs: bfloat16 [4, 4, 4, 2048, 1024], P('section', None, None, 'tile')
- grad_reduce: float32 [4, 1024, 256], P('section', 'tile')
- grad_conv: float32 [4, 3, 3, 256, 256], P('section', None, None, 'tile')
- grad_expand: float32 [4, 256, 1024], P('section', 'tile')
The draws below stay inside these ranges and needn't reach their ends.
All inputs are finite; a program needn't handle non-finite values. No bound on the sum of `tissue` on one device may be relied on, other than what follows from the above.
Results may differ from the reference program's by a relative error of at most 0.023.
The reference program's roundings to bfloat16 on the way count: a program that leaves them out, or rounds other values in their place, can miss the bound.
Values may be sent and summed in bfloat16 or wider, within the bound.
No kernel may reach another device: no remote copies, remote signals or barrier semaphores. Data moves between devices by JAX's collectives and lax.ppermute only.
A program may use at most 128 MiB of HBM per device.

```python
import jax
import jax.numpy as jnp
from jax import lax

CH = 1024
INNER = 256
ROWS = 4
HGT = 4
TILE_W = 8
WIDTH = 2048
TILES = 256
SECTIONS = 4


def with_ends(drawn, own_key, least, top_value):
    shape = drawn.shape
    index_at = [jax.random.randint(jax.random.fold_in(own_key, axis), (), 0, shape[axis]) for axis in range(len(shape))]
    drawn = drawn.at[tuple(index_at)].set(least)
    longest = shape.index(max(shape))
    index_at[longest] = (index_at[longest] + 1) % shape[longest]
    return drawn.at[tuple(index_at)].set(top_value)


def with_spikes(values, key, source, target, parts, factor):
    def block_of(axis_at):
        return (jnp.arange(values.shape[axis_at]) // (values.shape[axis_at] // parts)).reshape((-1,) + (1,) * (values.ndim - 1 - axis_at))

    first = jax.random.permutation(key, parts)[block_of(target)]
    far = (block_of(target) + parts // 2) % parts
    return jnp.where((block_of(source) == first) | (block_of(source) == far), factor * values, values)


def level_of(key, dims, split, smallest, largest):
    def one(dim, blocks):
        draws = jax.random.uniform(jax.random.fold_in(jax.random.fold_in(key, 6), dim), (blocks,), jnp.float32, smallest / len(split), largest / len(split))
        return jnp.repeat(jnp.exp(draws), dims[dim] // blocks).reshape((-1,) + (1,) * (len(dims) - dim - 1))

    gain = one(*split[0])
    for cut in split[1:]:
        gain = gain * one(*cut)
    return gain


def normal_values(stream_key, extent, scale, bound, shards=(), dtype=jnp.bfloat16):
    drawn = jax.random.normal(stream_key, extent, jnp.float32) * scale
    if len(shards) > 0:
        drawn = level_of(stream_key, extent, shards, -0.22, 0.18) * drawn
    return jnp.clip(drawn, min=-bound, max=bound).astype(dtype)


def bell_draw_with(stream_key, extent, scale, limit, split, heavy, dtype=jnp.bfloat16):
    values = scale * jax.random.normal(stream_key, extent, jnp.float32)
    if split:
        values = values * level_of(stream_key, extent, split, -0.22, 0.18)
    return jnp.clip(with_spikes(values, jax.random.fold_in(stream_key, 3), *heavy), -limit, limit).astype(dtype)


def setup_inputs(seed: int = 0) -> dict:
    keys = jax.random.split(jax.random.key(seed), 9)
    return {
        "block_inputs": bell_draw_with(keys[0], (SECTIONS, ROWS, HGT, WIDTH, CH), 1.0, 16.0, ((0, 4), (3, 64)), (3, 4, 64, 4.0)),
        "out_grad": normal_values(keys[1], (ROWS, HGT, WIDTH, CH), 0.5, 4.0, ((2, 64),)),
        "tissue": with_ends((jax.random.randint(keys[2], (ROWS, TILES), 0, 3) < 2).astype(jnp.int32), jax.random.fold_in(keys[2], 1), 0, 1),
        "w_reduce": normal_values(keys[3], (SECTIONS, CH, INNER), CH ** -0.5, 0.1875, ((0, 4),)),
        "w_conv": normal_values(keys[4], (SECTIONS, 3, 3, INNER, INNER), (9 * INNER) ** -0.5, 0.125, ((0, 4),)),
        "w_expand": normal_values(keys[5], (SECTIONS, INNER, CH), INNER ** -0.5, 0.375, ((0, 4),)),
        "inner_affine": jnp.clip(-0.5 + 1.5 * jax.random.uniform(keys[6], (SECTIONS, 4, INNER), jnp.float32) ** level_of(keys[6], (SECTIONS, 4, INNER), ((0, 4),), -0.2, 0.2), -0.5, 1.0),
        "outer_affine": jnp.clip(-0.5 + 1.5 * jax.random.uniform(keys[7], (SECTIONS, 2, CH), jnp.float32) ** level_of(keys[7], (SECTIONS, 2, CH), ((0, 4),), -0.2, 0.2), -0.5, 1.0),
    }


def contract(left, right):
    return lax.dot_general(left, right, (((0,), (0,)), ((), ())), preferred_element_type=jnp.float32)

def block_grad(inputs, grad_out, w_reduce, w_conv, w_expand, inner, outer):
    count, height, width, channels = inputs.shape
    inner_w = w_reduce.shape[1]
    flat_x = inputs.reshape(-1, channels)
    pre_one = jnp.dot(flat_x, w_reduce, preferred_element_type=jnp.float32) * inner[0] + inner[1]
    hidden_one = jnp.maximum(pre_one, 0.0).astype(jnp.bfloat16).reshape(count, height, width, inner_w)
    padded = jnp.pad(hidden_one, ((0, 0), (1, 1), (1, 1), (0, 0)))
    pieces = []
    for row_off in range(3):
        for col_off in range(3):
            pieces.append(padded[:, row_off:row_off + height, col_off:col_off + width].reshape(-1, inner_w))
    total = jnp.zeros((count * height * width, inner_w), jnp.float32)
    for offset in range(9):
        total = total + jnp.dot(pieces[offset], w_conv[offset // 3, offset % 3], preferred_element_type=jnp.float32)
    pre_two = total * inner[2] + inner[3]
    hidden_two = jnp.maximum(pre_two, 0.0).astype(jnp.bfloat16)
    summed = jnp.dot(hidden_two, w_expand, preferred_element_type=jnp.float32) * outer[0] + outer[1] + flat_x.astype(jnp.float32)
    flat_g = grad_out.reshape(-1, channels)
    grad_sum = jnp.where(summed > 0, flat_g.astype(jnp.float32), 0.0).astype(jnp.bfloat16)
    grad_three = (grad_sum.astype(jnp.float32) * outer[0]).astype(jnp.bfloat16)
    g_expand = contract(hidden_two, grad_three)
    grad_two = jnp.where(pre_two > 0, jnp.dot(grad_three, w_expand.T, preferred_element_type=jnp.float32) * inner[2], 0.0).astype(jnp.bfloat16)
    g_conv = jnp.stack([contract(pieces[offset], grad_two) for offset in range(9)]).reshape(3, 3, inner_w, inner_w)
    padded_grad = jnp.pad(grad_two.reshape(count, height, width, inner_w), ((0, 0), (1, 1), (1, 1), (0, 0)))
    back = jnp.zeros((count * height * width, inner_w), jnp.float32)
    for row_off in range(3):
        for col_off in range(3):
            piece = padded_grad[:, 2 - row_off:2 - row_off + height, 2 - col_off:2 - col_off + width].reshape(-1, inner_w)
            back = back + jnp.dot(piece, w_conv[row_off, col_off].T, preferred_element_type=jnp.float32)
    grad_one = jnp.where(pre_one > 0, back * inner[0], 0.0).astype(jnp.bfloat16)
    g_reduce = contract(flat_x, grad_one)
    grad_in = (grad_sum.astype(jnp.float32) + jnp.dot(grad_one, w_reduce.T, preferred_element_type=jnp.float32)).astype(jnp.bfloat16)
    return (grad_in.reshape(inputs.shape), g_reduce, g_conv, g_expand)

def reference(block_inputs, out_grad, tissue, w_reduce, w_conv, w_expand, inner_affine, outer_affine):
    coverage = jnp.repeat(tissue, TILE_W, axis=1).astype(jnp.bfloat16)[:, None, :, None]
    carried = out_grad * coverage
    grads_in, grads_r, grads_c, grads_e = ([], [], [], [])
    for block in range(SECTIONS - 1, -1, -1):
        carried, g_r, g_c, g_e = block_grad(block_inputs[block], carried, w_reduce[block], w_conv[block], w_expand[block], inner_affine[block], outer_affine[block])
        grads_in.insert(0, carried)
        grads_r.insert(0, g_r)
        grads_c.insert(0, g_c)
        grads_e.insert(0, g_e)
    return (jnp.stack(grads_in), jnp.stack(grads_r), jnp.stack(grads_c), jnp.stack(grads_e))
```

```python
import functools

import jax
import jax.numpy as jnp
from jax import lax
from jax.experimental import pallas as pl
from jax.experimental.pallas import tpu as pltpu
from jax.sharding import PartitionSpec as P

TILE_W = 8
X, Z, CORES = 4, 8, 2
EDGE = 8
RIM = 4
BF16, F32 = jnp.bfloat16, jnp.float32
LAG = 2
SEGS, A_SEGS = 17, 8
Z_ORDER = (7, 3, 5, 1, 6, 2, 4, 0)


def params(mib):
    return pltpu.CompilerParams(vmem_limit_bytes=mib * 1024 * 1024)


def dot(left, right):
    return jnp.dot(left, right, preferred_element_type=F32)


def full(shape):
    return pl.BlockSpec(shape, lambda *_: (0,) * len(shape), pipeline_mode=pl.Buffered(1))


def edges_kernel(x0_ref, x1_ref, og0_ref, og1_ref, cov0_ref, cov1_ref, first_ref, last_ref):
    for x_ref, og_ref, cov_ref, out in (
        (x0_ref, og0_ref, cov0_ref, first_ref),
        (x1_ref, og1_ref, cov1_ref, last_ref),
    ):
        out[0] = x_ref[...]
        out[1] = (og_ref[...].astype(F32) * cov_ref[:, :, 0:1][:, None]).astype(BF16)


def edges(x, og, cov):
    rows, hgt, width, ch = x.shape
    part = (rows, hgt, EDGE, ch)
    end = width // EDGE - 1

    def at(shape, block):
        index = (0,) * (len(shape) - 2) + (block, 0)
        return pl.BlockSpec(shape, lambda i: index)

    cov_part = (rows, EDGE, cov.shape[2])
    return pl.pallas_call(
        edges_kernel,
        out_shape=[jax.ShapeDtypeStruct((2,) + part, BF16)] * 2,
        grid=(1,),
        in_specs=[at(part, 0), at(part, end), at(part, 0), at(part, end), at(cov_part, 0), at(cov_part, end)],
        out_specs=[full((2,) + part)] * 2,
        compiler_params=params(60),
        name="edge_columns",
    )(x, x, og, og, cov, cov)


def forward_kernel(
    ends, x_ref, lo_ref, hi_ref, og_ref, cov_ref, wr_ref, wc_ref, we_ref, inner_ref, outer_ref,
    mz_ref, h2_ref, h1_ref, pad_ref, seed_ref, xs, hs, patches, ss,
):
    rows, hgt, width, ch = x_ref.shape
    inner_w = wr_ref.shape[1]
    wide = width + 2 * RIM
    per_row = hgt * wide
    hs[:, 0] = jnp.zeros((rows, width + 2 * EDGE, inner_w), F32)
    hs[:, hgt + 1] = jnp.zeros((rows, width + 2 * EDGE, inner_w), F32)
    sides = (
        (lo_ref.at[0], 0, ends[0]),
        (x_ref, EDGE, None),
        (hi_ref.at[0], EDGE + width, ends[1]),
    )
    for ref, at, keep in sides:
        part = ref[...]
        cols = part.shape[2]
        xs[:, :, at : at + cols] = part.astype(F32)
        pre = dot(part.astype(F32).reshape(-1, ch).astype(BF16), wr_ref[...])
        pre = pre * inner_ref[0:1] + inner_ref[1:2]
        hid = jnp.maximum(pre, 0.0).astype(BF16).astype(F32)
        if keep is not None:
            hid = hid * keep.astype(F32)
        hs[:, 1 : hgt + 1, at : at + cols] = hid.reshape(rows, hgt, cols, inner_w)
    pad_ref[...] = hs[...].astype(BF16)
    first = EDGE - RIM - 1
    for k in range(9):
        dr, dc = divmod(k, 3)
        piece = hs[:, dr : dr + hgt, first + dc : first + dc + wide]
        piece = piece.reshape(-1, inner_w).astype(BF16)
        patches[:, k * inner_w : (k + 1) * inner_w] = piece
        if k == 4:
            h1_ref[...] = piece.reshape(rows, hgt * wide, inner_w)
    pre = dot(patches[...], wc_ref[...]) * inner_ref[2:3] + inner_ref[3:4]
    hid = jnp.maximum(pre, 0.0).astype(BF16)
    h2_ref[...] = hid.reshape(rows, hgt * wide, inner_w)
    for r in range(rows):
        part = hid[r * per_row : (r + 1) * per_row]
        z = dot(part, we_ref[...]) * outer_ref[0:1] + outer_ref[1:2]
        z = z + xs[r, :, EDGE - RIM : EDGE - RIM + wide].reshape(per_row, ch)
        mz_ref[r] = jnp.where(z > 0, 1.0, 0.0).astype(BF16)
        ss[:, 0:EDGE] = lo_ref[1, r].astype(F32)
        ss[:, EDGE : EDGE + width] = og_ref[r].astype(F32) * cov_ref[r, :, 0:1][None]
        ss[:, EDGE + width :] = hi_ref[1, r].astype(F32)
        seed_ref[r] = ss[:, EDGE - RIM : EDGE - RIM + wide].reshape(per_row, ch).astype(BF16)


def forward(ends, x, lo, hi, og, cov, wr, wc, we, inner, outer):
    rows, hgt, width, ch = x.shape
    inner_w = wr.shape[1]
    wide = width + 2 * RIM
    pos = hgt * wide
    out_shapes = (
        (rows, pos, ch),
        (rows, pos, inner_w),
        (rows, pos, inner_w),
        (rows, hgt + 2, width + 2 * EDGE, inner_w),
        (rows, pos, ch),
    )
    args = (x, lo, hi, og, cov, wr, wc, we, inner, outer)
    return pl.pallas_call(
        forward_kernel,
        out_shape=[jax.ShapeDtypeStruct(s, BF16) for s in out_shapes],
        grid_spec=pltpu.PrefetchScalarGridSpec(
            num_scalar_prefetch=1,
            grid=(1,),
            in_specs=[full(a.shape) for a in args],
            out_specs=[full(s) for s in out_shapes],
            scratch_shapes=[
                pltpu.VMEM((rows, hgt, width + 2 * EDGE, ch), F32),
                pltpu.VMEM((rows, hgt + 2, width + 2 * EDGE, inner_w), F32),
                pltpu.VMEM((rows * pos, 9 * inner_w), BF16),
                pltpu.VMEM((hgt, width + 2 * EDGE, ch), F32),
            ],
        ),
        compiler_params=params(32),
        cost_estimate=pl.CostEstimate(flops=2_000_000_000, bytes_accessed=12_000_000, transcendentals=0),
        name="forward_all_rows",
    )(ends, *args)


def chain_kernel(
    info, gy_ref, seed_ref, mz_ref, h2_ref, h1_ref, wet_ref, wct_ref, wrt_ref, inner_ref, outer_ref,
    wire_ref, gi_ref, g3_ref, g2_ref, g1_ref, wide_s, pad_s,
):
    pos, ch = gy_ref.shape
    inner_w = wet_ref.shape[1]
    hgt, wide = wide_s.shape[:2]
    width = wide - 2 * RIM
    lead = 8

    def center(value):
        lanes = value.shape[1]
        wide_s[:, :, :lanes] = value.reshape(hgt, wide, lanes)
        return wide_s[:, RIM : RIM + width, :lanes].reshape(hgt * width, lanes).astype(BF16)

    gy = jnp.where(info[1] == 1, seed_ref[0], gy_ref[...]).astype(F32)
    gz = gy * mz_ref[0].astype(F32)
    g3 = (gz * outer_ref[0:1]).astype(BF16)
    g3_ref[...] = center(g3.astype(F32))
    g2 = jnp.where(h2_ref[0].astype(F32) > 0, dot(g3, wet_ref[...]) * inner_ref[2:3], 0.0)
    g2 = g2.astype(BF16).astype(F32)
    pad_s[...] = jnp.zeros_like(pad_s)
    pad_s[1 : hgt + 1, lead : lead + wide] = g2.reshape(hgt, wide, inner_w)
    g2_ref[...] = (
        pad_s[1 : hgt + 1, lead + RIM : lead + RIM + width].reshape(hgt * width, inner_w).astype(BF16)
    )
    pieces = []
    for k in range(9):
        dr, dc = divmod(k, 3)
        piece = pad_s[2 - dr : 2 - dr + hgt, lead + 1 - dc : lead + 1 - dc + wide]
        pieces.append(piece.reshape(pos, inner_w).astype(BF16))
    back = dot(jnp.concatenate(pieces, axis=1), wct_ref[...])
    g1 = jnp.where(h1_ref[0].astype(F32) > 0, back * inner_ref[0:1], 0.0).astype(BF16)
    g1_ref[...] = center(g1.astype(F32))
    gi = gz + dot(g1, wrt_ref[...])
    wire_ref[...] = gi.astype(BF16)
    gi_ref[...] = center(gi)


def chain_step(info, gy, seed, mz, h2, h1, wet, wct, wrt, inner, outer, hgt):
    pos, ch = gy.shape
    inner_w = wet.shape[1]
    wide = pos // hgt
    kept = hgt * (wide - 2 * RIM)

    def row(lanes):
        return pl.BlockSpec((1, pos, lanes), lambda i, info: (info[0], 0, 0))

    const = (wet, wct, wrt, inner, outer)
    out_shapes = (gy.shape, (kept, ch), (kept, ch), (kept, inner_w), (kept, inner_w))
    return pl.pallas_call(
        chain_kernel,
        out_shape=[jax.ShapeDtypeStruct(s, BF16) for s in out_shapes],
        grid_spec=pltpu.PrefetchScalarGridSpec(
            num_scalar_prefetch=1,
            grid=(1,),
            in_specs=[full(gy.shape), row(ch), row(ch), row(inner_w), row(inner_w)]
            + [full(c.shape) for c in const],
            out_specs=[full(s) for s in out_shapes],
            scratch_shapes=[
                pltpu.VMEM((hgt, wide, ch), F32),
                pltpu.VMEM((hgt + 2, wide + 16, inner_w), F32),
            ],
        ),
        compiler_params=params(24),
        cost_estimate=pl.CostEstimate(flops=360_000_000, bytes_accessed=5_000_000, transcendentals=0),
        name="chain_row",
    )(info, gy, seed, mz, h2, h1, *const)


def picks(inner_w, z):
    row = jnp.arange(inner_w)
    each = row % 4
    own = jnp.asarray(Z_ORDER, row.dtype)[(row // 4) % Z] ^ z
    mid = (row // (4 * Z)) % 4
    core = row // (4 * Z * 4)
    whole = ((mid * Z + own) * CORES + core) * 4 + each
    part = (own * CORES + core) * 16 + mid * 4 + each
    return (jnp.stack([whole, part])[:, :, None] == row[None, None]).astype(BF16)


def turn_kernel(x_ref, pad_ref, h2_ref, pick_ref, xt_ref, pt_ref, ht_ref):
    rows, hgt, width, ch = x_ref.shape
    inner_w = h2_ref.shape[2]
    half = inner_w // CORES
    wide = width + 2 * RIM

    def turned(order, value, ref, at, stride):
        out = lax.dot_general(
            pick_ref[order], value, (((1,), (1,)), ((), ())), preferred_element_type=F32
        ).astype(BF16)
        for core in range(CORES):
            ref[core * stride + at : core * stride + at + half] = out[core * half : (core + 1) * half]

    flat = x_ref[...].astype(F32).reshape(-1, ch).astype(BF16)
    for part in range(ch // inner_w):
        turned(1, flat[:, part * inner_w : (part + 1) * inner_w], xt_ref, part * half, ch // CORES)
    padded = pad_ref[...].astype(F32)
    for k in range(9):
        dr, dc = divmod(k, 3)
        piece = padded[:, dr : dr + hgt, EDGE - 1 + dc : EDGE - 1 + dc + width]
        turned(0, piece.reshape(-1, inner_w).astype(BF16), pt_ref, k * half, 9 * half)
    h2 = h2_ref[...].astype(F32).reshape(rows * hgt, wide, inner_w)[:, RIM : RIM + width]
    turned(0, h2.reshape(-1, inner_w).astype(BF16), ht_ref, 0, half)


def turn(x, pad, h2, pick):
    rows, hgt, width, ch = x.shape
    inner_w = h2.shape[2]
    pos = rows * hgt * width
    args = (x, pad, h2, pick)
    shapes = ((ch, pos), (9 * inner_w, pos), (inner_w, pos))
    return pl.pallas_call(
        turn_kernel,
        out_shape=[jax.ShapeDtypeStruct(s, BF16) for s in shapes],
        grid=(1,),
        in_specs=[full(a.shape) for a in args],
        out_specs=[full(s) for s in shapes],
        compiler_params=params(32),
        cost_estimate=pl.CostEstimate(flops=2_000_000_000, bytes_accessed=8_000_000, transcendentals=0),
        name="turn_activations",
    )(*args)


def place(segment, target, x):
    as_int = lambda cond: jnp.where(cond, 1, 0)
    if segment < A_SEGS:
        side = as_int((x == 1) | (x == 2))
        keep = as_int(side == (1 if target in (1, 2) else 0))
        last = as_int(x // 2 == target // 2)
        return ((keep * 2 + last) * A_SEGS + segment) * 32
    keep = as_int(x // 2 == target // 2)
    same = as_int(x % 2 == target % 2)
    last = jnp.where(keep == 1, same, 1 - same)
    return X * A_SEGS * 32 + ((keep * 2 + last) * (SEGS - A_SEGS) + segment - A_SEGS) * 32


def weights_kernel(slots, info, xt_ref, pt_ref, ht_ref, *refs):
    by_slot = [refs[i * slots : (i + 1) * slots] for i in range(4)]
    keep_ref, send_ref, gi_ref, g3_s, g2_s, g1_s, sems = refs[4 * slots :]
    core, x, section = info[0], info[1], info[2]
    rows, kept, ch = gi_ref.shape
    inner_w = ht_ref.shape[0]
    half = inner_w // CORES
    into = (g1_s, g2_s, g3_s, gi_ref)

    def copy(which, r, slot):
        return pltpu.make_async_copy(by_slot[which][slot], into[which].at[r], sems.at[which, r])

    sections = (slots - rows) // LAG + 1
    for s in range(sections):
        @pl.when(section == s)
        def _():
            for which in range(4):
                for r in range(rows):
                    copy(which, r, LAG * (sections - 1 - s) + r).start()

    def arrived(which):
        for r in range(rows):
            copy(which, r, r).wait()
        if which < 3:
            return into[which][...].reshape(rows * kept, into[which].shape[2])

    outs = ((keep_ref, core), (send_ref, 1 - core))

    def put(ref, target, segment, value):
        at = pl.multiple_of(place(segment, target, x), 32)
        ref[pl.ds(at, value.shape[0])] = value.astype(BF16)

    g1 = arrived(0)
    for ref, side in outs:
        total = dot(xt_ref[pl.ds(pl.multiple_of(side * (ch // CORES), half), ch // CORES)], g1)
        for target in range(X):
            put(ref, target, 0, total[target * half : (target + 1) * half])
    g2 = arrived(1)
    for ref, side in outs:
        total = dot(pt_ref[pl.ds(pl.multiple_of(side * 9 * half, half), 9 * half)], g2)
        for k in range(9):
            for target in range(X):
                at = k * half + target * 32
                put(ref, target, 4 + k, total[at : at + 32])
    g3 = arrived(2)
    for ref, side in outs:
        total = dot(ht_ref[pl.ds(pl.multiple_of(side * half, half), half)], g3)
        for j in range(4):
            for target in range(X):
                part = total[target * 32 : target * 32 + 32, j * inner_w : (j + 1) * inner_w]
                put(ref, target, 13 + j, part)
    arrived(3)


def weight_grads(info, xt, pt, ht, g1, g2, g3, gi, rows):
    inner_w = ht.shape[0]
    slots = len(gi)
    kept, ch = gi[0].shape
    shape = (SEGS * X * 32, inner_w)
    args = (xt, pt, ht)
    return pl.pallas_call(
        functools.partial(weights_kernel, slots),
        out_shape=[jax.ShapeDtypeStruct(s, BF16) for s in (shape, shape, (rows, kept, ch))],
        grid_spec=pltpu.PrefetchScalarGridSpec(
            num_scalar_prefetch=1,
            grid=(1,),
            in_specs=[full(a.shape) for a in args] + [pl.BlockSpec(memory_space=pl.ANY)] * (4 * slots),
            out_specs=[full(shape), full(shape), pl.BlockSpec(memory_space=pl.ANY)],
            scratch_shapes=[
                pltpu.VMEM((rows, kept, ch), BF16),
                pltpu.VMEM((rows, kept, inner_w), BF16),
                pltpu.VMEM((rows, kept, inner_w), BF16),
                pltpu.SemaphoreType.DMA((4, rows)),
            ],
        ),
        compiler_params=params(32),
        cost_estimate=pl.CostEstimate(flops=1_200_000_000, bytes_accessed=8_000_000, transcendentals=0),
        name="weight_gradients",
    )(info, *args, *g1, *g2, *g3, *gi)


def tile_pairs(partner):
    pairs = []
    for x in range(X):
        for z in range(Z):
            for c in range(CORES):
                px, pz, pc = partner(x, z, c)
                pairs.append(((x * Z + z) * CORES + c, (px * Z + pz) * CORES + pc))
    return pairs


def swap(value, partner):
    return lax.ppermute(value.astype(BF16), "tile", tile_pairs(partner))


def scatter_sum(keep, send):
    lanes = keep.shape[-1]
    got = swap(send, lambda x, z, c: (x, z, 1 - c))
    inner_pair = lambda x, z, c: (x ^ 1, z, c)
    outer_pair = lambda x, z, c: (3 - x, z, c)
    cut = X * A_SEGS * 32

    def own(first, last):
        return keep[first:last].astype(F32) + got[first:last].astype(F32)

    half_a, half_b = cut // 2, (keep.shape[0] - cut) // 2
    quart_a, quart_b = half_a // 2, half_b // 2
    got_a = swap(own(0, half_a), inner_pair)
    got_b = swap(own(cut, cut + half_b), outer_pair)
    at_a, at_b = half_a, cut + half_b
    got_a2 = swap(own(at_a, at_a + quart_a) + got_a[:quart_a].astype(F32), outer_pair)
    got_b2 = swap(own(at_b, at_b + quart_b) + got_b[:quart_b].astype(F32), inner_pair)
    part_a = own(at_a + quart_a, cut) + got_a[quart_a:].astype(F32) + got_a2.astype(F32)
    part_b = own(at_b + quart_b, keep.shape[0]) + got_b[quart_b:].astype(F32) + got_b2.astype(F32)
    total = jnp.concatenate([part_a, part_b], axis=0).reshape(SEGS, Z * 4, lanes)
    for bit in (1, 2, 4):
        count = total.shape[1] // 2
        got = swap(total[:, :count], lambda x, z, c, b=bit: (x, z ^ b, c))
        total = total[:, count:] + got.astype(F32)
    g_reduce = total[:4].reshape(16, lanes)
    g_conv = total[4:13].reshape(3, 3, 4, lanes)
    g_expand = total[13:].transpose(1, 0, 2).reshape(4, 4 * lanes)
    return g_reduce, g_conv, g_expand


def neighbours(first, last, tiles):
    pairs = [(i, i + 1) for i in range(tiles - 1)]
    low = lax.ppermute(last, "tile", pairs)
    high = lax.ppermute(first, "tile", [(b, a) for a, b in pairs])
    return low, high


def per_device(block_inputs, out_grad, tissue, w_reduce, w_conv, w_expand, inner_affine, outer_affine):
    section = lax.axis_index("section")
    sections = lax.axis_size("section")
    tile = lax.axis_index("tile")
    tiles = lax.axis_size("tile")
    x = block_inputs[0]
    rows, hgt, width, ch = x.shape
    wr, we = w_reduce[0], w_expand[0]
    inner_w = wr.shape[1]
    wc = w_conv[0].reshape(9 * inner_w, inner_w)
    inner, outer = inner_affine[0], outer_affine[0]
    pos = hgt * (width + 2 * RIM)

    cover = jnp.repeat(tissue.astype(F32), TILE_W, axis=1)[:, :, None]
    cover = jnp.broadcast_to(cover, (rows, width, 128))
    lo, hi = neighbours(*edges(x, out_grad, cover), tiles)

    wet = we.T
    wrt = wr.T
    wct = w_conv[0].transpose(0, 1, 3, 2).reshape(9 * inner_w, inner_w)

    ends = jnp.stack([tile > 0, tile < tiles - 1]).astype(jnp.int32)
    mz, h2, h1, pad, seed = forward(
        ends, x, lo, hi, out_grad, cover, wr, wc, we, inner, outer
    )
    z_now = (tile // CORES) % Z
    xt, pt, ht = turn(x, pad, h2, picks(inner_w, z_now))

    back_one = [(i, i - 1) for i in range(1, sections)]
    slots = rows + LAG * (sections - 1)
    arriving = [jnp.zeros((pos, ch), BF16)] * LAG
    per_slot = []
    for slot in range(slots):
        micro = slot - LAG * (sections - 1 - section)
        info = jnp.stack(
            [jnp.clip(micro, 0, rows - 1), (section == sections - 1).astype(micro.dtype)]
        ).astype(jnp.int32)
        wire, *saved = chain_step(
            info, arriving[slot], seed, mz, h2, h1, wet, wct, wrt, inner, outer, hgt
        )
        per_slot.append(saved)
        if slot + LAG < slots:
            arriving.append(lax.ppermute(wire, "section", back_one))
    gi, g3, g2, g1 = zip(*per_slot)
    info = jnp.stack([tile % CORES, tile // (CORES * Z), section]).astype(jnp.int32)
    keep, send, grad_inputs = weight_grads(info, xt, pt, ht, g1, g2, g3, gi, rows)
    g_reduce, g_conv, g_expand = scatter_sum(keep, send)
    grad_inputs = grad_inputs.reshape(rows, hgt, width, ch)
    return grad_inputs[None], g_reduce[None], g_conv[None], g_expand[None]


def solution(mesh):
    in_specs = (
        P("section", None, None, "tile", None),
        P(None, None, "tile", None),
        P(None, "tile"),
        P("section", None, None),
        P("section", None, None, None, None),
        P("section", None, None),
        P("section", None, None),
        P("section", None, None),
    )
    out_specs = (
        P("section", None, None, "tile", None),
        P("section", "tile", None),
        P("section", None, None, "tile", None),
        P("section", "tile", None),
    )
    return jax.shard_map(
        per_device, mesh=mesh, in_specs=in_specs, out_specs=out_specs, check_vma=False
    )
```

```python
import functools

import jax
import jax.numpy as jnp
from jax import lax
from jax.experimental import pallas as pl
from jax.experimental.pallas import tpu as pltpu
from jax.sharding import PartitionSpec as P

TILE_W = 8
X, Z, CORES = 4, 8, 2
EDGE = 8
RIM = 4
BF16, F32 = jnp.bfloat16, jnp.float32
LAG = 2
SEGS, A_SEGS = 17, 8
Z_ORDER = (7, 3, 5, 1, 6, 2, 4, 0)


def params(mib):
    return pltpu.CompilerParams(vmem_limit_bytes=mib * 1024 * 1024)


def dot(left, right):
    return jnp.dot(left, right, preferred_element_type=F32)


def dot_t(left, right):
    return lax.dot_general(left, right, (((1,), (1,)), ((), ())), preferred_element_type=F32)


def full(shape):
    return pl.BlockSpec(shape, lambda *_: (0,) * len(shape), pipeline_mode=pl.Buffered(1))


def edges_kernel(tissue, x0_ref, x1_ref, og0_ref, og1_ref, first_ref, last_ref):
    rows, hgt = x0_ref.shape[:2]
    for x_ref, og_ref, out, tile, at in (
        (x0_ref, og0_ref, first_ref, 0, 0),
        (x1_ref, og1_ref, last_ref, tissue.shape[1] - 1, EDGE - RIM),
    ):
        out[:, :hgt] = x_ref[...]
        for r in range(rows):
            seed = og_ref[r].astype(F32)[:, at : at + RIM] * tissue[r, tile].astype(F32)
            for pair in range(hgt // 2):
                both = jnp.concatenate([seed[2 * pair], seed[2 * pair + 1]], axis=0)
                out[r, hgt + pair] = both.astype(BF16)


def edges(tissue, x, og):
    rows, hgt, width, ch = x.shape
    part = (rows, hgt, EDGE, ch)
    out = (rows, hgt + hgt // 2, EDGE, ch)
    end = width // EDGE - 1

    def at(block):
        return pl.BlockSpec(part, lambda i, tissue: (0, 0, block, 0))

    return pl.pallas_call(
        edges_kernel,
        out_shape=[jax.ShapeDtypeStruct(out, BF16)] * 2,
        grid_spec=pltpu.PrefetchScalarGridSpec(
            num_scalar_prefetch=1,
            grid=(1,),
            in_specs=[at(0), at(end), at(0), at(end)],
            out_specs=[full(out)] * 2,
        ),
        compiler_params=params(60),
        name="edge_columns",
    )(tissue, x, x, og, og)


def hidden_one(part, wr, inner_ref):
    rows, hgt, cols, ch = part.shape
    flat = part.astype(F32).reshape(-1, ch).astype(BF16)
    pre = dot(flat, wr) * inner_ref[0:1] + inner_ref[1:2]
    return jnp.maximum(pre, 0.0).astype(BF16).astype(F32).reshape(rows, hgt, cols, -1)


def inside_kernel(x_ref, wr_ref, inner_ref, og_ref, wc_ref, we_ref, h1_ref, *kept):
    h1_ref[...] = hidden_one(x_ref[...], wr_ref[...], inner_ref).astype(BF16)
    for ref, out in zip((x_ref, og_ref, wr_ref, wc_ref, we_ref), kept):
        out[...] = ref[...]


def inside(x, wr, inner, og, wc, we):
    args = (x, wr, inner, og, wc, we)
    shapes = (x.shape[:3] + (wr.shape[1],),) + tuple(a.shape for a in (x, og, wr, wc, we))
    return pl.pallas_call(
        inside_kernel,
        out_shape=[jax.ShapeDtypeStruct(s, BF16) for s in shapes],
        grid=(1,),
        in_specs=[full(a.shape) for a in args],
        out_specs=[full(s) for s in shapes],
        compiler_params=params(12),
        cost_estimate=pl.CostEstimate(flops=300_000_000, bytes_accessed=9_000_000, transcendentals=0),
        name="forward_own_columns",
    )(*args)


def forward_kernel(
    ends, tissue, lo_ref, hi_ref, own_ref, inner_ref, outer_ref, x_ref, og_ref, wr_ref, wc_ref, we_ref,
    mz_ref, h2_ref, h1_ref, pad_ref, seed_ref,
    xs, hs, patches, ss,
):
    rows, hgt, width, ch = x_ref.shape
    inner_w = wr_ref.shape[1]
    wide = width + 2 * RIM
    per_row = hgt * wide
    hs[:, 0] = jnp.zeros((rows, width + 2 * EDGE, inner_w), F32)
    hs[:, hgt + 1] = jnp.zeros((rows, width + 2 * EDGE, inner_w), F32)
    hs[:, 1 : hgt + 1, EDGE : EDGE + width] = own_ref[...].astype(F32)
    for ref, at, keep in ((lo_ref, 0, ends[0]), (hi_ref, EDGE + width, ends[1])):
        part = ref[:, :hgt]
        xs[:, :, at : at + EDGE] = part.astype(F32)
        hs[:, 1 : hgt + 1, at : at + EDGE] = hidden_one(part, wr_ref[...], inner_ref) * keep.astype(F32)
    pad_ref[...] = hs[...].astype(BF16)
    first = EDGE - RIM - 1
    for k in range(9):
        dr, dc = divmod(k, 3)
        piece = hs[:, dr : dr + hgt, first + dc : first + dc + wide]
        piece = piece.reshape(-1, inner_w).astype(BF16)
        patches[:, k * inner_w : (k + 1) * inner_w] = piece
        if k == 4:
            h1_ref[...] = piece.reshape(rows, hgt * wide, inner_w)
    pre = dot(patches[...], wc_ref[...]) * inner_ref[2:3] + inner_ref[3:4]
    hid = jnp.maximum(pre, 0.0).astype(BF16)
    h2_ref[...] = hid.reshape(rows, hgt * wide, inner_w)
    xs[:, :, EDGE : EDGE + width] = x_ref[...].astype(F32)
    for r in range(rows):
        part = hid[r * per_row : (r + 1) * per_row]
        z = dot(part, we_ref[...]) * outer_ref[0:1] + outer_ref[1:2]
        z = z + xs[r, :, EDGE - RIM : EDGE - RIM + wide].reshape(per_row, ch)
        mz_ref[r] = jnp.where(z > 0, 1.0, 0.0).astype(BF16)
        for ref, at in ((lo_ref, 0), (hi_ref, RIM + width)):
            for pair in range(hgt // 2):
                both = ref[r, hgt + pair].astype(F32)
                ss[2 * pair, at : at + RIM] = both[:RIM]
                ss[2 * pair + 1, at : at + RIM] = both[RIM:]
        og = og_ref[r].astype(F32)
        for tile in range(width // TILE_W):
            cols = og[:, tile * TILE_W : (tile + 1) * TILE_W] * tissue[r, tile].astype(F32)
            ss[:, RIM + tile * TILE_W : RIM + (tile + 1) * TILE_W] = cols
        seed_ref[r] = ss[...].reshape(per_row, ch).astype(BF16)


def forward(ends, tissue, lo, hi, own, inner, outer, x, og, wr, wc, we):
    rows, hgt, width, ch = x.shape
    inner_w = wr.shape[1]
    wide = width + 2 * RIM
    pos = hgt * wide
    out_shapes = (
        (rows, pos, ch),
        (rows, pos, inner_w),
        (rows, pos, inner_w),
        (rows, hgt + 2, width + 2 * EDGE, inner_w),
        (rows, pos, ch),
    )
    blocks = (lo, hi, own, inner, outer, x, og, wr, wc, we)
    return pl.pallas_call(
        forward_kernel,
        out_shape=[jax.ShapeDtypeStruct(s, BF16) for s in out_shapes],
        grid_spec=pltpu.PrefetchScalarGridSpec(
            num_scalar_prefetch=2,
            grid=(1,),
            in_specs=[full(a.shape) for a in blocks],
            out_specs=[full(s) for s in out_shapes],
            scratch_shapes=[
                pltpu.VMEM((rows, hgt, width + 2 * EDGE, ch), F32),
                pltpu.VMEM((rows, hgt + 2, width + 2 * EDGE, inner_w), F32),
                pltpu.VMEM((rows * pos, 9 * inner_w), BF16),
                pltpu.VMEM((hgt, wide, ch), F32),
            ],
        ),
        compiler_params=params(20),
        cost_estimate=pl.CostEstimate(flops=2_000_000_000, bytes_accessed=12_000_000, transcendentals=0),
        name="forward_all_rows",
    )(ends, tissue, *blocks)


def chain_kernel(
    info, gy_ref, seed_ref, mz_ref, h2_ref, h1_ref, we_ref, wc_ref, wr_ref, inner_ref, outer_ref,
    gi_ref, g3_ref, g2_ref, g1_ref, *more,
):
    *wire_ref, wide_s, pad_s = more
    inner_w = we_ref.shape[0]
    hgt, wide, ch = wide_s.shape
    pos = hgt * wide
    width = wide - 2 * RIM
    lead = 8

    def center(value):
        lanes = value.shape[1]
        wide_s[:, :, :lanes] = value.reshape(hgt, wide, lanes)
        return wide_s[:, RIM : RIM + width, :lanes].reshape(hgt * width, lanes).astype(BF16)

    gy = jnp.where(info[1] == 1, seed_ref[0], gy_ref[...]).astype(F32)
    gz = gy * mz_ref[0].astype(F32)
    g3 = (gz * outer_ref[0:1]).astype(BF16)
    g3_ref[...] = center(g3.astype(F32))
    g2 = jnp.where(h2_ref[0].astype(F32) > 0, dot_t(g3, we_ref[...]) * inner_ref[2:3], 0.0)
    g2 = g2.astype(BF16).astype(F32)
    pad_s[...] = jnp.zeros_like(pad_s)
    pad_s[1 : hgt + 1, lead : lead + wide] = g2.reshape(hgt, wide, inner_w)
    g2_ref[...] = (
        pad_s[1 : hgt + 1, lead + RIM : lead + RIM + width].reshape(hgt * width, inner_w).astype(BF16)
    )
    back = jnp.zeros((pos, inner_w), F32)
    for k in range(9):
        dr, dc = divmod(k, 3)
        piece = pad_s[2 - dr : 2 - dr + hgt, lead + 1 - dc : lead + 1 - dc + wide]
        back = back + dot_t(piece.reshape(pos, inner_w).astype(BF16), wc_ref[k * inner_w : (k + 1) * inner_w])
    g1 = jnp.where(h1_ref[0].astype(F32) > 0, back * inner_ref[0:1], 0.0).astype(BF16)
    g1_ref[...] = center(g1.astype(F32))
    gi = gz + dot_t(g1, wr_ref[...])
    if wire_ref:
        wire_ref[0][...] = gi.astype(BF16)
    gi_ref[...] = center(gi)


def chain_step(info, gy, seed, mz, h2, h1, we, wc, wr, inner, outer, hgt, hand_on):
    pos, ch = seed.shape[1:]
    inner_w = we.shape[0]
    wide = pos // hgt
    kept = hgt * (wide - 2 * RIM)

    def row(lanes):
        return pl.BlockSpec((1, pos, lanes), lambda i, info: (info[0], 0, 0))

    const = (we, wc, wr, inner, outer)
    out_shapes = [(kept, ch), (kept, ch), (kept, inner_w), (kept, inner_w)] + [gy.shape] * hand_on
    return pl.pallas_call(
        chain_kernel,
        out_shape=[jax.ShapeDtypeStruct(s, BF16) for s in out_shapes],
        grid_spec=pltpu.PrefetchScalarGridSpec(
            num_scalar_prefetch=1,
            grid=(1,),
            in_specs=[full(gy.shape), row(ch), row(ch), row(inner_w), row(inner_w)]
            + [full(c.shape) for c in const],
            out_specs=[full(s) for s in out_shapes],
            scratch_shapes=[
                pltpu.VMEM((hgt, wide, ch), F32),
                pltpu.VMEM((hgt + 2, wide + 16, inner_w), F32),
            ],
        ),
        compiler_params=params(12),
        cost_estimate=pl.CostEstimate(flops=360_000_000, bytes_accessed=5_000_000, transcendentals=0),
        name="chain_row",
    )(info, gy, seed, mz, h2, h1, *const)


def picks(inner_w, z):
    row = jnp.arange(inner_w)
    each = row % 4
    own = jnp.asarray(Z_ORDER, row.dtype)[(row // 4) % Z] ^ z
    mid = (row // (4 * Z)) % 4
    core = row // (4 * Z * 4)
    whole = ((mid * Z + own) * CORES + core) * 4 + each
    part = (own * CORES + core) * 16 + mid * 4 + each
    return (jnp.stack([whole, part])[:, :, None] == row[None, None]).astype(BF16)


def turn_kernel(x_ref, pad_ref, h2_ref, pick_ref, xt_ref, pt_ref, ht_ref):
    rows, hgt, width, ch = x_ref.shape
    inner_w = h2_ref.shape[2]
    half = inner_w // CORES
    wide = width + 2 * RIM

    def turned(order, value, ref, at, stride):
        out = lax.dot_general(
            pick_ref[order], value, (((1,), (1,)), ((), ())), preferred_element_type=F32
        ).astype(BF16)
        for core in range(CORES):
            ref[core * stride + at : core * stride + at + half] = out[core * half : (core + 1) * half]

    flat = x_ref[...].astype(F32).reshape(-1, ch).astype(BF16)
    for part in range(ch // inner_w):
        turned(1, flat[:, part * inner_w : (part + 1) * inner_w], xt_ref, part * half, ch // CORES)
    padded = pad_ref[...].astype(F32)
    for k in range(9):
        dr, dc = divmod(k, 3)
        piece = padded[:, dr : dr + hgt, EDGE - 1 + dc : EDGE - 1 + dc + width]
        turned(0, piece.reshape(-1, inner_w).astype(BF16), pt_ref, k * half, 9 * half)
    h2 = h2_ref[...].astype(F32).reshape(rows * hgt, wide, inner_w)[:, RIM : RIM + width]
    turned(0, h2.reshape(-1, inner_w).astype(BF16), ht_ref, 0, half)


def turn(x, pad, h2, pick):
    rows, hgt, width, ch = x.shape
    inner_w = h2.shape[2]
    pos = rows * hgt * width
    args = (x, pad, h2, pick)
    shapes = ((ch, pos), (9 * inner_w, pos), (inner_w, pos))
    return pl.pallas_call(
        turn_kernel,
        out_shape=[jax.ShapeDtypeStruct(s, BF16) for s in shapes],
        grid=(1,),
        in_specs=[full(a.shape) for a in args],
        out_specs=[full(s) for s in shapes],
        compiler_params=params(20),
        cost_estimate=pl.CostEstimate(flops=2_000_000_000, bytes_accessed=8_000_000, transcendentals=0),
        name="turn_activations",
    )(*args)


def place(segment, target, x):
    as_int = lambda cond: jnp.where(cond, 1, 0)
    if segment < A_SEGS:
        side = as_int((x == 1) | (x == 2))
        keep = as_int(side == (1 if target in (1, 2) else 0))
        last = as_int(x // 2 == target // 2)
        return ((keep * 2 + last) * A_SEGS + segment) * 32
    keep = as_int(x // 2 == target // 2)
    same = as_int(x % 2 == target % 2)
    last = jnp.where(keep == 1, same, 1 - same)
    return X * A_SEGS * 32 + ((keep * 2 + last) * (SEGS - A_SEGS) + segment - A_SEGS) * 32


def weights_kernel(slots, info, xt_ref, pt_ref, ht_ref, *refs):
    by_slot = [refs[i * slots : (i + 1) * slots] for i in range(4)]
    keep_ref, send_ref, gi_ref, g3_s, g2_s, g1_s, sems = refs[4 * slots :]
    core, x, section = info[0], info[1], info[2]
    rows, kept, ch = gi_ref.shape
    inner_w = ht_ref.shape[0]
    half = inner_w // CORES
    into = (g1_s, g2_s, g3_s, gi_ref)

    def copy(which, r, slot):
        return pltpu.make_async_copy(by_slot[which][slot], into[which].at[r], sems.at[which, r])

    sections = (slots - rows) // LAG + 1
    for s in range(sections):
        @pl.when(section == s)
        def _():
            for which in range(4):
                for r in range(rows):
                    copy(which, r, LAG * (sections - 1 - s) + r).start()

    def arrived(which):
        for r in range(rows):
            copy(which, r, r).wait()
        if which < 3:
            return into[which][...].reshape(rows * kept, into[which].shape[2])

    outs = ((keep_ref, core), (send_ref, 1 - core))

    def put(ref, target, segment, value):
        at = pl.multiple_of(place(segment, target, x), 32)
        ref[pl.ds(at, value.shape[0])] = value.astype(BF16)

    g1 = arrived(0)
    for ref, side in outs:
        total = dot(xt_ref[pl.ds(pl.multiple_of(side * (ch // CORES), half), ch // CORES)], g1)
        for target in range(X):
            put(ref, target, 0, total[target * half : (target + 1) * half])
    g2 = arrived(1)
    for ref, side in outs:
        total = dot(pt_ref[pl.ds(pl.multiple_of(side * 9 * half, half), 9 * half)], g2)
        for k in range(9):
            for target in range(X):
                at = k * half + target * 32
                put(ref, target, 4 + k, total[at : at + 32])
    g3 = arrived(2)
    for ref, side in outs:
        total = dot(ht_ref[pl.ds(pl.multiple_of(side * half, half), half)], g3)
        for j in range(4):
            for target in range(X):
                part = total[target * 32 : target * 32 + 32, j * inner_w : (j + 1) * inner_w]
                put(ref, target, 13 + j, part)
    arrived(3)


def weight_grads(info, xt, pt, ht, g1, g2, g3, gi, rows):
    inner_w = ht.shape[0]
    slots = len(gi)
    kept, ch = gi[0].shape
    shape = (SEGS * X * 32, inner_w)
    args = (xt, pt, ht)
    return pl.pallas_call(
        functools.partial(weights_kernel, slots),
        out_shape=[jax.ShapeDtypeStruct(s, BF16) for s in (shape, shape, (rows, kept, ch))],
        grid_spec=pltpu.PrefetchScalarGridSpec(
            num_scalar_prefetch=1,
            grid=(1,),
            in_specs=[full(a.shape) for a in args] + [pl.BlockSpec(memory_space=pl.ANY)] * (4 * slots),
            out_specs=[full(shape), full(shape), pl.BlockSpec(memory_space=pl.ANY)],
            scratch_shapes=[
                pltpu.VMEM((rows, kept, ch), BF16),
                pltpu.VMEM((rows, kept, inner_w), BF16),
                pltpu.VMEM((rows, kept, inner_w), BF16),
                pltpu.SemaphoreType.DMA((4, rows)),
            ],
        ),
        compiler_params=params(20),
        cost_estimate=pl.CostEstimate(flops=1_200_000_000, bytes_accessed=8_000_000, transcendentals=0),
        name="weight_gradients",
    )(info, *args, *g1, *g2, *g3, *gi)


def tile_pairs(partner):
    pairs = []
    for x in range(X):
        for z in range(Z):
            for c in range(CORES):
                px, pz, pc = partner(x, z, c)
                pairs.append(((x * Z + z) * CORES + c, (px * Z + pz) * CORES + pc))
    return pairs


def swap(value, partner):
    return lax.ppermute(value.astype(BF16), "tile", tile_pairs(partner))


def scatter_sum(keep, send):
    lanes = keep.shape[-1]
    got = swap(send, lambda x, z, c: (x, z, 1 - c))
    inner_pair = lambda x, z, c: (x ^ 1, z, c)
    outer_pair = lambda x, z, c: (3 - x, z, c)
    cut = X * A_SEGS * 32

    def own(first, last):
        return keep[first:last].astype(F32) + got[first:last].astype(F32)

    half_a, half_b = cut // 2, (keep.shape[0] - cut) // 2
    quart_a, quart_b = half_a // 2, half_b // 2
    got_a = swap(own(0, half_a), inner_pair)
    got_b = swap(own(cut, cut + half_b), outer_pair)
    at_a, at_b = half_a, cut + half_b
    got_a2 = swap(own(at_a, at_a + quart_a) + got_a[:quart_a].astype(F32), outer_pair)
    got_b2 = swap(own(at_b, at_b + quart_b) + got_b[:quart_b].astype(F32), inner_pair)
    part_a = own(at_a + quart_a, cut) + got_a[quart_a:].astype(F32) + got_a2.astype(F32)
    part_b = own(at_b + quart_b, keep.shape[0]) + got_b[quart_b:].astype(F32) + got_b2.astype(F32)
    total = jnp.concatenate([part_a, part_b], axis=0).reshape(SEGS, Z * 4, lanes)
    count = Z * 4 // 2
    got = swap(total[:, :count], lambda x, z, c: (x, z ^ 1, c))
    total = total[:, count:] + got.astype(F32)
    shares = [
        swap(total[:, 4 * i : 4 * i + 4], lambda x, z, c, b=Z_ORDER[Z // 2 + i]: (x, z ^ b, c))
        for i in range(Z // 2 - 1)
    ]
    return finish(total[:, count - 4 :], shares)


def finish_kernel(own_ref, *refs):
    reduce_ref, conv_ref, expand_ref = refs[-3:]
    total = own_ref[...]
    for ref in refs[:-3]:
        total = total + ref[...].astype(F32)
    lanes = total.shape[2]
    for q in range(4):
        reduce_ref[4 * q : 4 * q + 4] = total[q]
        expand_ref[:, q * lanes : (q + 1) * lanes] = total[13 + q]
    conv_ref[...] = total[4:13]


def finish(own, shares):
    lanes = own.shape[2]
    shapes = ((16, lanes), (9, 4, lanes), (4, 4 * lanes))
    args = (own, *shares)
    g_reduce, g_conv, g_expand = pl.pallas_call(
        finish_kernel,
        out_shape=[jax.ShapeDtypeStruct(s, F32) for s in shapes],
        grid=(1,),
        in_specs=[full(a.shape) for a in args],
        out_specs=[full(s) for s in shapes],
        compiler_params=params(4),
        name="finish_gradients",
    )(*args)
    return g_reduce, g_conv.reshape(3, 3, 4, lanes), g_expand


def neighbours(first, last, tiles):
    pairs = [(i, i + 1) for i in range(tiles - 1)]
    low = lax.ppermute(last, "tile", pairs)
    high = lax.ppermute(first, "tile", [(b, a) for a, b in pairs])
    return low, high


def per_device(block_inputs, out_grad, tissue, w_reduce, w_conv, w_expand, inner_affine, outer_affine):
    section = lax.axis_index("section")
    sections = lax.axis_size("section")
    tile = lax.axis_index("tile")
    tiles = lax.axis_size("tile")
    x = block_inputs[0]
    rows, hgt, width, ch = x.shape
    wr, we = w_reduce[0], w_expand[0]
    inner_w = wr.shape[1]
    wc = w_conv[0].reshape(9 * inner_w, inner_w)
    inner, outer = inner_affine[0], outer_affine[0]

    lo, hi = neighbours(*edges(tissue, x, out_grad), tiles)
    own, *at_hand = inside(x, wr, inner, out_grad, wc, we)

    ends = jnp.stack([tile > 0, tile < tiles - 1]).astype(jnp.int32)
    mz, h2, h1, pad, seed = forward(
        ends, tissue, lo, hi, own, inner, outer, *at_hand
    )
    z_now = (tile // CORES) % Z
    xt, pt, ht = turn(x, pad, h2, picks(inner_w, z_now))

    back_one = [(i, i - 1) for i in range(1, sections)]
    slots = rows + LAG * (sections - 1)
    arriving = [jnp.zeros((hgt * (width + 2 * RIM), ch), BF16)] * LAG
    per_slot = []
    for slot in range(slots):
        micro = slot - LAG * (sections - 1 - section)
        info = jnp.stack(
            [jnp.clip(micro, 0, rows - 1), (section == sections - 1).astype(micro.dtype)]
        ).astype(jnp.int32)
        hand_on = slot + LAG < slots
        *saved, last = chain_step(
            info, arriving[slot], seed, mz, h2, h1, at_hand[4], at_hand[3], at_hand[2], inner, outer, hgt, hand_on
        )
        if hand_on:
            arriving.append(lax.ppermute(last, "section", back_one))
        else:
            saved.append(last)
        per_slot.append(saved)
    gi, g3, g2, g1 = zip(*per_slot)
    info = jnp.stack([tile % CORES, tile // (CORES * Z), section]).astype(jnp.int32)
    keep, send, grad_inputs = weight_grads(info, xt, pt, ht, g1, g2, g3, gi, rows)
    g_reduce, g_conv, g_expand = scatter_sum(keep, send)
    grad_inputs = grad_inputs.reshape(rows, hgt, width, ch)
    return grad_inputs[None], g_reduce[None], g_conv[None], g_expand[None]


def solution(mesh):
    in_specs = (
        P("section", None, None, "tile", None),
        P(None, None, "tile", None),
        P(None, "tile"),
        P("section", None, None),
        P("section", None, None, None, None),
        P("section", None, None),
        P("section", None, None),
        P("section", None, None),
    )
    out_specs = (
        P("section", None, None, "tile", None),
        P("section", "tile", None),
        P("section", None, None, "tile", None),
        P("section", "tile", None),
    )
    return jax.shard_map(
        per_device, mesh=mesh, in_specs=in_specs, out_specs=out_specs, check_vma=False
    )
```

```python
import functools

import jax
import jax.numpy as jnp
from jax import lax
from jax.experimental import pallas as pl
from jax.experimental.pallas import tpu as pltpu
from jax.sharding import PartitionSpec as P

TILE_W = 8
SECTIONS = 4
X, Z, CORES = 4, 8, 2
EDGE = 8
RIM = 4
BF16, F32 = jnp.bfloat16, jnp.float32
LAG = 2
SEGS, A_SEGS = 17, 8
Z_ORDER = (7, 3, 5, 1, 6, 2, 4, 0)


def params(mib):
    return pltpu.CompilerParams(vmem_limit_bytes=mib * 1024 * 1024)


def dot(left, right):
    return jnp.dot(left, right, preferred_element_type=F32)


def dot_t(left, right):
    return lax.dot_general(left, right, (((1,), (1,)), ((), ())), preferred_element_type=F32)


def full(shape):
    return pl.BlockSpec(shape, lambda *_: (0,) * len(shape), pipeline_mode=pl.Buffered(1))


def edges_kernel(tissue, x0_ref, x1_ref, og0_ref, og1_ref, first_ref, last_ref):
    rows, hgt = x0_ref.shape[:2]
    for x_ref, og_ref, out, tile, at in (
        (x0_ref, og0_ref, first_ref, 0, 0),
        (x1_ref, og1_ref, last_ref, tissue.shape[1] - 1, EDGE - RIM),
    ):
        out[:, :hgt] = x_ref[...]
        for r in range(rows):
            seed = og_ref[r].astype(F32)[:, at : at + RIM] * tissue[r, tile].astype(F32)
            for pair in range(hgt // 2):
                both = jnp.concatenate([seed[2 * pair], seed[2 * pair + 1]], axis=0)
                out[r, hgt + pair] = both.astype(BF16)


def edges(tissue, x, og):
    rows, hgt, width, ch = x.shape
    part = (rows, hgt, EDGE, ch)
    out = (rows, hgt + hgt // 2, EDGE, ch)
    end = width // EDGE - 1

    def at(block):
        return pl.BlockSpec(part, lambda i, tissue: (0, 0, block, 0))

    return pl.pallas_call(
        edges_kernel,
        out_shape=[jax.ShapeDtypeStruct(out, BF16)] * 2,
        grid_spec=pltpu.PrefetchScalarGridSpec(
            num_scalar_prefetch=1,
            grid=(1,),
            in_specs=[at(0), at(end), at(0), at(end)],
            out_specs=[full(out)] * 2,
        ),
        compiler_params=params(60),
        name="edge_columns",
    )(tissue, x, x, og, og)


def hidden_one(part, wr, inner_ref):
    rows, hgt, cols, ch = part.shape
    flat = part.astype(F32).reshape(-1, ch).astype(BF16)
    pre = dot(flat, wr) * inner_ref[0:1] + inner_ref[1:2]
    return jnp.maximum(pre, 0.0).astype(BF16).astype(F32).reshape(rows, hgt, cols, -1)


def inside_kernel(x_ref, wr_ref, inner_ref, og_ref, wc_ref, we_ref, h1_ref, *kept):
    h1_ref[...] = hidden_one(x_ref[...], wr_ref[...], inner_ref).astype(BF16)
    for ref, out in zip((x_ref, og_ref, wr_ref, wc_ref, we_ref), kept):
        out[...] = ref[...]


def inside(x, wr, inner, og, wc, we):
    args = (x, wr, inner, og, wc, we)
    shapes = (x.shape[:3] + (wr.shape[1],),) + tuple(a.shape for a in (x, og, wr, wc, we))
    return pl.pallas_call(
        inside_kernel,
        out_shape=[jax.ShapeDtypeStruct(s, BF16) for s in shapes],
        grid=(1,),
        in_specs=[full(a.shape) for a in args],
        out_specs=[full(s) for s in shapes],
        compiler_params=params(12),
        cost_estimate=pl.CostEstimate(flops=300_000_000, bytes_accessed=9_000_000, transcendentals=0),
        name="forward_own_columns",
    )(*args)


def forward_kernel(
    ends, tissue, lo_ref, hi_ref, own_ref, inner_ref, outer_ref, x_ref, og_ref, wr_ref, wc_ref, we_ref,
    mz_ref, h2_ref, h1_ref, pad_ref, seed_ref,
    xs, hs, patches, ss,
):
    rows, hgt, width, ch = x_ref.shape
    inner_w = wr_ref.shape[1]
    wide = width + 2 * RIM
    per_row = hgt * wide
    hs[:, 0] = jnp.zeros((rows, width + 2 * EDGE, inner_w), F32)
    hs[:, hgt + 1] = jnp.zeros((rows, width + 2 * EDGE, inner_w), F32)
    hs[:, 1 : hgt + 1, EDGE : EDGE + width] = own_ref[...].astype(F32)
    for ref, at, keep in ((lo_ref, 0, ends[0]), (hi_ref, EDGE + width, ends[1])):
        part = ref[:, :hgt]
        xs[:, :, at : at + EDGE] = part.astype(F32)
        hs[:, 1 : hgt + 1, at : at + EDGE] = hidden_one(part, wr_ref[...], inner_ref) * keep.astype(F32)
    pad_ref[...] = hs[...].astype(BF16)
    first = EDGE - RIM - 1
    for k in range(9):
        dr, dc = divmod(k, 3)
        piece = hs[:, dr : dr + hgt, first + dc : first + dc + wide]
        piece = piece.reshape(-1, inner_w).astype(BF16)
        patches[:, k * inner_w : (k + 1) * inner_w] = piece
        if k == 4:
            h1_ref[...] = piece.reshape(rows, hgt * wide, inner_w)
    pre = dot(patches[...], wc_ref[...]) * inner_ref[2:3] + inner_ref[3:4]
    hid = jnp.maximum(pre, 0.0).astype(BF16)
    h2_ref[...] = hid.reshape(rows, hgt * wide, inner_w)
    xs[:, :, EDGE : EDGE + width] = x_ref[...].astype(F32)
    for r in range(rows):
        part = hid[r * per_row : (r + 1) * per_row]
        z = dot(part, we_ref[...]) * outer_ref[0:1] + outer_ref[1:2]
        z = z + xs[r, :, EDGE - RIM : EDGE - RIM + wide].reshape(per_row, ch)
        mz_ref[r] = jnp.where(z > 0, 1.0, 0.0).astype(BF16)
        for ref, at in ((lo_ref, 0), (hi_ref, RIM + width)):
            for pair in range(hgt // 2):
                both = ref[r, hgt + pair].astype(F32)
                ss[2 * pair, at : at + RIM] = both[:RIM]
                ss[2 * pair + 1, at : at + RIM] = both[RIM:]
        og = og_ref[r].astype(F32)
        for tile in range(width // TILE_W):
            cols = og[:, tile * TILE_W : (tile + 1) * TILE_W] * tissue[r, tile].astype(F32)
            ss[:, RIM + tile * TILE_W : RIM + (tile + 1) * TILE_W] = cols
        seed_ref[r] = ss[...].reshape(per_row, ch).astype(BF16)


def forward(ends, tissue, lo, hi, own, inner, outer, x, og, wr, wc, we):
    rows, hgt, width, ch = x.shape
    inner_w = wr.shape[1]
    wide = width + 2 * RIM
    pos = hgt * wide
    out_shapes = (
        (rows, pos, ch),
        (rows, pos, inner_w),
        (rows, pos, inner_w),
        (rows, hgt + 2, width + 2 * EDGE, inner_w),
        (rows, pos, ch),
    )
    blocks = (lo, hi, own, inner, outer, x, og, wr, wc, we)
    return pl.pallas_call(
        forward_kernel,
        out_shape=[jax.ShapeDtypeStruct(s, BF16) for s in out_shapes],
        grid_spec=pltpu.PrefetchScalarGridSpec(
            num_scalar_prefetch=2,
            grid=(1,),
            in_specs=[full(a.shape) for a in blocks],
            out_specs=[full(s) for s in out_shapes],
            scratch_shapes=[
                pltpu.VMEM((rows, hgt, width + 2 * EDGE, ch), F32),
                pltpu.VMEM((rows, hgt + 2, width + 2 * EDGE, inner_w), F32),
                pltpu.VMEM((rows * pos, 9 * inner_w), BF16),
                pltpu.VMEM((hgt, wide, ch), F32),
            ],
        ),
        compiler_params=params(20),
        cost_estimate=pl.CostEstimate(flops=2_000_000_000, bytes_accessed=12_000_000, transcendentals=0),
        name="forward_all_rows",
    )(ends, tissue, *blocks)


def chain_kernel(
    info, gy_ref, seed_ref, mz_ref, h2_ref, h1_ref, we_ref, wc_ref, wr_ref, inner_ref, outer_ref,
    gi_ref, g3_ref, g2_ref, g1_ref, *more,
):
    *wire_ref, wide_s, pad_s, flat_s = more
    inner_w = we_ref.shape[0]
    hgt, wide, ch = wide_s.shape
    pos = hgt * wide
    width = wide - 2 * RIM
    lead = 8

    def center(value):
        lanes = value.shape[1]
        wide_s[:, :, :lanes] = value.reshape(hgt, wide, lanes)
        return wide_s[:, RIM : RIM + width, :lanes].reshape(hgt * width, lanes).astype(BF16)

    cols = gy_ref.shape[0] // hgt
    at = (wide - cols) // 2
    flat_s[: hgt * cols] = gy_ref[...].astype(F32)
    wide_s[...] = jnp.zeros_like(wide_s)
    for h in range(hgt):
        wide_s[h, at : at + cols] = flat_s[h * cols : (h + 1) * cols]
    gy = jnp.where(info[1] == 1, seed_ref[0].astype(F32), wide_s[...].reshape(pos, ch))
    gz = gy * mz_ref[0].astype(F32)
    g3 = (gz * outer_ref[0:1]).astype(BF16)
    g3_ref[...] = center(g3.astype(F32))
    g2 = jnp.where(h2_ref[0].astype(F32) > 0, dot_t(g3, we_ref[...]) * inner_ref[2:3], 0.0)
    g2 = g2.astype(BF16).astype(F32)
    pad_s[...] = jnp.zeros_like(pad_s)
    pad_s[1 : hgt + 1, lead : lead + wide] = g2.reshape(hgt, wide, inner_w)
    g2_ref[...] = (
        pad_s[1 : hgt + 1, lead + RIM : lead + RIM + width].reshape(hgt * width, inner_w).astype(BF16)
    )
    back = jnp.zeros((pos, inner_w), F32)
    for k in range(9):
        dr, dc = divmod(k, 3)
        piece = pad_s[2 - dr : 2 - dr + hgt, lead + 1 - dc : lead + 1 - dc + wide]
        back = back + dot_t(piece.reshape(pos, inner_w).astype(BF16), wc_ref[k * inner_w : (k + 1) * inner_w])
    g1 = jnp.where(h1_ref[0].astype(F32) > 0, back * inner_ref[0:1], 0.0).astype(BF16)
    g1_ref[...] = center(g1.astype(F32))
    gi = gz + dot_t(g1, wr_ref[...])
    gi_ref[...] = center(gi)
    if wire_ref:
        cols = wire_ref[0].shape[0] // hgt
        at = (wide - cols) // 2
        for h in range(hgt):
            flat_s[h * cols : (h + 1) * cols] = wide_s[h, at : at + cols]
        wire_ref[0][...] = flat_s[: hgt * cols].astype(BF16)


def chain_step(info, gy, seed, mz, h2, h1, we, wc, wr, inner, outer, hgt, hand_on, sent):
    pos, ch = seed.shape[1:]
    inner_w = we.shape[0]
    wide = pos // hgt
    kept = hgt * (wide - 2 * RIM)

    def row(lanes):
        return pl.BlockSpec((1, pos, lanes), lambda i, info: (info[0], 0, 0))

    const = (we, wc, wr, inner, outer)
    out_shapes = [(kept, ch), (kept, ch), (kept, inner_w), (kept, inner_w)] + [(hgt * sent, ch)] * hand_on
    return pl.pallas_call(
        chain_kernel,
        out_shape=[jax.ShapeDtypeStruct(s, BF16) for s in out_shapes],
        grid_spec=pltpu.PrefetchScalarGridSpec(
            num_scalar_prefetch=1,
            grid=(1,),
            in_specs=[full(gy.shape), row(ch), row(ch), row(inner_w), row(inner_w)]
            + [full(c.shape) for c in const],
            out_specs=[full(s) for s in out_shapes],
            scratch_shapes=[
                pltpu.VMEM((hgt, wide, ch), F32),
                pltpu.VMEM((hgt + 2, wide + 16, inner_w), F32),
                pltpu.VMEM((pos, ch), F32),
            ],
        ),
        compiler_params=params(12),
        cost_estimate=pl.CostEstimate(flops=3_600_000_000, bytes_accessed=50_000_000, transcendentals=0),
        name="chain_row",
    )(info, gy, seed, mz, h2, h1, *const)


def picks(inner_w, z):
    row = jnp.arange(inner_w)
    each = row % 4
    own = jnp.asarray(Z_ORDER, row.dtype)[(row // 4) % Z] ^ z
    mid = (row // (4 * Z)) % 4
    core = row // (4 * Z * 4)
    whole = ((mid * Z + own) * CORES + core) * 4 + each
    part = (own * CORES + core) * 16 + mid * 4 + each
    return (jnp.stack([whole, part])[:, :, None] == row[None, None]).astype(BF16)


def turn_kernel(x_ref, pad_ref, h2_ref, pick_ref, xt_ref, pt_ref, ht_ref):
    rows, hgt, width, ch = x_ref.shape
    inner_w = h2_ref.shape[2]
    half = inner_w // CORES
    wide = width + 2 * RIM

    def turned(order, value, ref, at, stride):
        out = lax.dot_general(
            pick_ref[order], value, (((1,), (1,)), ((), ())), preferred_element_type=F32
        ).astype(BF16)
        for core in range(CORES):
            ref[core * stride + at : core * stride + at + half] = out[core * half : (core + 1) * half]

    flat = x_ref[...].astype(F32).reshape(-1, ch).astype(BF16)
    for part in range(ch // inner_w):
        turned(1, flat[:, part * inner_w : (part + 1) * inner_w], xt_ref, part * half, ch // CORES)
    padded = pad_ref[...].astype(F32)
    for k in range(9):
        dr, dc = divmod(k, 3)
        piece = padded[:, dr : dr + hgt, EDGE - 1 + dc : EDGE - 1 + dc + width]
        turned(0, piece.reshape(-1, inner_w).astype(BF16), pt_ref, k * half, 9 * half)
    h2 = h2_ref[...].astype(F32).reshape(rows * hgt, wide, inner_w)[:, RIM : RIM + width]
    turned(0, h2.reshape(-1, inner_w).astype(BF16), ht_ref, 0, half)


def turn(x, pad, h2, pick):
    rows, hgt, width, ch = x.shape
    inner_w = h2.shape[2]
    pos = rows * hgt * width
    args = (x, pad, h2, pick)
    shapes = ((ch, pos), (9 * inner_w, pos), (inner_w, pos))
    return pl.pallas_call(
        turn_kernel,
        out_shape=[jax.ShapeDtypeStruct(s, BF16) for s in shapes],
        grid=(1,),
        in_specs=[full(a.shape) for a in args],
        out_specs=[full(s) for s in shapes],
        compiler_params=params(20),
        cost_estimate=pl.CostEstimate(flops=2_000_000_000, bytes_accessed=8_000_000, transcendentals=0),
        name="turn_activations",
    )(*args)


def place(segment, target, x):
    as_int = lambda cond: jnp.where(cond, 1, 0)
    if segment < A_SEGS:
        side = as_int((x == 1) | (x == 2))
        keep = as_int(side == (1 if target in (1, 2) else 0))
        last = as_int(x // 2 == target // 2)
        return ((keep * 2 + last) * A_SEGS + segment) * 32
    keep = as_int(x // 2 == target // 2)
    same = as_int(x % 2 == target % 2)
    last = jnp.where(keep == 1, same, 1 - same)
    return ((keep * 2 + last) * (SEGS - A_SEGS) + segment - A_SEGS) * 32


def products(part, side, x, left, right, cols, out_ref, so_far):
    first_ref, pt_ref = left
    inner_w = pt_ref.shape[0] // 9
    half = inner_w // CORES
    first = first_ref.shape[0] // CORES
    ks = range(A_SEGS - 4) if part == 0 else range(A_SEGS - 4, 9)

    def put(target, segment, value):
        rows = pl.ds(pl.multiple_of(place(segment, target, x), 32), value.shape[0])
        if so_far is not None:
            value = value + so_far[rows].astype(F32)
        out_ref[rows] = value.astype(BF16)

    total = dot(first_ref[pl.ds(pl.multiple_of(side * first, first), first), cols], right[0])
    if part == 0:
        for target in range(X):
            put(target, 0, total[target * half : (target + 1) * half])
    else:
        for j in range(4):
            for target in range(X):
                put(target, 13 + j, total[target * 32 : target * 32 + 32, j * inner_w : (j + 1) * inner_w])
    at = pl.multiple_of(side * 9 * half + ks[0] * half, half)
    total = dot(pt_ref[pl.ds(at, len(ks) * half), cols], right[1])
    for n, k in enumerate(ks):
        for target in range(X):
            put(target, 4 + k, total[n * half + target * 32 : n * half + target * 32 + 32])


def weights_kernel(parts, rows, by_row, added, info, *refs):
    count = len(parts)
    lefts, refs = refs[: 2 * count], refs[2 * count :]
    so_far, refs = (refs[: 2 * count], refs[2 * count :]) if added else ((None,) * (2 * count), refs)
    kinds = 2 if count == 1 else 3
    slots = []
    for _ in range(kinds):
        slots.append(refs[: len(by_row)])
        refs = refs[len(by_row) :]
    outs, stores, sems = refs[: 2 * count], refs[2 * count : 2 * count + kinds], refs[-1]
    core, x, section = info[0], info[1], info[2]

    def copy(kind, n, slot):
        return pltpu.make_async_copy(slots[kind][by_row.index(slot)], stores[kind].at[n], sems.at[kind, n])

    for s, used in enumerate(slots_of(rows)):
        @pl.when(section == s)
        def _():
            for kind in range(kinds):
                for n, slot in enumerate(used):
                    copy(kind, n, slot).start()

    held = []
    for kind in range(kinds):
        for n in range(len(rows)):
            copy(kind, n, by_row[0]).wait()
        kept, lanes = stores[kind].shape[1:]
        held.append(stores[kind][...].reshape(len(rows) * kept, lanes))
    cols = slice(rows[0] * kept, (rows[-1] + 1) * kept)
    for i, part in enumerate(parts):
        right = (held[0], held[1]) if count == 1 or part == 0 else (held[2], held[1])
        for n, side in enumerate((core, 1 - core)):
            products(part, side, x, lefts[2 * i : 2 * i + 2], right, cols, outs[2 * i + n], so_far[2 * i + n])


def slots_of(rows):
    return [[LAG * (SECTIONS - 1 - s) + r for r in rows] for s in range(SECTIONS)]


def weight_grads(info, parts, rows, lefts, saved, so_far, name):
    by_row = sorted({slot for used in slots_of(rows) for slot in used})
    kept = saved[0][0].shape[0]
    inner_w = lefts[1].shape[0] // 9
    sizes = [(A_SEGS if part == 0 else SEGS - A_SEGS) * X * 32 for part in parts]
    out_shapes = [(size, inner_w) for size in sizes for _ in range(2)]
    blocks = tuple(lefts) + tuple(so_far)
    return pl.pallas_call(
        functools.partial(weights_kernel, parts, rows, by_row, len(so_far) > 0),
        out_shape=[jax.ShapeDtypeStruct(s, BF16) for s in out_shapes],
        grid_spec=pltpu.PrefetchScalarGridSpec(
            num_scalar_prefetch=1,
            grid=(1,),
            in_specs=[full(a.shape) for a in blocks]
            + [pl.BlockSpec(memory_space=pl.ANY)] * (len(by_row) * len(saved)),
            out_specs=[full(s) for s in out_shapes],
            scratch_shapes=[pltpu.VMEM((len(rows), kept, kind[0].shape[1]), BF16) for kind in saved]
            + [pltpu.SemaphoreType.DMA((len(saved), len(rows)))],
        ),
        compiler_params=params(20),
        cost_estimate=pl.CostEstimate(
            flops=300_000_000 * len(rows), bytes_accessed=2_000_000 * len(rows), transcendentals=0
        ),
        name=name,
    )(info, *blocks, *[kind[slot] for kind in saved for slot in by_row])


def collect_kernel(slots, info, *refs):
    out_ref, sems = refs[slots], refs[slots + 1]
    rows = range(out_ref.shape[0])

    def copy(n, slot):
        return pltpu.make_async_copy(refs[slot], out_ref.at[n], sems.at[n])

    for s, used in enumerate(slots_of(rows)):
        @pl.when(info[2] == s)
        def _():
            for n, slot in enumerate(used):
                copy(n, slot).start()

    for n in rows:
        copy(n, n).wait()


def collect(info, gi, rows):
    return pl.pallas_call(
        functools.partial(collect_kernel, len(gi)),
        out_shape=jax.ShapeDtypeStruct((rows,) + gi[0].shape, BF16),
        grid_spec=pltpu.PrefetchScalarGridSpec(
            num_scalar_prefetch=1,
            grid=(1,),
            in_specs=[pl.BlockSpec(memory_space=pl.ANY)] * len(gi),
            out_specs=pl.BlockSpec(memory_space=pl.ANY),
            scratch_shapes=[pltpu.SemaphoreType.DMA((rows,))],
        ),
        compiler_params=params(4),
        cost_estimate=pl.CostEstimate(flops=0, bytes_accessed=2_000_000, transcendentals=0),
        name="collect_grad_inputs",
    )(info, *gi)


def tile_pairs(partner):
    pairs = []
    for x in range(X):
        for z in range(Z):
            for c in range(CORES):
                px, pz, pc = partner(x, z, c)
                pairs.append(((x * Z + z) * CORES + c, (px * Z + pz) * CORES + pc))
    return pairs


def swap(value, partner):
    return lax.ppermute(value.astype(BF16), "tile", tile_pairs(partner))


def scatter_sum(keep_a, send_a, keep_b, send_b):
    lanes = keep_a.shape[-1]
    other_core = lambda x, z, c: (x, z, 1 - c)
    inner_pair = lambda x, z, c: (x ^ 1, z, c)
    outer_pair = lambda x, z, c: (3 - x, z, c)

    def along_x(keep, send, pairs):
        got = swap(send, other_core)
        own = lambda first, last: keep[first:last].astype(F32) + got[first:last].astype(F32)
        size = keep.shape[0]
        half, quart = size // 2, size // 4
        got_1 = swap(own(0, half), pairs[0])
        got_2 = swap(own(half, half + quart) + got_1[:quart].astype(F32), pairs[1])
        return own(half + quart, size) + got_1[quart:].astype(F32) + got_2.astype(F32)

    part_a = along_x(keep_a, send_a, (inner_pair, outer_pair))
    part_b = along_x(keep_b, send_b, (outer_pair, inner_pair))
    total = jnp.concatenate([part_a, part_b], axis=0).reshape(SEGS, Z * 4, lanes)
    count = Z * 4 // 2
    got = swap(total[:, :count], lambda x, z, c: (x, z ^ 1, c))
    total = total[:, count:] + got.astype(F32)
    shares = [
        swap(total[:, 4 * i : 4 * i + 4], lambda x, z, c, b=Z_ORDER[Z // 2 + i]: (x, z ^ b, c))
        for i in range(Z // 2 - 1)
    ]
    return finish(total[:, count - 4 :], shares)


def finish_kernel(own_ref, *refs):
    reduce_ref, conv_ref, expand_ref = refs[-3:]
    total = own_ref[...]
    for ref in refs[:-3]:
        total = total + ref[...].astype(F32)
    lanes = total.shape[2]
    for q in range(4):
        reduce_ref[4 * q : 4 * q + 4] = total[q]
        expand_ref[:, q * lanes : (q + 1) * lanes] = total[13 + q]
    conv_ref[...] = total[4:13]


def finish(own, shares):
    lanes = own.shape[2]
    shapes = ((16, lanes), (9, 4, lanes), (4, 4 * lanes))
    args = (own, *shares)
    g_reduce, g_conv, g_expand = pl.pallas_call(
        finish_kernel,
        out_shape=[jax.ShapeDtypeStruct(s, F32) for s in shapes],
        grid=(1,),
        in_specs=[full(a.shape) for a in args],
        out_specs=[full(s) for s in shapes],
        compiler_params=params(4),
        name="finish_gradients",
    )(*args)
    return g_reduce, g_conv.reshape(3, 3, 4, lanes), g_expand


def neighbours(first, last, tiles):
    pairs = [(i, i + 1) for i in range(tiles - 1)]
    low = lax.ppermute(last, "tile", pairs)
    high = lax.ppermute(first, "tile", [(b, a) for a, b in pairs])
    return low, high


def per_device(block_inputs, out_grad, tissue, w_reduce, w_conv, w_expand, inner_affine, outer_affine):
    section = lax.axis_index("section")
    sections = lax.axis_size("section")
    tile = lax.axis_index("tile")
    tiles = lax.axis_size("tile")
    x = block_inputs[0]
    rows, hgt, width, ch = x.shape
    wr, we = w_reduce[0], w_expand[0]
    inner_w = wr.shape[1]
    wc = w_conv[0].reshape(9 * inner_w, inner_w)
    inner, outer = inner_affine[0], outer_affine[0]

    lo, hi = neighbours(*edges(tissue, x, out_grad), tiles)
    own, *at_hand = inside(x, wr, inner, out_grad, wc, we)

    ends = jnp.stack([tile > 0, tile < tiles - 1]).astype(jnp.int32)
    mz, h2, h1, pad, seed = forward(
        ends, tissue, lo, hi, own, inner, outer, *at_hand
    )
    z_now = (tile // CORES) % Z
    xt, pt, ht = turn(x, pad, h2, picks(inner_w, z_now))

    back_one = [(i, i - 1) for i in range(1, sections)]
    slots = rows + LAG * (sections - 1)
    arriving = [jnp.zeros((hgt * (width + 2), ch), BF16)] * LAG
    per_slot = []
    for slot in range(slots):
        micro = slot - LAG * (sections - 1 - section)
        info = jnp.stack(
            [jnp.clip(micro, 0, rows - 1), (section == sections - 1).astype(micro.dtype)]
        ).astype(jnp.int32)
        hand_on = slot + LAG < slots
        senders = [s for s in range(1, sections) if 0 <= slot - LAG * (sections - 1 - s) < rows]
        sent = width + 2 * max(senders, default=1)
        *saved, last = chain_step(
            info, arriving[slot], seed, mz, h2, h1, at_hand[4], at_hand[3], at_hand[2], inner, outer, hgt, hand_on, sent
        )
        if hand_on:
            arriving.append(lax.ppermute(last, "section", back_one))
        else:
            saved.append(last)
        per_slot.append(saved)
    gi, g3, g2, g1 = zip(*per_slot)
    info = jnp.stack([tile % CORES, tile // (CORES * Z), section]).astype(jnp.int32)
    early, late = range(rows - 1), range(rows - 1, rows)
    so_far = weight_grads(info, (0, 1), early, (xt, pt, ht, pt), (g1, g2, g3), (), "weight_gradients_early")
    sums_a = weight_grads(info, (0,), late, (xt, pt), (g1, g2), so_far[:2], "weight_gradients_a")
    sums_b = weight_grads(info, (1,), late, (ht, pt), (g3, g2), so_far[2:], "weight_gradients_b")
    g_reduce, g_conv, g_expand = scatter_sum(*sums_a, *sums_b)
    grad_inputs = collect(info, gi, rows)
    grad_inputs = grad_inputs.reshape(rows, hgt, width, ch)
    return grad_inputs[None], g_reduce[None], g_conv[None], g_expand[None]


def solution(mesh):
    in_specs = (
        P("section", None, None, "tile", None),
        P(None, None, "tile", None),
        P(None, "tile"),
        P("section", None, None),
        P("section", None, None, None, None),
        P("section", None, None),
        P("section", None, None),
        P("section", None, None),
    )
    out_specs = (
        P("section", None, None, "tile", None),
        P("section", "tile", None),
        P("section", None, None, "tile", None),
        P("section", "tile", None),
    )
    return jax.shard_map(
        per_device, mesh=mesh, in_specs=in_specs, out_specs=out_specs, check_vma=False
    )
```

```python
import functools

import jax
import jax.numpy as jnp
from jax import lax
from jax.experimental import pallas as pl
from jax.experimental.pallas import tpu as pltpu
from jax.sharding import PartitionSpec as P

TILE_W = 8
SECTIONS = 4
X, Z, CORES = 4, 8, 2
EDGE = 8
RIM = 4
BF16, F32 = jnp.bfloat16, jnp.float32
LAG = 2
SEGS, A_SEGS = 17, 8
Z_ORDER = (5, 3, 7, 1, 4, 2, 6, 0)


def params(mib):
    return pltpu.CompilerParams(vmem_limit_bytes=mib * 1024 * 1024)


def dot(left, right):
    return jnp.dot(left, right, preferred_element_type=F32)


def dot_t(left, right):
    return lax.dot_general(left, right, (((1,), (1,)), ((), ())), preferred_element_type=F32)


def full(shape):
    return pl.BlockSpec(shape, lambda *_: (0,) * len(shape), pipeline_mode=pl.Buffered(1))


def edges_kernel(tissue, x0_ref, x1_ref, og0_ref, og1_ref, first_ref, last_ref):
    rows, hgt = x0_ref.shape[:2]
    for x_ref, og_ref, out, tile, at in (
        (x0_ref, og0_ref, first_ref, 0, 0),
        (x1_ref, og1_ref, last_ref, tissue.shape[1] - 1, EDGE - RIM),
    ):
        out[:, :hgt] = x_ref[...]
        for r in range(rows):
            seed = og_ref[r].astype(F32)[:, at : at + RIM] * tissue[r, tile].astype(F32)
            for pair in range(hgt // 2):
                both = jnp.concatenate([seed[2 * pair], seed[2 * pair + 1]], axis=0)
                out[r, hgt + pair] = both.astype(BF16)


def edges(tissue, x, og):
    rows, hgt, width, ch = x.shape
    part = (rows, hgt, EDGE, ch)
    out = (rows, hgt + hgt // 2, EDGE, ch)
    end = width // EDGE - 1

    def at(block):
        return pl.BlockSpec(part, lambda i, tissue: (0, 0, block, 0))

    return pl.pallas_call(
        edges_kernel,
        out_shape=[jax.ShapeDtypeStruct(out, BF16)] * 2,
        grid_spec=pltpu.PrefetchScalarGridSpec(
            num_scalar_prefetch=1,
            grid=(1,),
            in_specs=[at(0), at(end), at(0), at(end)],
            out_specs=[full(out)] * 2,
        ),
        compiler_params=params(60),
        name="edge_columns",
    )(tissue, x, x, og, og)


def hidden_one(part, wr, inner_ref):
    rows, hgt, cols, ch = part.shape
    flat = part.astype(F32).reshape(-1, ch).astype(BF16)
    pre = dot(flat, wr) * inner_ref[0:1] + inner_ref[1:2]
    return jnp.maximum(pre, 0.0).astype(BF16).astype(F32).reshape(rows, hgt, cols, -1)


def inside_kernel(x_ref, wr_ref, inner_ref, og_ref, wc_ref, we_ref, h1_ref, *kept):
    h1_ref[...] = hidden_one(x_ref[...], wr_ref[...], inner_ref).astype(BF16)
    for ref, out in zip((x_ref, og_ref, wr_ref, wc_ref, we_ref), kept):
        out[...] = ref[...]


def inside(x, wr, inner, og, wc, we):
    args = (x, wr, inner, og, wc, we)
    shapes = (x.shape[:3] + (wr.shape[1],),) + tuple(a.shape for a in (x, og, wr, wc, we))
    return pl.pallas_call(
        inside_kernel,
        out_shape=[jax.ShapeDtypeStruct(s, BF16) for s in shapes],
        grid=(1,),
        in_specs=[full(a.shape) for a in args],
        out_specs=[full(s) for s in shapes],
        compiler_params=params(12),
        cost_estimate=pl.CostEstimate(flops=300_000_000, bytes_accessed=9_000_000, transcendentals=0),
        name="forward_own_columns",
    )(*args)


def forward_kernel(
    some, held, ends, tissue, lo_ref, hi_ref, own_ref, inner_ref, outer_ref, x_ref, og_ref, wr_ref, wc_ref, we_ref, *refs,
):
    before, refs = refs[:held], refs[held:]
    mz_ref, h2_ref, h1_ref, pad_ref, seed_ref, xs, hs, patches, ss = refs
    hgt, width, ch = x_ref.shape[1:]
    inner_w = wr_ref.shape[1]
    wide = width + 2 * RIM
    per_row = hgt * wide
    count, start = len(some), some[0]
    these = slice(start, start + count)
    for ref, out in zip(before, (mz_ref, h2_ref, h1_ref, pad_ref, seed_ref)):
        out[:start] = ref[...]
    into = pl.ds(start if held else 0, count)
    hs[:, 0] = jnp.zeros((count, width + 2 * EDGE, inner_w), F32)
    hs[:, hgt + 1] = jnp.zeros((count, width + 2 * EDGE, inner_w), F32)
    hs[:, 1 : hgt + 1, EDGE : EDGE + width] = own_ref[these].astype(F32)
    xs[:, :, EDGE : EDGE + width] = x_ref[these].astype(F32)
    for ref, at, keep in ((lo_ref, 0, ends[0]), (hi_ref, EDGE + width, ends[1])):
        part = ref[these, :hgt]
        xs[:, :, at : at + EDGE] = part.astype(F32)
        hs[:, 1 : hgt + 1, at : at + EDGE] = hidden_one(part, wr_ref[...], inner_ref) * keep.astype(F32)
    pad_ref[into] = hs[...].astype(BF16)
    first = EDGE - RIM - 1
    for k in range(9):
        dr, dc = divmod(k, 3)
        piece = hs[:, dr : dr + hgt, first + dc : first + dc + wide]
        piece = piece.reshape(-1, inner_w).astype(BF16)
        patches[:, k * inner_w : (k + 1) * inner_w] = piece
        if k == 4:
            h1_ref[into] = piece.reshape(count, per_row, inner_w)
    pre = dot(patches[...], wc_ref[...]) * inner_ref[2:3] + inner_ref[3:4]
    hid = jnp.maximum(pre, 0.0).astype(BF16)
    h2_ref[into] = hid.reshape(count, per_row, inner_w)
    for n, r in enumerate(some):
        out = r if held else n
        part = hid[n * per_row : (n + 1) * per_row]
        z = dot(part, we_ref[...]) * outer_ref[0:1] + outer_ref[1:2]
        z = z + xs[n, :, EDGE - RIM : EDGE - RIM + wide].reshape(per_row, ch)
        mz_ref[out] = jnp.where(z > 0, 1.0, 0.0).astype(BF16)
        for ref, at in ((lo_ref, 0), (hi_ref, RIM + width)):
            for pair in range(hgt // 2):
                both = ref[r, hgt + pair].astype(F32)
                ss[2 * pair, at : at + RIM] = both[:RIM]
                ss[2 * pair + 1, at : at + RIM] = both[RIM:]
        og = og_ref[r].astype(F32)
        for tile in range(width // TILE_W):
            cols = og[:, tile * TILE_W : (tile + 1) * TILE_W] * tissue[r, tile].astype(F32)
            ss[:, RIM + tile * TILE_W : RIM + (tile + 1) * TILE_W] = cols
        seed_ref[out] = ss[...].reshape(per_row, ch).astype(BF16)


def forward(some, before, ends, tissue, lo, hi, own, inner, outer, x, og, wr, wc, we):
    rows, hgt, width, ch = x.shape
    inner_w = wr.shape[1]
    wide = width + 2 * RIM
    pos = hgt * wide
    count = len(some)
    out_rows = rows if before else count
    out_shapes = (
        (out_rows, pos, ch),
        (out_rows, pos, inner_w),
        (out_rows, pos, inner_w),
        (out_rows, hgt + 2, width + 2 * EDGE, inner_w),
        (out_rows, pos, ch),
    )
    blocks = (lo, hi, own, inner, outer, x, og, wr, wc, we, *before)
    return pl.pallas_call(
        functools.partial(forward_kernel, some, len(before)),
        out_shape=[jax.ShapeDtypeStruct(s, BF16) for s in out_shapes],
        grid_spec=pltpu.PrefetchScalarGridSpec(
            num_scalar_prefetch=2,
            grid=(1,),
            in_specs=[full(a.shape) for a in blocks],
            out_specs=[full(s) for s in out_shapes],
            scratch_shapes=[
                pltpu.VMEM((count, hgt, width + 2 * EDGE, ch), F32),
                pltpu.VMEM((count, hgt + 2, width + 2 * EDGE, inner_w), F32),
                pltpu.VMEM((count * pos, 9 * inner_w), BF16),
                pltpu.VMEM((hgt, wide, ch), F32),
            ],
        ),
        compiler_params=params(20),
        cost_estimate=pl.CostEstimate(
            flops=600_000_000 * count, bytes_accessed=4_000_000 * count, transcendentals=0
        ),
        name="forward_rows",
    )(ends, tissue, *blocks)


def chain_kernel(
    info, gy_ref, seed_ref, mz_ref, h2_ref, h1_ref, we_ref, wc_ref, wr_ref, inner_ref, outer_ref,
    gi_ref, g3_ref, g2_ref, g1_ref, *more,
):
    *wire_ref, wide_s, pad_s, flat_s = more
    inner_w = we_ref.shape[0]
    hgt, wide, ch = wide_s.shape
    pos = hgt * wide
    width = wide - 2 * RIM
    lead = 8

    def center(value):
        lanes = value.shape[1]
        wide_s[:, :, :lanes] = value.reshape(hgt, wide, lanes)
        return wide_s[:, RIM : RIM + width, :lanes].reshape(hgt * width, lanes).astype(BF16)

    cols = gy_ref.shape[0] // hgt
    at = (wide - cols) // 2
    flat_s[: hgt * cols] = gy_ref[...].astype(F32)
    wide_s[...] = jnp.zeros_like(wide_s)
    for h in range(hgt):
        wide_s[h, at : at + cols] = flat_s[h * cols : (h + 1) * cols]
    gy = jnp.where(info[1] == 1, seed_ref[0].astype(F32), wide_s[...].reshape(pos, ch))
    gz = gy * mz_ref[0].astype(F32)
    g3 = (gz * outer_ref[0:1]).astype(BF16)
    g3_ref[...] = center(g3.astype(F32))
    g2 = jnp.where(h2_ref[0].astype(F32) > 0, dot_t(g3, we_ref[...]) * inner_ref[2:3], 0.0)
    g2 = g2.astype(BF16).astype(F32)
    pad_s[...] = jnp.zeros_like(pad_s)
    pad_s[1 : hgt + 1, lead : lead + wide] = g2.reshape(hgt, wide, inner_w)
    g2_ref[...] = (
        pad_s[1 : hgt + 1, lead + RIM : lead + RIM + width].reshape(hgt * width, inner_w).astype(BF16)
    )
    back = jnp.zeros((pos, inner_w), F32)
    for k in range(9):
        dr, dc = divmod(k, 3)
        piece = pad_s[2 - dr : 2 - dr + hgt, lead + 1 - dc : lead + 1 - dc + wide]
        back = back + dot_t(piece.reshape(pos, inner_w).astype(BF16), wc_ref[k * inner_w : (k + 1) * inner_w])
    g1 = jnp.where(h1_ref[0].astype(F32) > 0, back * inner_ref[0:1], 0.0).astype(BF16)
    g1_ref[...] = center(g1.astype(F32))
    gi = gz + dot_t(g1, wr_ref[...])
    gi_ref[...] = center(gi)
    if wire_ref:
        cols = wire_ref[0].shape[0] // hgt
        at = (wide - cols) // 2
        for h in range(hgt):
            flat_s[h * cols : (h + 1) * cols] = wide_s[h, at : at + cols]
        wire_ref[0][...] = flat_s[: hgt * cols].astype(BF16)


def chain_step(info, gy, seed, mz, h2, h1, we, wc, wr, inner, outer, hgt, hand_on, sent):
    pos, ch = seed.shape[1:]
    inner_w = we.shape[0]
    wide = pos // hgt
    kept = hgt * (wide - 2 * RIM)

    def row(lanes):
        return pl.BlockSpec((1, pos, lanes), lambda i, info: (info[0], 0, 0))

    const = (we, wc, wr, inner, outer)
    out_shapes = [(kept, ch), (kept, ch), (kept, inner_w), (kept, inner_w)] + [(hgt * sent, ch)] * hand_on
    return pl.pallas_call(
        chain_kernel,
        out_shape=[jax.ShapeDtypeStruct(s, BF16) for s in out_shapes],
        grid_spec=pltpu.PrefetchScalarGridSpec(
            num_scalar_prefetch=1,
            grid=(1,),
            in_specs=[full(gy.shape), row(ch), row(ch), row(inner_w), row(inner_w)]
            + [full(c.shape) for c in const],
            out_specs=[full(s) for s in out_shapes],
            scratch_shapes=[
                pltpu.VMEM((hgt, wide, ch), F32),
                pltpu.VMEM((hgt + 2, wide + 16, inner_w), F32),
                pltpu.VMEM((pos, ch), F32),
            ],
        ),
        compiler_params=params(12),
        cost_estimate=pl.CostEstimate(flops=3_600_000_000, bytes_accessed=50_000_000, transcendentals=0),
        name="chain_row",
    )(info, gy, seed, mz, h2, h1, *const)


def picks(inner_w, z):
    row = jnp.arange(inner_w)
    each = row % 4
    own = jnp.asarray(Z_ORDER, row.dtype)[(row // 4) % Z] ^ z
    mid = (row // (4 * Z)) % 4
    core = row // (4 * Z * 4)
    whole = ((mid * Z + own) * CORES + core) * 4 + each
    part = (own * CORES + core) * 16 + mid * 4 + each
    return (jnp.stack([whole, part])[:, :, None] == row[None, None]).astype(BF16)


def turn_kernel(x_ref, pad_ref, h2_ref, pick_ref, xt_ref, pt_ref, ht_ref):
    rows, hgt, width, ch = x_ref.shape
    inner_w = h2_ref.shape[2]
    half = inner_w // CORES
    wide = width + 2 * RIM

    def turned(order, value, ref, at, stride):
        out = lax.dot_general(
            pick_ref[order], value, (((1,), (1,)), ((), ())), preferred_element_type=F32
        ).astype(BF16)
        for core in range(CORES):
            ref[core * stride + at : core * stride + at + half] = out[core * half : (core + 1) * half]

    flat = x_ref[...].astype(F32).reshape(-1, ch).astype(BF16)
    for part in range(ch // inner_w):
        turned(1, flat[:, part * inner_w : (part + 1) * inner_w], xt_ref, part * half, ch // CORES)
    padded = pad_ref[...].astype(F32)
    for k in range(9):
        dr, dc = divmod(k, 3)
        piece = padded[:, dr : dr + hgt, EDGE - 1 + dc : EDGE - 1 + dc + width]
        turned(0, piece.reshape(-1, inner_w).astype(BF16), pt_ref, k * half, 9 * half)
    h2 = h2_ref[...].astype(F32).reshape(rows * hgt, wide, inner_w)[:, RIM : RIM + width]
    turned(0, h2.reshape(-1, inner_w).astype(BF16), ht_ref, 0, half)


def turn(x, pad, h2, pick):
    rows, hgt, width, ch = x.shape
    inner_w = h2.shape[2]
    pos = rows * hgt * width
    args = (x, pad, h2, pick)
    shapes = ((ch, pos), (9 * inner_w, pos), (inner_w, pos))
    return pl.pallas_call(
        turn_kernel,
        out_shape=[jax.ShapeDtypeStruct(s, BF16) for s in shapes],
        grid=(1,),
        in_specs=[full(a.shape) for a in args],
        out_specs=[full(s) for s in shapes],
        compiler_params=params(20),
        cost_estimate=pl.CostEstimate(flops=2_000_000_000, bytes_accessed=8_000_000, transcendentals=0),
        name="turn_activations",
    )(*args)


def place(segment, target, x):
    as_int = lambda cond: jnp.where(cond, 1, 0)
    if segment < A_SEGS:
        side = as_int((x == 1) | (x == 2))
        keep = as_int(side == (1 if target in (1, 2) else 0))
        last = as_int(x // 2 == target // 2)
        return ((keep * 2 + last) * A_SEGS + segment) * 32
    keep = as_int(x // 2 == target // 2)
    same = as_int(x % 2 == target % 2)
    last = jnp.where(keep == 1, same, 1 - same)
    return ((keep * 2 + last) * (SEGS - A_SEGS) + segment - A_SEGS) * 32


def products(part, side, x, left, right, cols, out_ref, so_far):
    first_ref, pt_ref = left
    inner_w = pt_ref.shape[0] // 9
    half = inner_w // CORES
    first = first_ref.shape[0] // CORES
    ks = range(A_SEGS - 4) if part == 0 else range(A_SEGS - 4, 9)

    def put(target, segment, value):
        rows = pl.ds(pl.multiple_of(place(segment, target, x), 32), value.shape[0])
        if so_far is not None:
            value = value + so_far[rows].astype(F32)
        out_ref[rows] = value.astype(BF16)

    total = dot(first_ref[pl.ds(pl.multiple_of(side * first, first), first), cols], right[0])
    if part == 0:
        for target in range(X):
            put(target, 0, total[target * half : (target + 1) * half])
    else:
        for j in range(4):
            for target in range(X):
                put(target, 13 + j, total[target * 32 : target * 32 + 32, j * inner_w : (j + 1) * inner_w])
    at = pl.multiple_of(side * 9 * half + ks[0] * half, half)
    total = dot(pt_ref[pl.ds(at, len(ks) * half), cols], right[1])
    for n, k in enumerate(ks):
        for target in range(X):
            put(target, 4 + k, total[n * half + target * 32 : n * half + target * 32 + 32])


def weights_kernel(parts, rows, by_row, added, info, *refs):
    count = len(parts)
    lefts, refs = refs[: 2 * count], refs[2 * count :]
    so_far, refs = (refs[: 2 * count], refs[2 * count :]) if added else ((None,) * (2 * count), refs)
    kinds = 2 if count == 1 else 3
    slots = []
    for _ in range(kinds):
        slots.append(refs[: len(by_row)])
        refs = refs[len(by_row) :]
    outs, stores, sems = refs[: 2 * count], refs[2 * count : 2 * count + kinds], refs[-1]
    core, x, section = info[0], info[1], info[2]

    def copy(kind, n, slot):
        return pltpu.make_async_copy(slots[kind][by_row.index(slot)], stores[kind].at[n], sems.at[kind, n])

    for s, used in enumerate(slots_of(rows)):
        @pl.when(section == s)
        def _():
            for kind in range(kinds):
                for n, slot in enumerate(used):
                    copy(kind, n, slot).start()

    held = []
    for kind in range(kinds):
        for n in range(len(rows)):
            copy(kind, n, by_row[0]).wait()
        kept, lanes = stores[kind].shape[1:]
        held.append(stores[kind][...].reshape(len(rows) * kept, lanes))
    cols = slice(rows[0] * kept, (rows[-1] + 1) * kept)
    for i, part in enumerate(parts):
        right = (held[0], held[1]) if count == 1 or part == 0 else (held[2], held[1])
        for n, side in enumerate((core, 1 - core)):
            products(part, side, x, lefts[2 * i : 2 * i + 2], right, cols, outs[2 * i + n], so_far[2 * i + n])


def slots_of(rows):
    return [[LAG * (SECTIONS - 1 - s) + r for r in rows] for s in range(SECTIONS)]


def weight_grads(info, parts, rows, lefts, saved, so_far, name):
    by_row = sorted({slot for used in slots_of(rows) for slot in used})
    kept = saved[0][0].shape[0]
    inner_w = lefts[1].shape[0] // 9
    sizes = [(A_SEGS if part == 0 else SEGS - A_SEGS) * X * 32 for part in parts]
    out_shapes = [(size, inner_w) for size in sizes for _ in range(2)]
    blocks = tuple(lefts) + tuple(so_far)
    return pl.pallas_call(
        functools.partial(weights_kernel, parts, rows, by_row, len(so_far) > 0),
        out_shape=[jax.ShapeDtypeStruct(s, BF16) for s in out_shapes],
        grid_spec=pltpu.PrefetchScalarGridSpec(
            num_scalar_prefetch=1,
            grid=(1,),
            in_specs=[full(a.shape) for a in blocks]
            + [pl.BlockSpec(memory_space=pl.ANY)] * (len(by_row) * len(saved)),
            out_specs=[full(s) for s in out_shapes],
            scratch_shapes=[pltpu.VMEM((len(rows), kept, kind[0].shape[1]), BF16) for kind in saved]
            + [pltpu.SemaphoreType.DMA((len(saved), len(rows)))],
        ),
        compiler_params=params(20),
        cost_estimate=pl.CostEstimate(
            flops=300_000_000 * len(rows), bytes_accessed=2_000_000 * len(rows), transcendentals=0
        ),
        name=name,
    )(info, *blocks, *[kind[slot] for kind in saved for slot in by_row])


def collect_kernel(slots, info, *refs):
    out_ref, sems = refs[slots], refs[slots + 1]
    rows = range(out_ref.shape[0])

    def copy(n, slot):
        return pltpu.make_async_copy(refs[slot], out_ref.at[n], sems.at[n])

    for s, used in enumerate(slots_of(rows)):
        @pl.when(info[2] == s)
        def _():
            for n, slot in enumerate(used):
                copy(n, slot).start()

    for n in rows:
        copy(n, n).wait()


def collect(info, gi, rows):
    return pl.pallas_call(
        functools.partial(collect_kernel, len(gi)),
        out_shape=jax.ShapeDtypeStruct((rows,) + gi[0].shape, BF16),
        grid_spec=pltpu.PrefetchScalarGridSpec(
            num_scalar_prefetch=1,
            grid=(1,),
            in_specs=[pl.BlockSpec(memory_space=pl.ANY)] * len(gi),
            out_specs=pl.BlockSpec(memory_space=pl.ANY),
            scratch_shapes=[pltpu.SemaphoreType.DMA((rows,))],
        ),
        compiler_params=params(4),
        cost_estimate=pl.CostEstimate(flops=0, bytes_accessed=2_000_000, transcendentals=0),
        name="collect_grad_inputs",
    )(info, *gi)


def tile_pairs(partner):
    pairs = []
    for x in range(X):
        for z in range(Z):
            for c in range(CORES):
                px, pz, pc = partner(x, z, c)
                pairs.append(((x * Z + z) * CORES + c, (px * Z + pz) * CORES + pc))
    return pairs


def swap(value, partner):
    return lax.ppermute(value.astype(BF16), "tile", tile_pairs(partner))


def scatter_sum(keep_a, send_a, keep_b, send_b):
    lanes = keep_a.shape[-1]
    other_core = lambda x, z, c: (x, z, 1 - c)
    inner_pair = lambda x, z, c: (x ^ 1, z, c)
    outer_pair = lambda x, z, c: (3 - x, z, c)

    def along_x(keep, send, pairs):
        got = swap(send, other_core)
        own = lambda first, last: keep[first:last].astype(F32) + got[first:last].astype(F32)
        size = keep.shape[0]
        half, quart = size // 2, size // 4
        got_1 = swap(own(0, half), pairs[0])
        got_2 = swap(own(half, half + quart) + got_1[:quart].astype(F32), pairs[1])
        return own(half + quart, size) + got_1[quart:].astype(F32) + got_2.astype(F32)

    part_a = along_x(keep_a, send_a, (inner_pair, outer_pair))
    part_b = along_x(keep_b, send_b, (outer_pair, inner_pair))
    total = jnp.concatenate([part_a, part_b], axis=0).reshape(SEGS, Z * 4, lanes)
    for bits in (1, 2):
        count = total.shape[1] // 2
        got = swap(total[:, :count], lambda x, z, c, b=bits: (x, z ^ b, c))
        total = total[:, count:] + got.astype(F32)
    return finish(total[:, 4:], [swap(total[:, :4], lambda x, z, c: (x, z ^ 6, c))])


def finish_kernel(own_ref, *refs):
    reduce_ref, conv_ref, expand_ref = refs[-3:]
    total = own_ref[...]
    for ref in refs[:-3]:
        total = total + ref[...].astype(F32)
    lanes = total.shape[2]
    for q in range(4):
        reduce_ref[4 * q : 4 * q + 4] = total[q]
        expand_ref[:, q * lanes : (q + 1) * lanes] = total[13 + q]
    conv_ref[...] = total[4:13]


def finish(own, shares):
    lanes = own.shape[2]
    shapes = ((16, lanes), (9, 4, lanes), (4, 4 * lanes))
    args = (own, *shares)
    g_reduce, g_conv, g_expand = pl.pallas_call(
        finish_kernel,
        out_shape=[jax.ShapeDtypeStruct(s, F32) for s in shapes],
        grid=(1,),
        in_specs=[full(a.shape) for a in args],
        out_specs=[full(s) for s in shapes],
        compiler_params=params(4),
        name="finish_gradients",
    )(*args)
    return g_reduce, g_conv.reshape(3, 3, 4, lanes), g_expand


def neighbours(first, last, tiles):
    pairs = [(i, i + 1) for i in range(tiles - 1)]
    low = lax.ppermute(last, "tile", pairs)
    high = lax.ppermute(first, "tile", [(b, a) for a, b in pairs])
    return low, high


def per_device(block_inputs, out_grad, tissue, w_reduce, w_conv, w_expand, inner_affine, outer_affine):
    section = lax.axis_index("section")
    sections = lax.axis_size("section")
    tile = lax.axis_index("tile")
    tiles = lax.axis_size("tile")
    x = block_inputs[0]
    rows, hgt, width, ch = x.shape
    wr, we = w_reduce[0], w_expand[0]
    inner_w = wr.shape[1]
    wc = w_conv[0].reshape(9 * inner_w, inner_w)
    inner, outer = inner_affine[0], outer_affine[0]

    lo, hi = neighbours(*edges(tissue, x, out_grad), tiles)
    own, *at_hand = inside(x, wr, inner, out_grad, wc, we)

    ends = jnp.stack([tile > 0, tile < tiles - 1]).astype(jnp.int32)
    ahead = (ends, tissue, lo, hi, own, inner, outer, *at_hand)
    first_row = forward(range(1), (), *ahead)
    all_rows = forward(range(1, rows), first_row, *ahead)
    mz, h2, h1, pad, seed = all_rows
    z_now = (tile // CORES) % Z
    xt, pt, ht = turn(x, pad, h2, picks(inner_w, z_now))

    back_one = [(i, i - 1) for i in range(1, sections)]
    slots = rows + LAG * (sections - 1)
    arriving = [jnp.zeros((hgt * (width + 2), ch), BF16)] * LAG
    per_slot = []
    for slot in range(slots):
        micro = slot - LAG * (sections - 1 - section)
        info = jnp.stack(
            [jnp.clip(micro, 0, rows - 1), (section == sections - 1).astype(micro.dtype)]
        ).astype(jnp.int32)
        hand_on = slot + LAG < slots
        senders = [s for s in range(1, sections) if 0 <= slot - LAG * (sections - 1 - s) < rows]
        sent = width + 2 * max(senders, default=1)
        mz_s, h2_s, h1_s, _, seed_s = all_rows if slot else first_row
        if slot == 0:
            info = info.at[0].set(0)
        *saved, last = chain_step(
            info, arriving[slot], seed_s, mz_s, h2_s, h1_s, *at_hand[:1:-1], inner, outer, hgt, hand_on, sent
        )
        if hand_on:
            arriving.append(lax.ppermute(last, "section", back_one))
        else:
            saved.append(last)
        per_slot.append(saved)
    gi, g3, g2, g1 = zip(*per_slot)
    info = jnp.stack([tile % CORES, tile // (CORES * Z), section]).astype(jnp.int32)
    early, late = range(rows - 1), range(rows - 1, rows)
    so_far = weight_grads(info, (0, 1), early, (xt, pt, ht, pt), (g1, g2, g3), (), "weight_gradients_early")
    sums_a = weight_grads(info, (0,), late, (xt, pt), (g1, g2), so_far[:2], "weight_gradients_a")
    sums_b = weight_grads(info, (1,), late, (ht, pt), (g3, g2), so_far[2:], "weight_gradients_b")
    g_reduce, g_conv, g_expand = scatter_sum(*sums_a, *sums_b)
    grad_inputs = collect(info, gi, rows)
    grad_inputs = grad_inputs.reshape(rows, hgt, width, ch)
    return grad_inputs[None], g_reduce[None], g_conv[None], g_expand[None]


def solution(mesh):
    in_specs = (
        P("section", None, None, "tile", None),
        P(None, None, "tile", None),
        P(None, "tile"),
        P("section", None, None),
        P("section", None, None, None, None),
        P("section", None, None),
        P("section", None, None),
        P("section", None, None),
    )
    out_specs = (
        P("section", None, None, "tile", None),
        P("section", "tile", None),
        P("section", None, None, "tile", None),
        P("section", "tile", None),
    )
    return jax.shard_map(
        per_device, mesh=mesh, in_specs=in_specs, out_specs=out_specs, check_vma=False
    )
```

```python
import functools

import jax
import jax.numpy as jnp
from jax import lax
from jax.experimental import pallas as pl
from jax.experimental.pallas import tpu as pltpu
from jax.sharding import PartitionSpec as P

TILE_W = 8
SECTIONS = 4
X, Z, CORES = 4, 8, 2
EDGE = 8
RIM = 4
BF16, F32 = jnp.bfloat16, jnp.float32
LAG = 2
SEGS, A_SEGS = 17, 8
Z_ORDER = (5, 3, 7, 1, 4, 2, 6, 0)


def params(mib):
    return pltpu.CompilerParams(vmem_limit_bytes=mib * 1024 * 1024)


def dot(left, right):
    return jnp.dot(left, right, preferred_element_type=F32)


def dot_t(left, right):
    return lax.dot_general(left, right, (((1,), (1,)), ((), ())), preferred_element_type=F32)


def full(shape):
    return pl.BlockSpec(shape, lambda *_: (0,) * len(shape), pipeline_mode=pl.Buffered(1))


def edges_kernel(tissue, x_ref, og_ref, first_ref, last_ref, og_s, seed_s, sems):
    rows, hgt, width, ch = x_ref.shape
    sides = (
        (first_ref, 0, 0, 0),
        (last_ref, width - EDGE, tissue.shape[1] - 1, EDGE - RIM),
    )
    plain, fetched, handed = [], [], []
    for n, (out, start, _, _) in enumerate(sides):
        cols = pl.ds(start, EDGE)
        fetched.append(pltpu.make_async_copy(og_ref.at[:, :, cols], og_s.at[n], sems.at[n]))
        plain.append(pltpu.make_async_copy(x_ref.at[:, :, cols], out.at[:, pl.ds(0, hgt)], sems.at[2 + n]))
        handed.append(pltpu.make_async_copy(seed_s.at[n], out.at[:, pl.ds(hgt, hgt // 2)], sems.at[4 + n]))
    for copy in fetched + plain:
        copy.start()
    for n, (_, _, tile, at) in enumerate(sides):
        fetched[n].wait()
        for r in range(rows):
            seed = og_s[n, r].astype(F32)[:, at : at + RIM] * tissue[r, tile].astype(F32)
            for pair in range(hgt // 2):
                both = jnp.concatenate([seed[2 * pair], seed[2 * pair + 1]], axis=0)
                seed_s[n, r, pair] = both.astype(BF16)
        handed[n].start()
    for copy in plain + handed:
        copy.wait()


def edges(tissue, x, og):
    rows, hgt, width, ch = x.shape
    out = (rows, hgt + hgt // 2, EDGE, ch)
    return pl.pallas_call(
        edges_kernel,
        out_shape=[jax.ShapeDtypeStruct(out, BF16)] * 2,
        grid_spec=pltpu.PrefetchScalarGridSpec(
            num_scalar_prefetch=1,
            grid=(1,),
            in_specs=[pl.BlockSpec(memory_space=pl.ANY)] * 2,
            out_specs=[pl.BlockSpec(memory_space=pl.ANY)] * 2,
            scratch_shapes=[
                pltpu.VMEM((2, rows, hgt, EDGE, ch), BF16),
                pltpu.VMEM((2, rows, hgt // 2, EDGE, ch), BF16),
                pltpu.SemaphoreType.DMA((6,)),
            ],
        ),
        compiler_params=params(60),
        name="edge_columns",
    )(tissue, x, og)


def hidden_one(part, wr, inner_ref):
    rows, hgt, cols, ch = part.shape
    flat = part.astype(F32).reshape(-1, ch).astype(BF16)
    pre = dot(flat, wr) * inner_ref[0:1] + inner_ref[1:2]
    return jnp.maximum(pre, 0.0).astype(BF16).astype(F32).reshape(rows, hgt, cols, -1)


def inside_kernel(x_ref, wr_ref, inner_ref, og_ref, wc_ref, we_ref, h1_ref, *kept):
    h1_ref[...] = hidden_one(x_ref[...], wr_ref[...], inner_ref).astype(BF16)
    for ref, out in zip((x_ref, og_ref, wr_ref, wc_ref, we_ref), kept):
        out[...] = ref[...]


def inside(x, wr, inner, og, wc, we):
    args = (x, wr, inner, og, wc, we)
    shapes = (x.shape[:3] + (wr.shape[1],),) + tuple(a.shape for a in (x, og, wr, wc, we))
    return pl.pallas_call(
        inside_kernel,
        out_shape=[jax.ShapeDtypeStruct(s, BF16) for s in shapes],
        grid=(1,),
        in_specs=[full(a.shape) for a in args],
        out_specs=[full(s) for s in shapes],
        compiler_params=params(12),
        cost_estimate=pl.CostEstimate(flops=300_000_000, bytes_accessed=9_000_000, transcendentals=0),
        name="forward_own_columns",
    )(*args)


def forward_kernel(
    some, held, ends, tissue, lo_ref, hi_ref, own_ref, inner_ref, outer_ref, x_ref, og_ref, wr_ref, wc_ref, we_ref, *refs,
):
    before, refs = refs[:held], refs[held:]
    mz_ref, h2_ref, h1_ref, pad_ref, seed_ref, xs, hs, patches, ss = refs
    hgt, width, ch = x_ref.shape[1:]
    inner_w = wr_ref.shape[1]
    wide = width + 2 * RIM
    per_row = hgt * wide
    count, start = len(some), some[0]
    these = slice(start, start + count)
    for ref, out in zip(before, (mz_ref, h2_ref, h1_ref, pad_ref, seed_ref)):
        out[:start] = ref[...]
    into = pl.ds(start if held else 0, count)
    hs[:, 0] = jnp.zeros((count, width + 2 * EDGE, inner_w), F32)
    hs[:, hgt + 1] = jnp.zeros((count, width + 2 * EDGE, inner_w), F32)
    hs[:, 1 : hgt + 1, EDGE : EDGE + width] = own_ref[these].astype(F32)
    xs[:, :, EDGE : EDGE + width] = x_ref[these].astype(F32)
    for ref, at, keep in ((lo_ref, 0, ends[0]), (hi_ref, EDGE + width, ends[1])):
        part = ref[these, :hgt]
        xs[:, :, at : at + EDGE] = part.astype(F32)
        hs[:, 1 : hgt + 1, at : at + EDGE] = hidden_one(part, wr_ref[...], inner_ref) * keep.astype(F32)
    pad_ref[into] = hs[...].astype(BF16)
    first = EDGE - RIM - 1
    for k in range(9):
        dr, dc = divmod(k, 3)
        piece = hs[:, dr : dr + hgt, first + dc : first + dc + wide]
        piece = piece.reshape(-1, inner_w).astype(BF16)
        patches[:, k * inner_w : (k + 1) * inner_w] = piece
        if k == 4:
            h1_ref[into] = piece.reshape(count, per_row, inner_w)
    pre = dot(patches[...], wc_ref[...]) * inner_ref[2:3] + inner_ref[3:4]
    hid = jnp.maximum(pre, 0.0).astype(BF16)
    h2_ref[into] = hid.reshape(count, per_row, inner_w)
    for n, r in enumerate(some):
        out = r if held else n
        part = hid[n * per_row : (n + 1) * per_row]
        z = dot(part, we_ref[...]) * outer_ref[0:1] + outer_ref[1:2]
        z = z + xs[n, :, EDGE - RIM : EDGE - RIM + wide].reshape(per_row, ch)
        mz_ref[out] = jnp.where(z > 0, 1.0, 0.0).astype(BF16)
        for ref, at in ((lo_ref, 0), (hi_ref, RIM + width)):
            for pair in range(hgt // 2):
                both = ref[r, hgt + pair].astype(F32)
                ss[2 * pair, at : at + RIM] = both[:RIM]
                ss[2 * pair + 1, at : at + RIM] = both[RIM:]
        og = og_ref[r].astype(F32)
        for tile in range(width // TILE_W):
            cols = og[:, tile * TILE_W : (tile + 1) * TILE_W] * tissue[r, tile].astype(F32)
            ss[:, RIM + tile * TILE_W : RIM + (tile + 1) * TILE_W] = cols
        seed_ref[out] = ss[...].reshape(per_row, ch).astype(BF16)


def forward(some, before, ends, tissue, lo, hi, own, inner, outer, x, og, wr, wc, we):
    rows, hgt, width, ch = x.shape
    inner_w = wr.shape[1]
    wide = width + 2 * RIM
    pos = hgt * wide
    count = len(some)
    out_rows = rows if before else count
    out_shapes = (
        (out_rows, pos, ch),
        (out_rows, pos, inner_w),
        (out_rows, pos, inner_w),
        (out_rows, hgt + 2, width + 2 * EDGE, inner_w),
        (out_rows, pos, ch),
    )
    blocks = (lo, hi, own, inner, outer, x, og, wr, wc, we, *before)
    return pl.pallas_call(
        functools.partial(forward_kernel, some, len(before)),
        out_shape=[jax.ShapeDtypeStruct(s, BF16) for s in out_shapes],
        grid_spec=pltpu.PrefetchScalarGridSpec(
            num_scalar_prefetch=2,
            grid=(1,),
            in_specs=[full((some[-1] + 1,) + a.shape[1:]) for a in blocks[:2]] + [full(a.shape) for a in blocks[2:]],
            out_specs=[full(s) for s in out_shapes],
            scratch_shapes=[
                pltpu.VMEM((count, hgt, width + 2 * EDGE, ch), F32),
                pltpu.VMEM((count, hgt + 2, width + 2 * EDGE, inner_w), F32),
                pltpu.VMEM((count * pos, 9 * inner_w), BF16),
                pltpu.VMEM((hgt, wide, ch), F32),
            ],
        ),
        compiler_params=params(20),
        cost_estimate=pl.CostEstimate(
            flops=600_000_000 * count, bytes_accessed=4_000_000 * count, transcendentals=0
        ),
        name="forward_rows",
    )(ends, tissue, *blocks)


def chain_kernel(
    info, gy_ref, seed_ref, mz_ref, h2_ref, h1_ref, we_ref, wc_ref, wr_ref, inner_ref, outer_ref,
    g3_ref, g2_ref, g1_ref, *more, with_gi,
):
    gi_ref, more = (more[0], more[1:]) if with_gi else (None, more)
    *wire_ref, wide_s, pad_s, flat_s = more
    inner_w = we_ref.shape[0]
    hgt, wide, ch = wide_s.shape
    pos = hgt * wide
    width = wide - 2 * RIM
    lead = 8

    def center(value):
        lanes = value.shape[1]
        wide_s[:, :, :lanes] = value.reshape(hgt, wide, lanes)
        return wide_s[:, RIM : RIM + width, :lanes].reshape(hgt * width, lanes).astype(BF16)

    cols = gy_ref.shape[0] // hgt
    at = (wide - cols) // 2
    flat_s[: hgt * cols] = gy_ref[...].astype(F32)
    wide_s[...] = jnp.zeros_like(wide_s)
    for h in range(hgt):
        wide_s[h, at : at + cols] = flat_s[h * cols : (h + 1) * cols]
    gy = jnp.where(info[1] == 1, seed_ref[0].astype(F32), wide_s[...].reshape(pos, ch))
    gz = gy * mz_ref[0].astype(F32)
    g3 = (gz * outer_ref[0:1]).astype(BF16)
    g3_ref[...] = center(g3.astype(F32))
    g2 = jnp.where(h2_ref[0].astype(F32) > 0, dot_t(g3, we_ref[...]) * inner_ref[2:3], 0.0)
    g2 = g2.astype(BF16).astype(F32)
    pad_s[...] = jnp.zeros_like(pad_s)
    pad_s[1 : hgt + 1, lead : lead + wide] = g2.reshape(hgt, wide, inner_w)
    g2_ref[...] = (
        pad_s[1 : hgt + 1, lead + RIM : lead + RIM + width].reshape(hgt * width, inner_w).astype(BF16)
    )
    back = jnp.zeros((pos, inner_w), F32)
    for k in range(9):
        dr, dc = divmod(k, 3)
        piece = pad_s[2 - dr : 2 - dr + hgt, lead + 1 - dc : lead + 1 - dc + wide]
        back = back + dot_t(piece.reshape(pos, inner_w).astype(BF16), wc_ref[k * inner_w : (k + 1) * inner_w])
    g1 = jnp.where(h1_ref[0].astype(F32) > 0, back * inner_ref[0:1], 0.0).astype(BF16)
    g1_ref[...] = center(g1.astype(F32))
    if gi_ref is None:
        return
    gi = gz + dot_t(g1, wr_ref[...])
    gi_ref[...] = center(gi)
    if wire_ref:
        cols = wire_ref[0].shape[0] // hgt
        at = (wide - cols) // 2
        for h in range(hgt):
            flat_s[h * cols : (h + 1) * cols] = wide_s[h, at : at + cols]
        wire_ref[0][...] = flat_s[: hgt * cols].astype(BF16)


def chain_step(info, gy, seed, mz, h2, h1, we, wc, wr, inner, outer, hgt, hand_on, sent, with_gi=True):
    pos, ch = seed.shape[1:]
    inner_w = we.shape[0]
    wide = pos // hgt
    kept = hgt * (wide - 2 * RIM)

    def row(lanes):
        return pl.BlockSpec((1, pos, lanes), lambda i, info: (info[0], 0, 0))

    const = (we, wc, wr, inner, outer)
    out_shapes = [(kept, ch), (kept, inner_w), (kept, inner_w)] + [(kept, ch)] * with_gi + [(hgt * sent, ch)] * hand_on
    return pl.pallas_call(
        functools.partial(chain_kernel, with_gi=with_gi),
        out_shape=[jax.ShapeDtypeStruct(s, BF16) for s in out_shapes],
        grid_spec=pltpu.PrefetchScalarGridSpec(
            num_scalar_prefetch=1,
            grid=(1,),
            in_specs=[full(gy.shape), row(ch), row(ch), row(inner_w), row(inner_w)]
            + [full(c.shape) for c in const],
            out_specs=[full(s) for s in out_shapes],
            scratch_shapes=[
                pltpu.VMEM((hgt, wide, ch), F32),
                pltpu.VMEM((hgt + 2, wide + 16, inner_w), F32),
                pltpu.VMEM((pos, ch), F32),
            ],
        ),
        compiler_params=params(12),
        cost_estimate=pl.CostEstimate(flops=3_600_000_000, bytes_accessed=50_000_000, transcendentals=0),
        name="chain_row",
    )(info, gy, seed, mz, h2, h1, *const)


def picks(inner_w, z):
    row = jnp.arange(inner_w)
    each = row % 4
    own = jnp.asarray(Z_ORDER, row.dtype)[(row // 4) % Z] ^ z
    mid = (row // (4 * Z)) % 4
    core = row // (4 * Z * 4)
    whole = ((mid * Z + own) * CORES + core) * 4 + each
    part = (own * CORES + core) * 16 + mid * 4 + each
    return (jnp.stack([whole, part])[:, :, None] == row[None, None]).astype(BF16)


def turn_kernel(x_ref, pad_ref, h2_ref, pick_ref, xt_ref, pt_ref, ht_ref):
    rows, hgt, width, ch = x_ref.shape
    inner_w = h2_ref.shape[2]
    half = inner_w // CORES
    wide = width + 2 * RIM

    def turned(order, value, ref, at, stride):
        out = lax.dot_general(
            pick_ref[order], value, (((1,), (1,)), ((), ())), preferred_element_type=F32
        ).astype(BF16)
        for core in range(CORES):
            ref[core * stride + at : core * stride + at + half] = out[core * half : (core + 1) * half]

    flat = x_ref[...].astype(F32).reshape(-1, ch).astype(BF16)
    for part in range(ch // inner_w):
        turned(1, flat[:, part * inner_w : (part + 1) * inner_w], xt_ref, part * half, ch // CORES)
    padded = pad_ref[...].astype(F32)
    for k in range(9):
        dr, dc = divmod(k, 3)
        piece = padded[:, dr : dr + hgt, EDGE - 1 + dc : EDGE - 1 + dc + width]
        turned(0, piece.reshape(-1, inner_w).astype(BF16), pt_ref, k * half, 9 * half)
    h2 = h2_ref[...].astype(F32).reshape(rows * hgt, wide, inner_w)[:, RIM : RIM + width]
    turned(0, h2.reshape(-1, inner_w).astype(BF16), ht_ref, 0, half)


def turn(x, pad, h2, pick):
    rows, hgt, width, ch = x.shape
    inner_w = h2.shape[2]
    pos = rows * hgt * width
    args = (x, pad, h2, pick)
    shapes = ((ch, pos), (9 * inner_w, pos), (inner_w, pos))
    return pl.pallas_call(
        turn_kernel,
        out_shape=[jax.ShapeDtypeStruct(s, BF16) for s in shapes],
        grid=(1,),
        in_specs=[full(a.shape) for a in args],
        out_specs=[full(s) for s in shapes],
        compiler_params=params(20),
        cost_estimate=pl.CostEstimate(flops=2_000_000_000, bytes_accessed=8_000_000, transcendentals=0),
        name="turn_activations",
    )(*args)


def place(segment, target, x):
    as_int = lambda cond: jnp.where(cond, 1, 0)
    if segment < A_SEGS:
        side = as_int((x == 1) | (x == 2))
        keep = as_int(side == (1 if target in (1, 2) else 0))
        last = as_int(x // 2 == target // 2)
        return ((keep * 2 + last) * A_SEGS + segment) * 32
    keep = as_int(x // 2 == target // 2)
    same = as_int(x % 2 == target % 2)
    last = jnp.where(keep == 1, same, 1 - same)
    return ((keep * 2 + last) * (SEGS - A_SEGS) + segment - A_SEGS) * 32


def products(part, side, x, left, right, cols, out_ref, so_far):
    first_ref, pt_ref = left
    inner_w = pt_ref.shape[0] // 9
    half = inner_w // CORES
    first = first_ref.shape[0] // CORES
    ks = range(A_SEGS - 4) if part == 0 else range(A_SEGS - 4, 9)

    def put(target, segment, value):
        rows = pl.ds(pl.multiple_of(place(segment, target, x), 32), value.shape[0])
        if so_far is not None:
            value = value + so_far[rows].astype(F32)
        out_ref[rows] = value.astype(BF16)

    total = dot(first_ref[pl.ds(pl.multiple_of(side * first, first), first), cols], right[0])
    if part == 0:
        for target in range(X):
            put(target, 0, total[target * half : (target + 1) * half])
    else:
        for j in range(4):
            for target in range(X):
                put(target, 13 + j, total[target * 32 : target * 32 + 32, j * inner_w : (j + 1) * inner_w])
    at = pl.multiple_of(side * 9 * half + ks[0] * half, half)
    total = dot(pt_ref[pl.ds(at, len(ks) * half), cols], right[1])
    for n, k in enumerate(ks):
        for target in range(X):
            put(target, 4 + k, total[n * half + target * 32 : n * half + target * 32 + 32])


def weights_kernel(parts, rows, by_row, added, info, *refs):
    count = len(parts)
    lefts, refs = refs[: 2 * count], refs[2 * count :]
    so_far, refs = (refs[: 2 * count], refs[2 * count :]) if added else ((None,) * (2 * count), refs)
    kinds = 2 if count == 1 else 3
    slots = []
    for _ in range(kinds):
        slots.append(refs[: len(by_row)])
        refs = refs[len(by_row) :]
    outs, stores, sems = refs[: 2 * count], refs[2 * count : 2 * count + kinds], refs[-1]
    core, x, section = info[0], info[1], info[2]

    def copy(kind, n, slot):
        return pltpu.make_async_copy(slots[kind][by_row.index(slot)], stores[kind].at[n], sems.at[kind, n])

    for s, used in enumerate(slots_of(rows)):
        @pl.when(section == s)
        def _():
            for kind in range(kinds):
                for n, slot in enumerate(used):
                    copy(kind, n, slot).start()

    held = []
    for kind in range(kinds):
        for n in range(len(rows)):
            copy(kind, n, by_row[0]).wait()
        kept, lanes = stores[kind].shape[1:]
        held.append(stores[kind][...].reshape(len(rows) * kept, lanes))
    cols = slice(rows[0] * kept, (rows[-1] + 1) * kept)
    for i, part in enumerate(parts):
        right = (held[0], held[1]) if count == 1 or part == 0 else (held[2], held[1])
        for n, side in enumerate((core, 1 - core)):
            products(part, side, x, lefts[2 * i : 2 * i + 2], right, cols, outs[2 * i + n], so_far[2 * i + n])


def slots_of(rows):
    return [[LAG * (SECTIONS - 1 - s) + r for r in rows] for s in range(SECTIONS)]


def weight_grads(info, parts, rows, lefts, saved, so_far, name):
    by_row = sorted({slot for used in slots_of(rows) for slot in used})
    kept = saved[0][0].shape[0]
    inner_w = lefts[1].shape[0] // 9
    sizes = [(A_SEGS if part == 0 else SEGS - A_SEGS) * X * 32 for part in parts]
    out_shapes = [(size, inner_w) for size in sizes for _ in range(2)]
    blocks = tuple(lefts) + tuple(so_far)
    return pl.pallas_call(
        functools.partial(weights_kernel, parts, rows, by_row, len(so_far) > 0),
        out_shape=[jax.ShapeDtypeStruct(s, BF16) for s in out_shapes],
        grid_spec=pltpu.PrefetchScalarGridSpec(
            num_scalar_prefetch=1,
            grid=(1,),
            in_specs=[full(a.shape) for a in blocks]
            + [pl.BlockSpec(memory_space=pl.ANY)] * (len(by_row) * len(saved)),
            out_specs=[full(s) for s in out_shapes],
            scratch_shapes=[pltpu.VMEM((len(rows), kept, kind[0].shape[1]), BF16) for kind in saved]
            + [pltpu.SemaphoreType.DMA((len(saved), len(rows)))],
        ),
        compiler_params=params(20),
        cost_estimate=pl.CostEstimate(
            flops=300_000_000 * len(rows), bytes_accessed=2_000_000 * len(rows), transcendentals=0
        ),
        name=name,
    )(info, *blocks, *[kind[slot] for kind in saved for slot in by_row])


def collect_kernel(slots, info, *refs):
    out_ref, sems = refs[slots], refs[slots + 1]
    rows = range(out_ref.shape[0])

    def copy(n, slot):
        return pltpu.make_async_copy(refs[slot], out_ref.at[n], sems.at[n])

    for s, used in enumerate(slots_of(rows)):
        @pl.when(info[2] == s)
        def _():
            for n, slot in enumerate(used):
                copy(n, slot).start()

    for n in rows:
        copy(n, n).wait()


def collect(info, gi, rows):
    return pl.pallas_call(
        functools.partial(collect_kernel, len(gi)),
        out_shape=jax.ShapeDtypeStruct((rows,) + gi[0].shape, BF16),
        grid_spec=pltpu.PrefetchScalarGridSpec(
            num_scalar_prefetch=1,
            grid=(1,),
            in_specs=[pl.BlockSpec(memory_space=pl.ANY)] * len(gi),
            out_specs=pl.BlockSpec(memory_space=pl.ANY),
            scratch_shapes=[pltpu.SemaphoreType.DMA((rows,))],
        ),
        compiler_params=params(4),
        cost_estimate=pl.CostEstimate(flops=0, bytes_accessed=2_000_000, transcendentals=0),
        name="collect_grad_inputs",
    )(info, *gi)


def tile_pairs(partner):
    pairs = []
    for x in range(X):
        for z in range(Z):
            for c in range(CORES):
                px, pz, pc = partner(x, z, c)
                pairs.append(((x * Z + z) * CORES + c, (px * Z + pz) * CORES + pc))
    return pairs


def swap(value, partner):
    return lax.ppermute(value.astype(BF16), "tile", tile_pairs(partner))


def scatter_sum(beside, keep_a, send_a, keep_b, send_b):
    lanes = keep_a.shape[-1]
    other_core = lambda x, z, c: (x, z, 1 - c)
    inner_pair = lambda x, z, c: (x ^ 1, z, c)
    outer_pair = lambda x, z, c: (3 - x, z, c)

    def along_x(keep, send, pairs):
        got = swap(send, other_core)
        own = lambda first, last: keep[first:last].astype(F32) + got[first:last].astype(F32)
        size = keep.shape[0]
        half, quart = size // 2, size // 4
        got_1 = swap(own(0, half), pairs[0])
        got_2 = swap(own(half, half + quart) + got_1[:quart].astype(F32), pairs[1])
        return own(half + quart, size) + got_1[quart:].astype(F32) + got_2.astype(F32)

    part_a = along_x(keep_a, send_a, (inner_pair, outer_pair))
    part_b = along_x(keep_b, send_b, (outer_pair, inner_pair))
    total = jnp.concatenate([part_a, part_b], axis=0).reshape(SEGS, Z * 4, lanes)
    total, beside = lax.optimization_barrier((total, beside))
    for bits in (1, 2):
        count = total.shape[1] // 2
        got = swap(total[:, :count], lambda x, z, c, b=bits: (x, z ^ b, c))
        total = total[:, count:] + got.astype(F32)
    shares = finish(total[:, 4:], [swap(total[:, :4], lambda x, z, c: (x, z ^ 6, c))])
    return (*shares, beside)


def finish_kernel(own_ref, *refs):
    reduce_ref, conv_ref, expand_ref = refs[-3:]
    total = own_ref[...]
    for ref in refs[:-3]:
        total = total + ref[...].astype(F32)
    lanes = total.shape[2]
    for q in range(4):
        reduce_ref[4 * q : 4 * q + 4] = total[q]
        expand_ref[:, q * lanes : (q + 1) * lanes] = total[13 + q]
    conv_ref[...] = total[4:13]


def finish(own, shares):
    lanes = own.shape[2]
    shapes = ((16, lanes), (9, 4, lanes), (4, 4 * lanes))
    args = (own, *shares)
    g_reduce, g_conv, g_expand = pl.pallas_call(
        finish_kernel,
        out_shape=[jax.ShapeDtypeStruct(s, F32) for s in shapes],
        grid=(1,),
        in_specs=[full(a.shape) for a in args],
        out_specs=[full(s) for s in shapes],
        compiler_params=params(4),
        name="finish_gradients",
    )(*args)
    return g_reduce, g_conv.reshape(3, 3, 4, lanes), g_expand


def neighbours(first, last, tiles):
    pairs = [(i, i + 1) for i in range(tiles - 1)]
    low = lax.ppermute(last, "tile", pairs)
    high = lax.ppermute(first, "tile", [(b, a) for a, b in pairs])
    return low, high


def per_device(block_inputs, out_grad, tissue, w_reduce, w_conv, w_expand, inner_affine, outer_affine):
    section = lax.axis_index("section")
    sections = lax.axis_size("section")
    tile = lax.axis_index("tile")
    tiles = lax.axis_size("tile")
    x = block_inputs[0]
    rows, hgt, width, ch = x.shape
    wr, we = w_reduce[0], w_expand[0]
    inner_w = wr.shape[1]
    wc = w_conv[0].reshape(9 * inner_w, inner_w)
    inner, outer = inner_affine[0], outer_affine[0]

    lo, hi = neighbours(*edges(tissue, x, out_grad), tiles)
    own, *at_hand = inside(x, wr, inner, out_grad, wc, we)

    ends = jnp.stack([tile > 0, tile < tiles - 1]).astype(jnp.int32)
    ahead = (ends, tissue, lo, hi, own, inner, outer, *at_hand)
    first_row = forward(range(1), (), *ahead)
    all_rows = forward(range(1, rows), first_row, *ahead)
    mz, h2, h1, pad, seed = all_rows
    z_now = (tile // CORES) % Z
    xt, pt, ht = turn(x, pad, h2, picks(inner_w, z_now))

    back_one = [(i, i - 1) for i in range(1, sections)]
    slots = rows + LAG * (sections - 1)
    arriving = [jnp.zeros((hgt * (width + 2), ch), BF16)] * LAG
    per_slot = []
    for slot in range(slots):
        micro = slot - LAG * (sections - 1 - section)
        info = jnp.stack(
            [jnp.clip(micro, 0, rows - 1), (section == sections - 1).astype(micro.dtype)]
        ).astype(jnp.int32)
        hand_on = slot + LAG < slots
        senders = [s for s in range(1, sections) if 0 <= slot - LAG * (sections - 1 - s) < rows]
        sent = width + 2 * max(senders, default=1)
        mz_s, h2_s, h1_s, _, seed_s = all_rows if slot else first_row
        if slot == 0:
            info = info.at[0].set(0)
        step = functools.partial(
            chain_step, info, arriving[slot], seed_s, mz_s, h2_s, h1_s, *at_hand[:1:-1], inner, outer, hgt, hand_on, sent
        )
        saved = step()
        if hand_on:
            arriving.append(lax.ppermute(saved[4], "section", back_one))
        if slot == slots - 1:
            saved = [*step(with_gi=False), saved[3]]
        per_slot.append(saved[:4])
    g3, g2, g1, gi = zip(*per_slot)
    info = jnp.stack([tile % CORES, tile // (CORES * Z), section]).astype(jnp.int32)
    early, late = range(rows - 1), range(rows - 1, rows)
    so_far = weight_grads(info, (0, 1), early, (xt, pt, ht, pt), (g1, g2, g3), (), "weight_gradients_early")
    sums_a = weight_grads(info, (0,), late, (xt, pt), (g1, g2), so_far[:2], "weight_gradients_a")
    sums_b = weight_grads(info, (1,), late, (ht, pt), (g3, g2), so_far[2:], "weight_gradients_b")
    g_reduce, g_conv, g_expand, grad_inputs = scatter_sum(collect(info, gi, rows), *sums_a, *sums_b)
    grad_inputs = grad_inputs.reshape(rows, hgt, width, ch)
    return grad_inputs[None], g_reduce[None], g_conv[None], g_expand[None]


def solution(mesh):
    in_specs = (
        P("section", None, None, "tile", None),
        P(None, None, "tile", None),
        P(None, "tile"),
        P("section", None, None),
        P("section", None, None, None, None),
        P("section", None, None),
        P("section", None, None),
        P("section", None, None),
    )
    out_specs = (
        P("section", None, None, "tile", None),
        P("section", "tile", None),
        P("section", None, None, "tile", None),
        P("section", "tile", None),
    )
    return jax.shard_map(
        per_device, mesh=mesh, in_specs=in_specs, out_specs=out_specs, check_vma=False
    )
```

```python
import functools

import jax
import jax.numpy as jnp
from jax import lax
from jax.experimental import pallas as pl
from jax.experimental.pallas import tpu as pltpu
from jax.sharding import PartitionSpec as P

TILE_W = 8
SECTIONS = 4
X, Z, CORES = 4, 8, 2
EDGE = 8
RIM = 4
BF16, F32 = jnp.bfloat16, jnp.float32
LAG = 2
SEGS, A_SEGS = 17, 8
Z_ORDER = (5, 3, 7, 1, 4, 2, 6, 0)


def params(mib):
    return pltpu.CompilerParams(vmem_limit_bytes=mib * 1024 * 1024)


def dot(left, right):
    return jnp.dot(left, right, preferred_element_type=F32)


def dot_t(left, right):
    return lax.dot_general(left, right, (((1,), (1,)), ((), ())), preferred_element_type=F32)


def full(shape):
    return pl.BlockSpec(shape, lambda *_: (0,) * len(shape), pipeline_mode=pl.Buffered(1))


def edges_kernel(tissue, x_ref, og_ref, first_ref, last_ref, og_s, stage, sems):
    rows, hgt, width, ch = x_ref.shape
    sides = (
        (first_ref, 0, 0, 0),
        (last_ref, width - EDGE, tissue.shape[1] - 1, EDGE - RIM),
    )
    from_og, from_x, handed = [], [], []
    for n, (out, start, _, _) in enumerate(sides):
        cols = pl.ds(start, EDGE)
        from_og.append(pltpu.make_async_copy(og_ref.at[:, :, cols], og_s.at[n], sems.at[n]))
        from_x.append(
            pltpu.make_async_copy(x_ref.at[:, :, cols], stage.at[n, :, pl.ds(0, hgt)], sems.at[2 + n])
        )
        handed.append(pltpu.make_async_copy(stage.at[n], out, sems.at[4 + n]))
    for copy in from_og + from_x:
        copy.start()
    for n, (_, _, tile, at) in enumerate(sides):
        from_og[n].wait()
        for r in range(rows):
            seed = og_s[n, r].astype(F32)[:, at : at + RIM] * tissue[r, tile].astype(F32)
            for pair in range(hgt // 2):
                both = jnp.concatenate([seed[2 * pair], seed[2 * pair + 1]], axis=0)
                stage[n, r, hgt + pair] = both.astype(BF16)
        from_x[n].wait()
        handed[n].start()
    for copy in handed:
        copy.wait()


def edges(tissue, x, og):
    rows, hgt, width, ch = x.shape
    out = (rows, hgt + hgt // 2, EDGE, ch)
    return pl.pallas_call(
        edges_kernel,
        out_shape=[jax.ShapeDtypeStruct(out, BF16)] * 2,
        grid_spec=pltpu.PrefetchScalarGridSpec(
            num_scalar_prefetch=1,
            grid=(1,),
            in_specs=[pl.BlockSpec(memory_space=pl.ANY)] * 2,
            out_specs=[pl.BlockSpec(memory_space=pl.ANY)] * 2,
            scratch_shapes=[
                pltpu.VMEM((2, rows, hgt, EDGE, ch), BF16),
                pltpu.VMEM((2,) + out, BF16),
                pltpu.SemaphoreType.DMA((6,)),
            ],
        ),
        compiler_params=params(60),
        name="edge_columns",
    )(tissue, x, og)


def hidden_one(part, wr, inner_ref):
    rows, hgt, cols, ch = part.shape
    flat = part.astype(F32).reshape(-1, ch).astype(BF16)
    pre = dot(flat, wr) * inner_ref[0:1] + inner_ref[1:2]
    return jnp.maximum(pre, 0.0).astype(BF16).astype(F32).reshape(rows, hgt, cols, -1)


def inside_kernel(x_ref, wr_ref, inner_ref, og_ref, wc_ref, we_ref, h1_ref, *kept):
    h1_ref[...] = hidden_one(x_ref[...], wr_ref[...], inner_ref).astype(BF16)
    for ref, out in zip((x_ref, og_ref, wr_ref, wc_ref, we_ref), kept):
        out[...] = ref[...]


def inside(x, wr, inner, og, wc, we):
    args = (x, wr, inner, og, wc, we)
    shapes = (x.shape[:3] + (wr.shape[1],),) + tuple(a.shape for a in (x, og, wr, wc, we))
    return pl.pallas_call(
        inside_kernel,
        out_shape=[jax.ShapeDtypeStruct(s, BF16) for s in shapes],
        grid=(1,),
        in_specs=[full(a.shape) for a in args],
        out_specs=[full(s) for s in shapes],
        compiler_params=params(12),
        cost_estimate=pl.CostEstimate(flops=300_000_000, bytes_accessed=9_000_000, transcendentals=0),
        name="forward_own_columns",
    )(*args)


def forward_kernel(
    some, held, ends, tissue, lo_ref, hi_ref, own_ref, inner_ref, outer_ref, x_ref, og_ref, wr_ref, wc_ref, we_ref, *refs,
):
    before, refs = refs[:held], refs[held:]
    mz_ref, h2_ref, h1_ref, pad_ref, seed_ref, xs, hs, patches, ss = refs
    hgt, width, ch = x_ref.shape[1:]
    inner_w = wr_ref.shape[1]
    wide = width + 2 * RIM
    per_row = hgt * wide
    count, start = len(some), some[0]
    these = slice(start, start + count)
    for ref, out in zip(before, (mz_ref, h2_ref, h1_ref, pad_ref, seed_ref)):
        out[:start] = ref[...]
    into = pl.ds(start if held else 0, count)
    hs[:, 0] = jnp.zeros((count, width + 2 * EDGE, inner_w), F32)
    hs[:, hgt + 1] = jnp.zeros((count, width + 2 * EDGE, inner_w), F32)
    hs[:, 1 : hgt + 1, EDGE : EDGE + width] = own_ref[these].astype(F32)
    xs[:, :, EDGE : EDGE + width] = x_ref[these].astype(F32)
    for ref, at, keep in ((lo_ref, 0, ends[0]), (hi_ref, EDGE + width, ends[1])):
        part = ref[these, :hgt]
        xs[:, :, at : at + EDGE] = part.astype(F32)
        hs[:, 1 : hgt + 1, at : at + EDGE] = hidden_one(part, wr_ref[...], inner_ref) * keep.astype(F32)
    pad_ref[into] = hs[...].astype(BF16)
    first = EDGE - RIM - 1
    for k in range(9):
        dr, dc = divmod(k, 3)
        piece = hs[:, dr : dr + hgt, first + dc : first + dc + wide]
        piece = piece.reshape(-1, inner_w).astype(BF16)
        patches[:, k * inner_w : (k + 1) * inner_w] = piece
        if k == 4:
            h1_ref[into] = piece.reshape(count, per_row, inner_w)
    pre = dot(patches[...], wc_ref[...]) * inner_ref[2:3] + inner_ref[3:4]
    hid = jnp.maximum(pre, 0.0).astype(BF16)
    h2_ref[into] = hid.reshape(count, per_row, inner_w)
    for n, r in enumerate(some):
        out = r if held else n
        part = hid[n * per_row : (n + 1) * per_row]
        z = dot(part, we_ref[...]) * outer_ref[0:1] + outer_ref[1:2]
        z = z + xs[n, :, EDGE - RIM : EDGE - RIM + wide].reshape(per_row, ch)
        mz_ref[out] = jnp.where(z > 0, 1.0, 0.0).astype(BF16)
        for ref, at in ((lo_ref, 0), (hi_ref, RIM + width)):
            for pair in range(hgt // 2):
                both = ref[r, hgt + pair].astype(F32)
                ss[2 * pair, at : at + RIM] = both[:RIM]
                ss[2 * pair + 1, at : at + RIM] = both[RIM:]
        og = og_ref[r].astype(F32)
        for tile in range(width // TILE_W):
            cols = og[:, tile * TILE_W : (tile + 1) * TILE_W] * tissue[r, tile].astype(F32)
            ss[:, RIM + tile * TILE_W : RIM + (tile + 1) * TILE_W] = cols
        seed_ref[out] = ss[...].reshape(per_row, ch).astype(BF16)


def forward(some, before, ends, tissue, lo, hi, own, inner, outer, x, og, wr, wc, we):
    rows, hgt, width, ch = x.shape
    inner_w = wr.shape[1]
    wide = width + 2 * RIM
    pos = hgt * wide
    count = len(some)
    out_rows = rows if before else count
    out_shapes = (
        (out_rows, pos, ch),
        (out_rows, pos, inner_w),
        (out_rows, pos, inner_w),
        (out_rows, hgt + 2, width + 2 * EDGE, inner_w),
        (out_rows, pos, ch),
    )
    blocks = (lo, hi, own, inner, outer, x, og, wr, wc, we, *before)
    return pl.pallas_call(
        functools.partial(forward_kernel, some, len(before)),
        out_shape=[jax.ShapeDtypeStruct(s, BF16) for s in out_shapes],
        grid_spec=pltpu.PrefetchScalarGridSpec(
            num_scalar_prefetch=2,
            grid=(1,),
            in_specs=[full((some[-1] + 1,) + a.shape[1:]) for a in blocks[:2]] + [full(a.shape) for a in blocks[2:]],
            out_specs=[full(s) for s in out_shapes],
            scratch_shapes=[
                pltpu.VMEM((count, hgt, width + 2 * EDGE, ch), F32),
                pltpu.VMEM((count, hgt + 2, width + 2 * EDGE, inner_w), F32),
                pltpu.VMEM((count * pos, 9 * inner_w), BF16),
                pltpu.VMEM((hgt, wide, ch), F32),
            ],
        ),
        compiler_params=params(20),
        cost_estimate=pl.CostEstimate(
            flops=600_000_000 * count, bytes_accessed=4_000_000 * count, transcendentals=0
        ),
        name="forward_rows",
    )(ends, tissue, *blocks)


def chain_kernel(
    info, gy_ref, seed_ref, mz_ref, h2_ref, h1_ref, we_ref, wc_ref, wr_ref, inner_ref, outer_ref,
    g3_ref, g2_ref, g1_ref, *more, with_gi,
):
    gi_ref, more = (more[0], more[1:]) if with_gi else (None, more)
    *wire_ref, wide_s, pad_s, flat_s = more
    inner_w = we_ref.shape[0]
    hgt, wide, ch = wide_s.shape
    pos = hgt * wide
    width = wide - 2 * RIM
    lead = 8

    def center(value):
        lanes = value.shape[1]
        wide_s[:, :, :lanes] = value.reshape(hgt, wide, lanes)
        return wide_s[:, RIM : RIM + width, :lanes].reshape(hgt * width, lanes).astype(BF16)

    cols = gy_ref.shape[0] // hgt
    at = (wide - cols) // 2
    flat_s[: hgt * cols] = gy_ref[...].astype(F32)
    wide_s[...] = jnp.zeros_like(wide_s)
    for h in range(hgt):
        wide_s[h, at : at + cols] = flat_s[h * cols : (h + 1) * cols]
    gy = jnp.where(info[1] == 1, seed_ref[0].astype(F32), wide_s[...].reshape(pos, ch))
    gz = gy * mz_ref[0].astype(F32)
    g3 = (gz * outer_ref[0:1]).astype(BF16)
    g3_ref[...] = center(g3.astype(F32))
    g2 = jnp.where(h2_ref[0].astype(F32) > 0, dot_t(g3, we_ref[...]) * inner_ref[2:3], 0.0)
    g2 = g2.astype(BF16).astype(F32)
    pad_s[...] = jnp.zeros_like(pad_s)
    pad_s[1 : hgt + 1, lead : lead + wide] = g2.reshape(hgt, wide, inner_w)
    g2_ref[...] = (
        pad_s[1 : hgt + 1, lead + RIM : lead + RIM + width].reshape(hgt * width, inner_w).astype(BF16)
    )
    back = jnp.zeros((pos, inner_w), F32)
    for k in range(9):
        dr, dc = divmod(k, 3)
        piece = pad_s[2 - dr : 2 - dr + hgt, lead + 1 - dc : lead + 1 - dc + wide]
        back = back + dot_t(piece.reshape(pos, inner_w).astype(BF16), wc_ref[k * inner_w : (k + 1) * inner_w])
    g1 = jnp.where(h1_ref[0].astype(F32) > 0, back * inner_ref[0:1], 0.0).astype(BF16)
    g1_ref[...] = center(g1.astype(F32))
    if gi_ref is None:
        return
    gi = gz + dot_t(g1, wr_ref[...])
    gi_ref[...] = center(gi)
    if wire_ref:
        cols = wire_ref[0].shape[0] // hgt
        at = (wide - cols) // 2
        for h in range(hgt):
            flat_s[h * cols : (h + 1) * cols] = wide_s[h, at : at + cols]
        wire_ref[0][...] = flat_s[: hgt * cols].astype(BF16)


def chain_step(info, gy, seed, mz, h2, h1, we, wc, wr, inner, outer, hgt, hand_on, sent, with_gi=True):
    pos, ch = seed.shape[1:]
    inner_w = we.shape[0]
    wide = pos // hgt
    kept = hgt * (wide - 2 * RIM)

    def row(lanes):
        return pl.BlockSpec((1, pos, lanes), lambda i, info: (info[0], 0, 0))

    const = (we, wc, wr, inner, outer)
    out_shapes = [(kept, ch), (kept, inner_w), (kept, inner_w)] + [(kept, ch)] * with_gi + [(hgt * sent, ch)] * hand_on
    return pl.pallas_call(
        functools.partial(chain_kernel, with_gi=with_gi),
        out_shape=[jax.ShapeDtypeStruct(s, BF16) for s in out_shapes],
        grid_spec=pltpu.PrefetchScalarGridSpec(
            num_scalar_prefetch=1,
            grid=(1,),
            in_specs=[full(gy.shape), row(ch), row(ch), row(inner_w), row(inner_w)]
            + [full(c.shape) for c in const],
            out_specs=[full(s) for s in out_shapes],
            scratch_shapes=[
                pltpu.VMEM((hgt, wide, ch), F32),
                pltpu.VMEM((hgt + 2, wide + 16, inner_w), F32),
                pltpu.VMEM((pos, ch), F32),
            ],
        ),
        compiler_params=params(12),
        cost_estimate=pl.CostEstimate(flops=3_600_000_000, bytes_accessed=50_000_000, transcendentals=0),
        name="chain_row",
    )(info, gy, seed, mz, h2, h1, *const)


def picks(inner_w, z):
    row = jnp.arange(inner_w)
    each = row % 4
    own = jnp.asarray(Z_ORDER, row.dtype)[(row // 4) % Z] ^ z
    mid = (row // (4 * Z)) % 4
    core = row // (4 * Z * 4)
    whole = ((mid * Z + own) * CORES + core) * 4 + each
    part = (own * CORES + core) * 16 + mid * 4 + each
    return (jnp.stack([whole, part])[:, :, None] == row[None, None]).astype(BF16)


def turn_kernel(x_ref, pad_ref, h2_ref, pick_ref, xt_ref, pt_ref, ht_ref):
    rows, hgt, width, ch = x_ref.shape
    inner_w = h2_ref.shape[2]
    half = inner_w // CORES
    wide = width + 2 * RIM

    def turned(order, value, ref, at, stride):
        out = lax.dot_general(
            pick_ref[order], value, (((1,), (1,)), ((), ())), preferred_element_type=F32
        ).astype(BF16)
        for core in range(CORES):
            ref[core * stride + at : core * stride + at + half] = out[core * half : (core + 1) * half]

    flat = x_ref[...].astype(F32).reshape(-1, ch).astype(BF16)
    for part in range(ch // inner_w):
        turned(1, flat[:, part * inner_w : (part + 1) * inner_w], xt_ref, part * half, ch // CORES)
    padded = pad_ref[...].astype(F32)
    for k in range(9):
        dr, dc = divmod(k, 3)
        piece = padded[:, dr : dr + hgt, EDGE - 1 + dc : EDGE - 1 + dc + width]
        turned(0, piece.reshape(-1, inner_w).astype(BF16), pt_ref, k * half, 9 * half)
    h2 = h2_ref[...].astype(F32).reshape(rows * hgt, wide, inner_w)[:, RIM : RIM + width]
    turned(0, h2.reshape(-1, inner_w).astype(BF16), ht_ref, 0, half)


def turn(x, pad, h2, pick):
    rows, hgt, width, ch = x.shape
    inner_w = h2.shape[2]
    pos = rows * hgt * width
    args = (x, pad, h2, pick)
    shapes = ((ch, pos), (9 * inner_w, pos), (inner_w, pos))
    return pl.pallas_call(
        turn_kernel,
        out_shape=[jax.ShapeDtypeStruct(s, BF16) for s in shapes],
        grid=(1,),
        in_specs=[full(a.shape) for a in args],
        out_specs=[full(s) for s in shapes],
        compiler_params=params(20),
        cost_estimate=pl.CostEstimate(flops=2_000_000_000, bytes_accessed=8_000_000, transcendentals=0),
        name="turn_activations",
    )(*args)


def place(segment, target, x):
    as_int = lambda cond: jnp.where(cond, 1, 0)
    if segment < A_SEGS:
        side = as_int((x == 1) | (x == 2))
        keep = as_int(side == (1 if target in (1, 2) else 0))
        last = as_int(x // 2 == target // 2)
        return ((keep * 2 + last) * A_SEGS + segment) * 32
    keep = as_int(x // 2 == target // 2)
    same = as_int(x % 2 == target % 2)
    last = jnp.where(keep == 1, same, 1 - same)
    return ((keep * 2 + last) * (SEGS - A_SEGS) + segment - A_SEGS) * 32


def products(part, side, x, left, right, cols, out_ref, so_far):
    first_ref, pt_ref = left
    inner_w = pt_ref.shape[0] // 9
    half = inner_w // CORES
    first = first_ref.shape[0] // CORES
    ks = range(A_SEGS - 4) if part == 0 else range(A_SEGS - 4, 9)

    def put(target, segment, value):
        rows = pl.ds(pl.multiple_of(place(segment, target, x), 32), value.shape[0])
        if so_far is not None:
            value = value + so_far[rows].astype(F32)
        out_ref[rows] = value.astype(BF16)

    total = dot(first_ref[pl.ds(pl.multiple_of(side * first, first), first), cols], right[0])
    if part == 0:
        for target in range(X):
            put(target, 0, total[target * half : (target + 1) * half])
    else:
        for j in range(4):
            for target in range(X):
                put(target, 13 + j, total[target * 32 : target * 32 + 32, j * inner_w : (j + 1) * inner_w])
    at = pl.multiple_of(side * 9 * half + ks[0] * half, half)
    total = dot(pt_ref[pl.ds(at, len(ks) * half), cols], right[1])
    for n, k in enumerate(ks):
        for target in range(X):
            put(target, 4 + k, total[n * half + target * 32 : n * half + target * 32 + 32])


def weights_kernel(parts, rows, by_row, added, info, *refs):
    count = len(parts)
    lefts, refs = refs[: 2 * count], refs[2 * count :]
    so_far, refs = (refs[: 2 * count], refs[2 * count :]) if added else ((None,) * (2 * count), refs)
    kinds = 2 if count == 1 else 3
    slots = []
    for _ in range(kinds):
        slots.append(refs[: len(by_row)])
        refs = refs[len(by_row) :]
    outs, stores, sems = refs[: 2 * count], refs[2 * count : 2 * count + kinds], refs[-1]
    core, x, section = info[0], info[1], info[2]

    def copy(kind, n, slot):
        return pltpu.make_async_copy(slots[kind][by_row.index(slot)], stores[kind].at[n], sems.at[kind, n])

    for s, used in enumerate(slots_of(rows)):
        @pl.when(section == s)
        def _():
            for kind in range(kinds):
                for n, slot in enumerate(used):
                    copy(kind, n, slot).start()

    held = []
    for kind in range(kinds):
        for n in range(len(rows)):
            copy(kind, n, by_row[0]).wait()
        kept, lanes = stores[kind].shape[1:]
        held.append(stores[kind][...].reshape(len(rows) * kept, lanes))
    cols = slice(rows[0] * kept, (rows[-1] + 1) * kept)
    for i, part in enumerate(parts):
        right = (held[0], held[1]) if count == 1 or part == 0 else (held[2], held[1])
        for n, side in enumerate((core, 1 - core)):
            products(part, side, x, lefts[2 * i : 2 * i + 2], right, cols, outs[2 * i + n], so_far[2 * i + n])


def slots_of(rows):
    return [[LAG * (SECTIONS - 1 - s) + r for r in rows] for s in range(SECTIONS)]


def weight_grads(info, parts, rows, lefts, saved, so_far, name):
    by_row = sorted({slot for used in slots_of(rows) for slot in used})
    kept = saved[0][0].shape[0]
    inner_w = lefts[1].shape[0] // 9
    sizes = [(A_SEGS if part == 0 else SEGS - A_SEGS) * X * 32 for part in parts]
    out_shapes = [(size, inner_w) for size in sizes for _ in range(2)]
    blocks = tuple(lefts) + tuple(so_far)
    return pl.pallas_call(
        functools.partial(weights_kernel, parts, rows, by_row, len(so_far) > 0),
        out_shape=[jax.ShapeDtypeStruct(s, BF16) for s in out_shapes],
        grid_spec=pltpu.PrefetchScalarGridSpec(
            num_scalar_prefetch=1,
            grid=(1,),
            in_specs=[full(a.shape) for a in blocks]
            + [pl.BlockSpec(memory_space=pl.ANY)] * (len(by_row) * len(saved)),
            out_specs=[full(s) for s in out_shapes],
            scratch_shapes=[pltpu.VMEM((len(rows), kept, kind[0].shape[1]), BF16) for kind in saved]
            + [pltpu.SemaphoreType.DMA((len(saved), len(rows)))],
        ),
        compiler_params=params(20),
        cost_estimate=pl.CostEstimate(
            flops=300_000_000 * len(rows), bytes_accessed=2_000_000 * len(rows), transcendentals=0
        ),
        name=name,
    )(info, *blocks, *[kind[slot] for kind in saved for slot in by_row])


def collect_kernel(slots, info, *refs):
    out_ref, sems = refs[slots], refs[slots + 1]
    rows = range(out_ref.shape[0])

    def copy(n, slot):
        return pltpu.make_async_copy(refs[slot], out_ref.at[n], sems.at[n])

    for s, used in enumerate(slots_of(rows)):
        @pl.when(info[2] == s)
        def _():
            for n, slot in enumerate(used):
                copy(n, slot).start()

    for n in rows:
        copy(n, n).wait()


def collect(info, gi, rows):
    return pl.pallas_call(
        functools.partial(collect_kernel, len(gi)),
        out_shape=jax.ShapeDtypeStruct((rows,) + gi[0].shape, BF16),
        grid_spec=pltpu.PrefetchScalarGridSpec(
            num_scalar_prefetch=1,
            grid=(1,),
            in_specs=[pl.BlockSpec(memory_space=pl.ANY)] * len(gi),
            out_specs=pl.BlockSpec(memory_space=pl.ANY),
            scratch_shapes=[pltpu.SemaphoreType.DMA((rows,))],
        ),
        compiler_params=params(4),
        cost_estimate=pl.CostEstimate(flops=0, bytes_accessed=2_000_000, transcendentals=0),
        name="collect_grad_inputs",
    )(info, *gi)


def tile_pairs(partner):
    pairs = []
    for x in range(X):
        for z in range(Z):
            for c in range(CORES):
                px, pz, pc = partner(x, z, c)
                pairs.append(((x * Z + z) * CORES + c, (px * Z + pz) * CORES + pc))
    return pairs


def swap(value, partner):
    return lax.ppermute(value.astype(BF16), "tile", tile_pairs(partner))


def scatter_sum(beside, keep_a, send_a, keep_b, send_b):
    lanes = keep_a.shape[-1]
    other_core = lambda x, z, c: (x, z, 1 - c)
    inner_pair = lambda x, z, c: (x ^ 1, z, c)
    outer_pair = lambda x, z, c: (3 - x, z, c)

    def along_x(keep, send, pairs):
        got = swap(send, other_core)
        own = lambda first, last: keep[first:last].astype(F32) + got[first:last].astype(F32)
        size = keep.shape[0]
        half, quart = size // 2, size // 4
        got_1 = swap(own(0, half), pairs[0])
        got_2 = swap(own(half, half + quart) + got_1[:quart].astype(F32), pairs[1])
        return own(half + quart, size) + got_1[quart:].astype(F32) + got_2.astype(F32)

    part_a = along_x(keep_a, send_a, (inner_pair, outer_pair))
    part_b = along_x(keep_b, send_b, (outer_pair, inner_pair))
    total = jnp.concatenate([part_a, part_b], axis=0).reshape(SEGS, Z * 4, lanes)
    total, beside = lax.optimization_barrier((total, beside))
    for bits in (1, 2):
        count = total.shape[1] // 2
        got = swap(total[:, :count], lambda x, z, c, b=bits: (x, z ^ b, c))
        total = total[:, count:] + got.astype(F32)
    shares = finish(total[:, 4:], [swap(total[:, :4], lambda x, z, c: (x, z ^ 6, c))])
    return (*shares, beside)


def finish_kernel(own_ref, *refs):
    reduce_ref, conv_ref, expand_ref = refs[-3:]
    total = own_ref[...]
    for ref in refs[:-3]:
        total = total + ref[...].astype(F32)
    lanes = total.shape[2]
    for q in range(4):
        reduce_ref[4 * q : 4 * q + 4] = total[q]
        expand_ref[:, q * lanes : (q + 1) * lanes] = total[13 + q]
    conv_ref[...] = total[4:13]


def finish(own, shares):
    lanes = own.shape[2]
    shapes = ((16, lanes), (9, 4, lanes), (4, 4 * lanes))
    args = (own, *shares)
    g_reduce, g_conv, g_expand = pl.pallas_call(
        finish_kernel,
        out_shape=[jax.ShapeDtypeStruct(s, F32) for s in shapes],
        grid=(1,),
        in_specs=[full(a.shape) for a in args],
        out_specs=[full(s) for s in shapes],
        compiler_params=params(4),
        name="finish_gradients",
    )(*args)
    return g_reduce, g_conv.reshape(3, 3, 4, lanes), g_expand


def neighbours(first, last, tiles):
    pairs = [(i, i + 1) for i in range(tiles - 1)]
    low = lax.ppermute(last, "tile", pairs)
    high = lax.ppermute(first, "tile", [(b, a) for a, b in pairs])
    return low, high


def per_device(block_inputs, out_grad, tissue, w_reduce, w_conv, w_expand, inner_affine, outer_affine):
    section = lax.axis_index("section")
    sections = lax.axis_size("section")
    tile = lax.axis_index("tile")
    tiles = lax.axis_size("tile")
    x = block_inputs[0]
    rows, hgt, width, ch = x.shape
    wr, we = w_reduce[0], w_expand[0]
    inner_w = wr.shape[1]
    wc = w_conv[0].reshape(9 * inner_w, inner_w)
    inner, outer = inner_affine[0], outer_affine[0]

    lo, hi = neighbours(*edges(tissue, x, out_grad), tiles)
    own, *at_hand = inside(x, wr, inner, out_grad, wc, we)

    ends = jnp.stack([tile > 0, tile < tiles - 1]).astype(jnp.int32)
    ahead = (ends, tissue, lo, hi, own, inner, outer, *at_hand)
    first_row = forward(range(1), (), *ahead)
    all_rows = forward(range(1, rows), first_row, *ahead)
    mz, h2, h1, pad, seed = all_rows
    z_now = (tile // CORES) % Z
    xt, pt, ht = turn(x, pad, h2, picks(inner_w, z_now))

    back_one = [(i, i - 1) for i in range(1, sections)]
    slots = rows + LAG * (sections - 1)
    arriving = [jnp.zeros((hgt * (width + 2), ch), BF16)] * LAG
    per_slot = []
    for slot in range(slots):
        micro = slot - LAG * (sections - 1 - section)
        info = jnp.stack(
            [jnp.clip(micro, 0, rows - 1), (section == sections - 1).astype(micro.dtype)]
        ).astype(jnp.int32)
        hand_on = slot + LAG < slots
        senders = [s for s in range(1, sections) if 0 <= slot - LAG * (sections - 1 - s) < rows]
        sent = width + 2 * max(senders, default=1)
        mz_s, h2_s, h1_s, _, seed_s = all_rows if slot else first_row
        if slot == 0:
            info = info.at[0].set(0)
        step = functools.partial(
            chain_step, info, arriving[slot], seed_s, mz_s, h2_s, h1_s, *at_hand[:1:-1], inner, outer, hgt, hand_on, sent
        )
        saved = step()
        if hand_on:
            arriving.append(lax.ppermute(saved[4], "section", back_one))
        if slot == slots - 1:
            saved = [*step(with_gi=False), saved[3]]
        per_slot.append(saved[:4])
    g3, g2, g1, gi = zip(*per_slot)
    info = jnp.stack([tile % CORES, tile // (CORES * Z), section]).astype(jnp.int32)
    early, late = range(rows - 1), range(rows - 1, rows)
    so_far = weight_grads(info, (0, 1), early, (xt, pt, ht, pt), (g1, g2, g3), (), "weight_gradients_early")
    sums_a = weight_grads(info, (0,), late, (xt, pt), (g1, g2), so_far[:2], "weight_gradients_a")
    sums_b = weight_grads(info, (1,), late, (ht, pt), (g3, g2), so_far[2:], "weight_gradients_b")
    g_reduce, g_conv, g_expand, grad_inputs = scatter_sum(collect(info, gi, rows), *sums_a, *sums_b)
    grad_inputs = grad_inputs.reshape(rows, hgt, width, ch)
    return grad_inputs[None], g_reduce[None], g_conv[None], g_expand[None]


def solution(mesh):
    in_specs = (
        P("section", None, None, "tile", None),
        P(None, None, "tile", None),
        P(None, "tile"),
        P("section", None, None),
        P("section", None, None, None, None),
        P("section", None, None),
        P("section", None, None),
        P("section", None, None),
    )
    out_specs = (
        P("section", None, None, "tile", None),
        P("section", "tile", None),
        P("section", None, None, "tile", None),
        P("section", "tile", None),
    )
    return jax.shard_map(
        per_device, mesh=mesh, in_specs=in_specs, out_specs=out_specs, check_vma=False
    )
```

```python
import functools

import jax
import jax.numpy as jnp
from jax import lax
from jax.experimental import pallas as pl
from jax.experimental.pallas import tpu as pltpu
from jax.sharding import PartitionSpec as P

TILE_W = 8
SECTIONS = 4
X, Z, CORES = 4, 8, 2
EDGE = 8
RIM = 4
BF16, F32 = jnp.bfloat16, jnp.float32
LAG = 2
SEGS, A_SEGS = 17, 8
Z_ORDER = (5, 3, 7, 1, 4, 2, 6, 0)


def params(mib):
    return pltpu.CompilerParams(vmem_limit_bytes=mib * 1024 * 1024)


def dot(left, right):
    return jnp.dot(left, right, preferred_element_type=F32)


def dot_t(left, right):
    return lax.dot_general(left, right, (((1,), (1,)), ((), ())), preferred_element_type=F32)


def full(shape):
    return pl.BlockSpec(shape, lambda *_: (0,) * len(shape), pipeline_mode=pl.Buffered(1))


def edges_kernel(tissue, x_ref, og_ref, first_ref, last_ref, og_s, stage, sems):
    rows, hgt, width, ch = x_ref.shape
    sides = (
        (first_ref, 0, 0, 0),
        (last_ref, width - EDGE, tissue.shape[1] - 1, EDGE - RIM),
    )
    from_og, from_x, handed = [], [], []
    for n, (out, start, _, _) in enumerate(sides):
        cols = pl.ds(start, EDGE)
        from_og.append(pltpu.make_async_copy(og_ref.at[:, :, cols], og_s.at[n], sems.at[n]))
        from_x.append(
            pltpu.make_async_copy(x_ref.at[:, :, cols], stage.at[n, :, pl.ds(0, hgt)], sems.at[2 + n])
        )
        handed.append(pltpu.make_async_copy(stage.at[n], out, sems.at[4 + n]))
    for copy in from_og + from_x:
        copy.start()
    for n, (_, _, tile, at) in enumerate(sides):
        from_og[n].wait()
        for r in range(rows):
            seed = og_s[n, r].astype(F32)[:, at : at + RIM] * tissue[r, tile].astype(F32)
            for pair in range(hgt // 2):
                both = jnp.concatenate([seed[2 * pair], seed[2 * pair + 1]], axis=0)
                stage[n, r, hgt + pair] = both.astype(BF16)
        from_x[n].wait()
        handed[n].start()
    for copy in handed:
        copy.wait()


def edges(tissue, x, og):
    rows, hgt, width, ch = x.shape
    out = (rows, hgt + hgt // 2, EDGE, ch)
    return pl.pallas_call(
        edges_kernel,
        out_shape=[jax.ShapeDtypeStruct(out, BF16)] * 2,
        grid_spec=pltpu.PrefetchScalarGridSpec(
            num_scalar_prefetch=1,
            grid=(1,),
            in_specs=[pl.BlockSpec(memory_space=pl.ANY)] * 2,
            out_specs=[pl.BlockSpec(memory_space=pl.ANY)] * 2,
            scratch_shapes=[
                pltpu.VMEM((2, rows, hgt, EDGE, ch), BF16),
                pltpu.VMEM((2,) + out, BF16),
                pltpu.SemaphoreType.DMA((6,)),
            ],
        ),
        compiler_params=params(60),
        name="edge_columns",
    )(tissue, x, og)


def hidden_one(part, wr, inner_ref):
    rows, hgt, cols, ch = part.shape
    flat = part.astype(F32).reshape(-1, ch).astype(BF16)
    pre = dot(flat, wr) * inner_ref[0:1] + inner_ref[1:2]
    return jnp.maximum(pre, 0.0).astype(BF16).astype(F32).reshape(rows, hgt, cols, -1)


def inside_kernel(x_ref, wr_ref, inner_ref, og_ref, wc_ref, we_ref, h1_ref, *kept):
    h1_ref[...] = hidden_one(x_ref[...], wr_ref[...], inner_ref).astype(BF16)
    for ref, out in zip((x_ref, og_ref, wr_ref, wc_ref, we_ref), kept):
        out[...] = ref[...]


def inside(x, wr, inner, og, wc, we):
    args = (x, wr, inner, og, wc, we)
    shapes = (x.shape[:3] + (wr.shape[1],),) + tuple(a.shape for a in (x, og, wr, wc, we))
    return pl.pallas_call(
        inside_kernel,
        out_shape=[jax.ShapeDtypeStruct(s, BF16) for s in shapes],
        grid=(1,),
        in_specs=[full(a.shape) for a in args],
        out_specs=[full(s) for s in shapes],
        compiler_params=params(12),
        cost_estimate=pl.CostEstimate(flops=300_000_000, bytes_accessed=9_000_000, transcendentals=0),
        name="forward_own_columns",
    )(*args)


def forward_kernel(
    some, held, ends, tissue, lo_ref, hi_ref, own_ref, inner_ref, outer_ref, x_ref, og_ref, wr_ref, wc_ref, we_ref, *refs,
):
    before, refs = refs[:held], refs[held:]
    mz_ref, h2_ref, h1_ref, pad_ref, seed_ref, xs, hs, patches, ss = refs
    hgt, width, ch = x_ref.shape[1:]
    inner_w = wr_ref.shape[1]
    wide = width + 2 * RIM
    per_row = hgt * wide
    count, start = len(some), some[0]
    these = slice(start, start + count)
    for ref, out in zip(before, (mz_ref, h2_ref, h1_ref, pad_ref, seed_ref)):
        out[:start] = ref[...]
    into = pl.ds(start if held else 0, count)
    hs[:, 0] = jnp.zeros((count, width + 2 * EDGE, inner_w), F32)
    hs[:, hgt + 1] = jnp.zeros((count, width + 2 * EDGE, inner_w), F32)
    hs[:, 1 : hgt + 1, EDGE : EDGE + width] = own_ref[these].astype(F32)
    xs[:, :, EDGE : EDGE + width] = x_ref[these].astype(F32)
    parts = jnp.concatenate([lo_ref[these, :hgt], hi_ref[these, :hgt]], axis=0)
    outside = hidden_one(parts, wr_ref[...], inner_ref)
    for n, (at, keep) in enumerate(((0, ends[0]), (EDGE + width, ends[1]))):
        side = slice(n * count, (n + 1) * count)
        xs[:, :, at : at + EDGE] = parts[side].astype(F32)
        hs[:, 1 : hgt + 1, at : at + EDGE] = outside[side] * keep.astype(F32)
    pad_ref[into] = hs[...].astype(BF16)
    first = EDGE - RIM - 1
    for k in range(9):
        dr, dc = divmod(k, 3)
        piece = hs[:, dr : dr + hgt, first + dc : first + dc + wide]
        piece = piece.reshape(-1, inner_w).astype(BF16)
        patches[:, k * inner_w : (k + 1) * inner_w] = piece
        if k == 4:
            h1_ref[into] = piece.reshape(count, per_row, inner_w)
    pre = dot(patches[...], wc_ref[...]) * inner_ref[2:3] + inner_ref[3:4]
    hid = jnp.maximum(pre, 0.0).astype(BF16)
    h2_ref[into] = hid.reshape(count, per_row, inner_w)
    for n, r in enumerate(some):
        out = r if held else n
        part = hid[n * per_row : (n + 1) * per_row]
        z = dot(part, we_ref[...]) * outer_ref[0:1] + outer_ref[1:2]
        z = z + xs[n, :, EDGE - RIM : EDGE - RIM + wide].reshape(per_row, ch)
        mz_ref[out] = jnp.where(z > 0, 1.0, 0.0).astype(BF16)
        for ref, at in ((lo_ref, 0), (hi_ref, RIM + width)):
            for pair in range(hgt // 2):
                both = ref[r, hgt + pair].astype(F32)
                ss[2 * pair, at : at + RIM] = both[:RIM]
                ss[2 * pair + 1, at : at + RIM] = both[RIM:]
        og = og_ref[r].astype(F32)
        for tile in range(width // TILE_W):
            cols = og[:, tile * TILE_W : (tile + 1) * TILE_W] * tissue[r, tile].astype(F32)
            ss[:, RIM + tile * TILE_W : RIM + (tile + 1) * TILE_W] = cols
        seed_ref[out] = ss[...].reshape(per_row, ch).astype(BF16)


def forward(some, before, ends, tissue, lo, hi, own, inner, outer, x, og, wr, wc, we):
    rows, hgt, width, ch = x.shape
    inner_w = wr.shape[1]
    wide = width + 2 * RIM
    pos = hgt * wide
    count = len(some)
    out_rows = rows if before else count
    out_shapes = (
        (out_rows, pos, ch),
        (out_rows, pos, inner_w),
        (out_rows, pos, inner_w),
        (out_rows, hgt + 2, width + 2 * EDGE, inner_w),
        (out_rows, pos, ch),
    )
    blocks = (lo, hi, own, inner, outer, x, og, wr, wc, we, *before)
    return pl.pallas_call(
        functools.partial(forward_kernel, some, len(before)),
        out_shape=[jax.ShapeDtypeStruct(s, BF16) for s in out_shapes],
        grid_spec=pltpu.PrefetchScalarGridSpec(
            num_scalar_prefetch=2,
            grid=(1,),
            in_specs=[full((some[-1] + 1,) + a.shape[1:]) for a in blocks[:2]] + [full(a.shape) for a in blocks[2:]],
            out_specs=[full(s) for s in out_shapes],
            scratch_shapes=[
                pltpu.VMEM((count, hgt, width + 2 * EDGE, ch), F32),
                pltpu.VMEM((count, hgt + 2, width + 2 * EDGE, inner_w), F32),
                pltpu.VMEM((count * pos, 9 * inner_w), BF16),
                pltpu.VMEM((hgt, wide, ch), F32),
            ],
        ),
        compiler_params=params(20),
        cost_estimate=pl.CostEstimate(
            flops=600_000_000 * count, bytes_accessed=4_000_000 * count, transcendentals=0
        ),
        name="forward_rows",
    )(ends, tissue, *blocks)


def chain_kernel(
    info, gy_ref, seed_ref, mz_ref, h2_ref, h1_ref, we_ref, wc_ref, wr_ref, inner_ref, outer_ref,
    g3_ref, g2_ref, g1_ref, *more, with_gi,
):
    gi_ref, more = (more[0], more[1:]) if with_gi else (None, more)
    *wire_ref, wide_s, pad_s, flat_s = more
    inner_w = we_ref.shape[0]
    hgt, wide, ch = wide_s.shape
    pos = hgt * wide
    width = wide - 2 * RIM
    lead = 8

    def center(value):
        lanes = value.shape[1]
        wide_s[:, :, :lanes] = value.reshape(hgt, wide, lanes)
        return wide_s[:, RIM : RIM + width, :lanes].reshape(hgt * width, lanes).astype(BF16)

    cols = gy_ref.shape[0] // hgt
    at = (wide - cols) // 2
    flat_s[: hgt * cols] = gy_ref[...].astype(F32)
    wide_s[:, :8] = jnp.zeros((hgt, 8, ch), F32)
    wide_s[:, wide - 8 :] = jnp.zeros((hgt, 8, ch), F32)
    for h in range(hgt):
        wide_s[h, at : at + cols] = flat_s[h * cols : (h + 1) * cols]
    gy = jnp.where(info[1] == 1, seed_ref[0].astype(F32), wide_s[...].reshape(pos, ch))
    gz = gy * mz_ref[0].astype(F32)
    g3 = (gz * outer_ref[0:1]).astype(BF16)
    g3_ref[...] = center(g3.astype(F32))
    g2 = jnp.where(h2_ref[0].astype(F32) > 0, dot_t(g3, we_ref[...]) * inner_ref[2:3], 0.0)
    g2 = g2.astype(BF16).astype(F32)
    pad_s[...] = jnp.zeros_like(pad_s)
    pad_s[1 : hgt + 1, lead : lead + wide] = g2.reshape(hgt, wide, inner_w)
    g2_ref[...] = (
        pad_s[1 : hgt + 1, lead + RIM : lead + RIM + width].reshape(hgt * width, inner_w).astype(BF16)
    )
    back = jnp.zeros((pos, inner_w), F32)
    for k in range(9):
        dr, dc = divmod(k, 3)
        piece = pad_s[2 - dr : 2 - dr + hgt, lead + 1 - dc : lead + 1 - dc + wide]
        back = back + dot_t(piece.reshape(pos, inner_w).astype(BF16), wc_ref[k * inner_w : (k + 1) * inner_w])
    g1 = jnp.where(h1_ref[0].astype(F32) > 0, back * inner_ref[0:1], 0.0).astype(BF16)
    g1_ref[...] = center(g1.astype(F32))
    if gi_ref is None:
        return
    gi = gz + dot_t(g1, wr_ref[...])
    gi_ref[...] = center(gi)
    if wire_ref:
        cols = wire_ref[0].shape[0] // hgt
        at = (wide - cols) // 2
        for h in range(hgt):
            flat_s[h * cols : (h + 1) * cols] = wide_s[h, at : at + cols]
        wire_ref[0][...] = flat_s[: hgt * cols].astype(BF16)


def chain_step(info, gy, seed, mz, h2, h1, we, wc, wr, inner, outer, hgt, hand_on, sent, with_gi=True):
    pos, ch = seed.shape[1:]
    inner_w = we.shape[0]
    wide = pos // hgt
    kept = hgt * (wide - 2 * RIM)

    def row(lanes):
        return pl.BlockSpec((1, pos, lanes), lambda i, info: (info[0], 0, 0))

    const = (we, wc, wr, inner, outer)
    out_shapes = [(kept, ch), (kept, inner_w), (kept, inner_w)] + [(kept, ch)] * with_gi + [(hgt * sent, ch)] * hand_on
    return pl.pallas_call(
        functools.partial(chain_kernel, with_gi=with_gi),
        out_shape=[jax.ShapeDtypeStruct(s, BF16) for s in out_shapes],
        grid_spec=pltpu.PrefetchScalarGridSpec(
            num_scalar_prefetch=1,
            grid=(1,),
            in_specs=[full(gy.shape), row(ch), row(ch), row(inner_w), row(inner_w)]
            + [full(c.shape) for c in const],
            out_specs=[full(s) for s in out_shapes],
            scratch_shapes=[
                pltpu.VMEM((hgt, wide, ch), F32),
                pltpu.VMEM((hgt + 2, wide + 16, inner_w), F32),
                pltpu.VMEM((pos, ch), F32),
            ],
        ),
        compiler_params=params(12),
        cost_estimate=pl.CostEstimate(flops=3_600_000_000, bytes_accessed=50_000_000, transcendentals=0),
        name="chain_row",
    )(info, gy, seed, mz, h2, h1, *const)


def picks(inner_w, z):
    row = jnp.arange(inner_w)
    each = row % 4
    own = jnp.asarray(Z_ORDER, row.dtype)[(row // 4) % Z] ^ z
    mid = (row // (4 * Z)) % 4
    core = row // (4 * Z * 4)
    whole = ((mid * Z + own) * CORES + core) * 4 + each
    part = (own * CORES + core) * 16 + mid * 4 + each
    return (jnp.stack([whole, part])[:, :, None] == row[None, None]).astype(BF16)


def turn_kernel(x_ref, pad_ref, h2_ref, pick_ref, xt_ref, pt_ref, ht_ref):
    rows, hgt, width, ch = x_ref.shape
    inner_w = h2_ref.shape[2]
    half = inner_w // CORES
    wide = width + 2 * RIM

    def turned(order, value, ref, at, stride):
        out = lax.dot_general(
            pick_ref[order], value, (((1,), (1,)), ((), ())), preferred_element_type=F32
        ).astype(BF16)
        for core in range(CORES):
            ref[core * stride + at : core * stride + at + half] = out[core * half : (core + 1) * half]

    flat = x_ref[...].astype(F32).reshape(-1, ch).astype(BF16)
    for part in range(ch // inner_w):
        turned(1, flat[:, part * inner_w : (part + 1) * inner_w], xt_ref, part * half, ch // CORES)
    padded = pad_ref[...].astype(F32)
    for k in range(9):
        dr, dc = divmod(k, 3)
        piece = padded[:, dr : dr + hgt, EDGE - 1 + dc : EDGE - 1 + dc + width]
        turned(0, piece.reshape(-1, inner_w).astype(BF16), pt_ref, k * half, 9 * half)
    h2 = h2_ref[...].astype(F32).reshape(rows * hgt, wide, inner_w)[:, RIM : RIM + width]
    turned(0, h2.reshape(-1, inner_w).astype(BF16), ht_ref, 0, half)


def turn(x, pad, h2, pick):
    rows, hgt, width, ch = x.shape
    inner_w = h2.shape[2]
    pos = rows * hgt * width
    args = (x, pad, h2, pick)
    shapes = ((ch, pos), (9 * inner_w, pos), (inner_w, pos))
    return pl.pallas_call(
        turn_kernel,
        out_shape=[jax.ShapeDtypeStruct(s, BF16) for s in shapes],
        grid=(1,),
        in_specs=[full(a.shape) for a in args],
        out_specs=[full(s) for s in shapes],
        compiler_params=params(20),
        cost_estimate=pl.CostEstimate(flops=2_000_000_000, bytes_accessed=8_000_000, transcendentals=0),
        name="turn_activations",
    )(*args)


def place(segment, target, x):
    as_int = lambda cond: jnp.where(cond, 1, 0)
    if segment < A_SEGS:
        side = as_int((x == 1) | (x == 2))
        keep = as_int(side == (1 if target in (1, 2) else 0))
        last = as_int(x // 2 == target // 2)
        return ((keep * 2 + last) * A_SEGS + segment) * 32
    keep = as_int(x // 2 == target // 2)
    same = as_int(x % 2 == target % 2)
    last = jnp.where(keep == 1, same, 1 - same)
    return ((keep * 2 + last) * (SEGS - A_SEGS) + segment - A_SEGS) * 32


def products(part, side, x, left, right, cols, out_ref, so_far):
    first_ref, pt_ref = left
    inner_w = pt_ref.shape[0] // 9
    half = inner_w // CORES
    first = first_ref.shape[0] // CORES
    ks = range(A_SEGS - 4) if part == 0 else range(A_SEGS - 4, 9)

    def put(target, segment, value):
        rows = pl.ds(pl.multiple_of(place(segment, target, x), 32), value.shape[0])
        if so_far is not None:
            value = value + so_far[rows].astype(F32)
        out_ref[rows] = value.astype(BF16)

    total = dot(first_ref[pl.ds(pl.multiple_of(side * first, first), first), cols], right[0])
    if part == 0:
        for target in range(X):
            put(target, 0, total[target * half : (target + 1) * half])
    else:
        for j in range(4):
            for target in range(X):
                put(target, 13 + j, total[target * 32 : target * 32 + 32, j * inner_w : (j + 1) * inner_w])
    at = pl.multiple_of(side * 9 * half + ks[0] * half, half)
    total = dot(pt_ref[pl.ds(at, len(ks) * half), cols], right[1])
    for n, k in enumerate(ks):
        for target in range(X):
            put(target, 4 + k, total[n * half + target * 32 : n * half + target * 32 + 32])


def weights_kernel(parts, rows, by_row, added, info, *refs):
    count = len(parts)
    lefts, refs = refs[: 2 * count], refs[2 * count :]
    so_far, refs = (refs[: 2 * count], refs[2 * count :]) if added else ((None,) * (2 * count), refs)
    kinds = 2 if count == 1 else 3
    slots = []
    for _ in range(kinds):
        slots.append(refs[: len(by_row)])
        refs = refs[len(by_row) :]
    outs, stores, sems = refs[: 2 * count], refs[2 * count : 2 * count + kinds], refs[-1]
    core, x, section = info[0], info[1], info[2]

    def copy(kind, n, slot):
        return pltpu.make_async_copy(slots[kind][by_row.index(slot)], stores[kind].at[n], sems.at[kind, n])

    for s, used in enumerate(slots_of(rows)):
        @pl.when(section == s)
        def _():
            for kind in range(kinds):
                for n, slot in enumerate(used):
                    copy(kind, n, slot).start()

    held = []
    for kind in range(kinds):
        for n in range(len(rows)):
            copy(kind, n, by_row[0]).wait()
        kept, lanes = stores[kind].shape[1:]
        held.append(stores[kind][...].reshape(len(rows) * kept, lanes))
    cols = slice(rows[0] * kept, (rows[-1] + 1) * kept)
    for i, part in enumerate(parts):
        right = (held[0], held[1]) if count == 1 or part == 0 else (held[2], held[1])
        for n, side in enumerate((core, 1 - core)):
            products(part, side, x, lefts[2 * i : 2 * i + 2], right, cols, outs[2 * i + n], so_far[2 * i + n])


def slots_of(rows):
    return [[LAG * (SECTIONS - 1 - s) + r for r in rows] for s in range(SECTIONS)]


def weight_grads(info, parts, rows, lefts, saved, so_far, name):
    by_row = sorted({slot for used in slots_of(rows) for slot in used})
    kept = saved[0][0].shape[0]
    inner_w = lefts[1].shape[0] // 9
    sizes = [(A_SEGS if part == 0 else SEGS - A_SEGS) * X * 32 for part in parts]
    out_shapes = [(size, inner_w) for size in sizes for _ in range(2)]
    blocks = tuple(lefts) + tuple(so_far)
    return pl.pallas_call(
        functools.partial(weights_kernel, parts, rows, by_row, len(so_far) > 0),
        out_shape=[jax.ShapeDtypeStruct(s, BF16) for s in out_shapes],
        grid_spec=pltpu.PrefetchScalarGridSpec(
            num_scalar_prefetch=1,
            grid=(1,),
            in_specs=[full(a.shape) for a in blocks]
            + [pl.BlockSpec(memory_space=pl.ANY)] * (len(by_row) * len(saved)),
            out_specs=[full(s) for s in out_shapes],
            scratch_shapes=[pltpu.VMEM((len(rows), kept, kind[0].shape[1]), BF16) for kind in saved]
            + [pltpu.SemaphoreType.DMA((len(saved), len(rows)))],
        ),
        compiler_params=params(20),
        cost_estimate=pl.CostEstimate(
            flops=300_000_000 * len(rows), bytes_accessed=2_000_000 * len(rows), transcendentals=0
        ),
        name=name,
    )(info, *blocks, *[kind[slot] for kind in saved for slot in by_row])


def collect_kernel(slots, info, *refs):
    out_ref, sems = refs[slots], refs[slots + 1]
    rows = range(out_ref.shape[0])

    def copy(n, slot):
        return pltpu.make_async_copy(refs[slot], out_ref.at[n], sems.at[n])

    for s, used in enumerate(slots_of(rows)):
        @pl.when(info[2] == s)
        def _():
            for n, slot in enumerate(used):
                copy(n, slot).start()

    for n in rows:
        copy(n, n).wait()


def collect(info, gi, rows):
    return pl.pallas_call(
        functools.partial(collect_kernel, len(gi)),
        out_shape=jax.ShapeDtypeStruct((rows,) + gi[0].shape, BF16),
        grid_spec=pltpu.PrefetchScalarGridSpec(
            num_scalar_prefetch=1,
            grid=(1,),
            in_specs=[pl.BlockSpec(memory_space=pl.ANY)] * len(gi),
            out_specs=pl.BlockSpec(memory_space=pl.ANY),
            scratch_shapes=[pltpu.SemaphoreType.DMA((rows,))],
        ),
        compiler_params=params(4),
        cost_estimate=pl.CostEstimate(flops=0, bytes_accessed=2_000_000, transcendentals=0),
        name="collect_grad_inputs",
    )(info, *gi)


def tile_pairs(partner):
    pairs = []
    for x in range(X):
        for z in range(Z):
            for c in range(CORES):
                px, pz, pc = partner(x, z, c)
                pairs.append(((x * Z + z) * CORES + c, (px * Z + pz) * CORES + pc))
    return pairs


def swap(value, partner):
    return lax.ppermute(value.astype(BF16), "tile", tile_pairs(partner))


def scatter_sum(beside, keep_a, send_a, keep_b, send_b):
    lanes = keep_a.shape[-1]
    other_core = lambda x, z, c: (x, z, 1 - c)
    inner_pair = lambda x, z, c: (x ^ 1, z, c)
    outer_pair = lambda x, z, c: (3 - x, z, c)

    def along_x(keep, send, pairs):
        got = swap(send, other_core)
        own = lambda first, last: keep[first:last].astype(F32) + got[first:last].astype(F32)
        size = keep.shape[0]
        half, quart = size // 2, size // 4
        got_1 = swap(own(0, half), pairs[0])
        got_2 = swap(own(half, half + quart) + got_1[:quart].astype(F32), pairs[1])
        return own(half + quart, size) + got_1[quart:].astype(F32) + got_2.astype(F32)

    part_a = along_x(keep_a, send_a, (inner_pair, outer_pair))
    part_b = along_x(keep_b, send_b, (outer_pair, inner_pair))
    total = jnp.concatenate([part_a, part_b], axis=0).reshape(SEGS, Z * 4, lanes)
    total, beside = lax.optimization_barrier((total, beside))
    for bits in (1, 2):
        count = total.shape[1] // 2
        got = swap(total[:, :count], lambda x, z, c, b=bits: (x, z ^ b, c))
        total = total[:, count:] + got.astype(F32)
    shares = finish(total[:, 4:], [swap(total[:, :4], lambda x, z, c: (x, z ^ 6, c))])
    return (*shares, beside)


def finish_kernel(own_ref, *refs):
    reduce_ref, conv_ref, expand_ref = refs[-3:]
    total = own_ref[...]
    for ref in refs[:-3]:
        total = total + ref[...].astype(F32)
    lanes = total.shape[2]
    for q in range(4):
        reduce_ref[4 * q : 4 * q + 4] = total[q]
        expand_ref[:, q * lanes : (q + 1) * lanes] = total[13 + q]
    conv_ref[...] = total[4:13]


def finish(own, shares):
    lanes = own.shape[2]
    shapes = ((16, lanes), (9, 4, lanes), (4, 4 * lanes))
    args = (own, *shares)
    g_reduce, g_conv, g_expand = pl.pallas_call(
        finish_kernel,
        out_shape=[jax.ShapeDtypeStruct(s, F32) for s in shapes],
        grid=(1,),
        in_specs=[full(a.shape) for a in args],
        out_specs=[full(s) for s in shapes],
        compiler_params=params(4),
        name="finish_gradients",
    )(*args)
    return g_reduce, g_conv.reshape(3, 3, 4, lanes), g_expand


def neighbours(first, last, tiles):
    pairs = [(i, i + 1) for i in range(tiles - 1)]
    low = lax.ppermute(last, "tile", pairs)
    high = lax.ppermute(first, "tile", [(b, a) for a, b in pairs])
    return low, high


def per_device(block_inputs, out_grad, tissue, w_reduce, w_conv, w_expand, inner_affine, outer_affine):
    section = lax.axis_index("section")
    sections = lax.axis_size("section")
    tile = lax.axis_index("tile")
    tiles = lax.axis_size("tile")
    x = block_inputs[0]
    rows, hgt, width, ch = x.shape
    wr, we = w_reduce[0], w_expand[0]
    inner_w = wr.shape[1]
    wc = w_conv[0].reshape(9 * inner_w, inner_w)
    inner, outer = inner_affine[0], outer_affine[0]

    lo, hi = neighbours(*edges(tissue, x, out_grad), tiles)
    own, *at_hand = inside(x, wr, inner, out_grad, wc, we)

    ends = jnp.stack([tile > 0, tile < tiles - 1]).astype(jnp.int32)
    ahead = (ends, tissue, lo, hi, own, inner, outer, *at_hand)
    first_row = forward(range(1), (), *ahead)
    all_rows = forward(range(1, rows), first_row, *ahead)
    mz, h2, h1, pad, seed = all_rows
    z_now = (tile // CORES) % Z
    xt, pt, ht = turn(x, pad, h2, picks(inner_w, z_now))

    back_one = [(i, i - 1) for i in range(1, sections)]
    slots = rows + LAG * (sections - 1)
    arriving = [jnp.zeros((hgt * (width + 2), ch), BF16)] * LAG
    per_slot = []
    for slot in range(slots):
        micro = slot - LAG * (sections - 1 - section)
        info = jnp.stack(
            [jnp.clip(micro, 0, rows - 1), (section == sections - 1).astype(micro.dtype)]
        ).astype(jnp.int32)
        hand_on = slot + LAG < slots
        senders = [s for s in range(1, sections) if 0 <= slot - LAG * (sections - 1 - s) < rows]
        sent = width + 2 * max(senders, default=1)
        mz_s, h2_s, h1_s, _, seed_s = all_rows if slot else first_row
        if slot == 0:
            info = info.at[0].set(0)
        step = functools.partial(
            chain_step, info, arriving[slot], seed_s, mz_s, h2_s, h1_s, *at_hand[:1:-1], inner, outer, hgt, hand_on, sent
        )
        saved = step()
        if hand_on:
            arriving.append(lax.ppermute(saved[4], "section", back_one))
        if slot == slots - 1:
            saved = [*step(with_gi=False), saved[3]]
        per_slot.append(saved[:4])
    g3, g2, g1, gi = zip(*per_slot)
    info = jnp.stack([tile % CORES, tile // (CORES * Z), section]).astype(jnp.int32)
    early, late = range(rows - 1), range(rows - 1, rows)
    so_far = weight_grads(info, (0, 1), early, (xt, pt, ht, pt), (g1, g2, g3), (), "weight_gradients_early")
    sums_a = weight_grads(info, (0,), late, (xt, pt), (g1, g2), so_far[:2], "weight_gradients_a")
    sums_b = weight_grads(info, (1,), late, (ht, pt), (g3, g2), so_far[2:], "weight_gradients_b")
    g_reduce, g_conv, g_expand, grad_inputs = scatter_sum(collect(info, gi, rows), *sums_a, *sums_b)
    grad_inputs = grad_inputs.reshape(rows, hgt, width, ch)
    return grad_inputs[None], g_reduce[None], g_conv[None], g_expand[None]


def solution(mesh):
    in_specs = (
        P("section", None, None, "tile", None),
        P(None, None, "tile", None),
        P(None, "tile"),
        P("section", None, None),
        P("section", None, None, None, None),
        P("section", None, None),
        P("section", None, None),
        P("section", None, None),
    )
    out_specs = (
        P("section", None, None, "tile", None),
        P("section", "tile", None),
        P("section", None, None, "tile", None),
        P("section", "tile", None),
    )
    return jax.shard_map(
        per_device, mesh=mesh, in_specs=in_specs, out_specs=out_specs, check_vma=False
    )
```
